32 devices in a mesh: head: 4 (over z), node: 8 (over y, x, core).
Axes of the slice: x: 2, y: 2, z: 4, core: 2. Of those that a mesh axis runs over, the one named last changes fastest.
Arguments:
- node_input: bfloat16 [8192, 512], P('node'), may hold values from -6 to 6
- cotangent: bfloat16 [8192, 512], P('node'), may hold values from -6 to 6
- sigma_embed: bfloat16 [4, 512], replicated, may hold values from -5 to 5
- neighbours: int32 [8192, 16], P('node'), may hold values from 0 to 8191, as said below
- neighbour_valid: int32 [8192, 16], P('node'), may hold values 0 or 1
- batch_counts: int32 [4], replicated, may hold values from 1 to 4096, 8192 in all
- step_count: int32 [1], replicated, may hold values from 1 to 20
- ada_master: float32 [512, 2048], P('node'), may hold values from -0.125 to 0.125
- ada_first: float32 [512, 2048], P('node'), may hold values from -768 to 768
- ada_second: float32 [512, 2048], P('node'), may hold values from 16384 to 65536
- qkv_master: float32 [512, 1536], P('node', 'head'), may hold values from -0.375 to 0.375
- qkv_first: float32 [512, 1536], P('node', 'head'), may hold values from -1024 to 1024
- qkv_second: float32 [512, 1536], P('node', 'head'), may hold values from 32768 to 131072
- out_master: float32 [512, 512], P(('head', 'node')), may hold values from -0.5 to 0.5
- out_first: float32 [512, 512], P(('head', 'node')), may hold values from -384 to 384
- out_second: float32 [512, 512], P(('head', 'node')), may hold values from 4096 to 16384
- up_master: float32 [512, 2048], P('node', 'head'), may hold values from -0.25 to 0.25
- up_first: float32 [512, 2048], P('node', 'head'), may hold values from -128 to 128
- up_second: float32 [512, 2048], P('node', 'head'), may hold values from 491.52 to 2048
- down_master: float32 [2048, 512], P(('head', 'node')), may hold values from -0.125 to 0.125
- down_first: float32 [2048, 512], P(('head', 'node')), may hold values from -256 to 256
- down_second: float32 [2048, 512], P(('head', 'node')), may hold values from 2048 to 8192
Outputs:
- node_output: bfloat16 [8192, 512], P('node')
- input_grad: float32 [8192, 512], P('node')
- ada_new: float32 [512, 2048], P('node')
- ada_first_new: float32 [512, 2048], P('node')
- ada_second_new: float32 [512, 2048], P('node')
- qkv_new: float32 [512, 1536], P('node', 'head')
- qkv_first_new: float32 [512, 1536], P('node', 'head')
- qkv_second_new: float32 [512, 1536], P('node', 'head')
- out_new: float32 [512, 512], P(('head', 'node'))
- out_first_new: float32 [512, 512], P(('head', 'node'))
- out_second_new: float32 [512, 512], P(('head', 'node'))
- up_new: float32 [512, 2048], P('node', 'head')
- up_first_new: float32 [512, 2048], P('node', 'head')
- up_second_new: float32 [512, 2048], P('node', 'head')
- down_new: float32 [2048, 512], P(('head', 'node'))
- down_first_new: float32 [2048, 512], P(('head', 'node'))
- down_second_new: float32 [2048, 512], P(('head', 'node'))
The draws below stay inside these ranges and needn't reach their ends.
Inputs may be any that keep to these rules, and one draw needn't show every extreme that they name: `batch_counts`: the counts sum to 8192; the largest is exactly 4096. Node n's neighbours lie in its own aligned block of 1024 nodes or in the two blocks on either side of it, counted cyclically over the 8192 nodes.
All inputs are finite; a program needn't handle non-finite values. No bound on the sum of `neighbour_valid` on one device may be relied on, other than what follows from the above.
Results may differ from the reference program's by a relative error of at most 0.018.
The reference program's roundings to bfloat16 on the way count: a program that leaves them out, or rounds other values in their place, can miss the bound.
Values may be sent and summed in bfloat16 or wider, within the bound.
A program may use at most 128 MiB of HBM per device.

```python
import math
import jax
import jax.numpy as jnp
import numpy as np
from jax import lax

WIDTH = 512
HEADS = 4
HEAD_DIM = 128
HIDDEN_SIZE = 2048
COND = 512
NEIGHBOURS = 16
BATCHES = 4
NODE_DEV = 1024
NODES = 8192


def draw_neighbours(key, part):
    positions = jnp.arange(NODES, dtype=jnp.int32)
    block_start = positions // NODE_DEV * NODE_DEV
    offsets = jax.random.randint(key, (NODES, NEIGHBOURS), -2 * NODE_DEV, 3 * NODE_DEV, dtype=jnp.int32)
    return jnp.mod(block_start[:, None] + offsets, NODES).astype(jnp.int32)


def place_ends(drawn, stream_key, smallest, high):
    index_at = [jax.random.randint(jax.random.fold_in(stream_key, axis), (), 0, length) for axis, length in enumerate(drawn.shape)]
    widest = drawn.shape.index(max(drawn.shape))
    neighbour = index_at[:widest] + [(index_at[widest] + 1) % drawn.shape[widest]] + index_at[widest + 1:]
    return drawn.at[tuple(index_at)].set(smallest).at[tuple(neighbour)].set(high)


def levels(key, shape, cuts, low, top_value):
    factor_of, own = 1.0, jax.random.fold_in(key, 6)
    for axis_at, parts in cuts:
        heights = jnp.exp(jax.random.uniform(jax.random.fold_in(own, axis_at), (parts,), jnp.float32, low / len(cuts), top_value / len(cuts)))
        factor_of = factor_of * jnp.repeat(heights, shape[axis_at] // parts).reshape([-1 if axis == axis_at else 1 for axis in range(len(shape))])
    return factor_of


def split_up(count, total, most, skew):
    weights = [(1 << 20) // math.isqrt(rank ** skew) + 1 for rank in range(2, count + 1)]
    spare, given = total - most - (count - 1), [1] * (count - 1)
    while spare > 0:
        free = [i for i in range(count - 1) if given[i] < most]
        whole, left = sum([weights[i] for i in free]), spare
        for i in free:
            addition = min(most - given[i], max(1, left * weights[i] // whole), spare)
            given[i] = given[i] + addition
            spare = spare - addition
    return np.array([most] + given)


def uneven_parts(own_key, number_of, total, limit, lean):
    if number_of == 2:
        one = jax.random.randint(own_key, (), max(1, total - limit), min(limit, total - 1) + 1)
        return jnp.stack([one, total - one])
    sizes = jnp.asarray(split_up(number_of, total, limit, lean), jnp.int32)
    couples = (number_of - 1) // 2
    donor, sink = sizes[1:1 + 2 * couples:2], sizes[2:2 + 2 * couples:2]
    room = jnp.minimum(donor - 1, limit - sink)
    passed = jax.random.randint(jax.random.fold_in(own_key, 1), (couples,), 0, 1 << 20) % (room + 1)
    sizes = sizes.at[1:1 + 2 * couples:2].set(donor - passed).at[2:2 + 2 * couples:2].set(sink + passed)
    return sizes[jax.random.permutation(jax.random.fold_in(own_key, 2), number_of)]


def scatter_about(stream_key, extent, scale, limit, pieces=(), kind=jnp.bfloat16):
    gain = levels(stream_key, extent, pieces, -0.22, 0.18) if pieces else 1.0
    entries = jax.random.normal(stream_key, extent, jnp.float32) * scale * gain
    return jnp.minimum(jnp.maximum(entries, -limit), limit).astype(kind)


def setup_inputs(seed: int = 0) -> dict:
    seeds = jax.random.split(jax.random.key(seed), 23)
    node_input = scatter_about(seeds[0], (NODES, WIDTH), 1.0, 6.0, ((0, 8),))
    cotangent = scatter_about(seeds[1], (NODES, WIDTH), 1.0, 6.0, ((0, 8),))
    sigma_embed = scatter_about(seeds[2], (BATCHES, COND), 1.0, 5.0)
    neighbours = draw_neighbours(jax.random.fold_in(seeds[22], 71), 0)
    neighbour_valid = place_ends((jax.random.randint(seeds[4], (NODES, NEIGHBOURS), 0, 4) < 3).astype(jnp.int32), jax.random.fold_in(seeds[4], 1), 0, 1)
    batch_counts = uneven_parts(seeds[5], BATCHES, NODES, NODES // 2, 2).astype(jnp.int32)
    step_count = jax.random.randint(seeds[6], (1,), 1, 21).astype(jnp.int32)
    ada_master = scatter_about(seeds[7], (COND, 4 * WIDTH), (4 * COND) ** -0.5, 0.125, ((0, 8),), jnp.float32)
    ada_first = scatter_about(seeds[8], (COND, 4 * WIDTH), (1.4 * NODES ** 0.5), 768.0, ((0, 8),), jnp.float32)
    ada_second = jnp.clip(jnp.exp(math.log(65536.0) - 1.3862944 * jax.random.uniform(seeds[9], (COND, 4 * WIDTH), jnp.float32) ** levels(seeds[9], (COND, 4 * WIDTH), ((0, 8),), -0.2, 0.2)), 16384.0, 65536.0)
    qkv_master = scatter_about(seeds[10], (WIDTH, 3 * WIDTH), (WIDTH // 2) ** -0.5, 0.375, ((0, 8), (1, 4)), jnp.float32)
    qkv_first = scatter_about(seeds[11], (WIDTH, 3 * WIDTH), (2.0 * NODES ** 0.5), 1024.0, ((0, 8), (1, 4)), jnp.float32)
    qkv_second = jnp.clip(jnp.exp(math.log(131072.0) - 1.3862944 * jax.random.uniform(seeds[12], (WIDTH, 3 * WIDTH), jnp.float32) ** levels(seeds[12], (WIDTH, 3 * WIDTH), ((0, 8), (1, 4)), -0.2, 0.2)), 32768.0, 131072.0)
    out_master = scatter_about(seeds[13], (WIDTH, WIDTH), (WIDTH // 4) ** -0.5, 0.5, ((0, 32),), jnp.float32)
    out_first = scatter_about(seeds[14], (WIDTH, WIDTH), (0.7 * NODES ** 0.5), 384.0, ((0, 32),), jnp.float32)
    out_second = jnp.clip(jnp.exp(math.log(16384.0) - 1.3862944 * jax.random.uniform(seeds[15], (WIDTH, WIDTH), jnp.float32) ** levels(seeds[15], (WIDTH, WIDTH), ((0, 32),), -0.2, 0.2)), 4096.0, 16384.0)
    up_master = scatter_about(seeds[16], (WIDTH, HIDDEN_SIZE), WIDTH ** -0.5, 0.25, ((0, 8), (1, 4)), jnp.float32)
    up_first = scatter_about(seeds[17], (WIDTH, HIDDEN_SIZE), (0.25 * NODES ** 0.5), 128.0, ((0, 8), (1, 4)), jnp.float32)
    up_second = jnp.clip(jnp.exp(math.log(2048.0) - 1.4271164 * jax.random.uniform(seeds[18], (WIDTH, HIDDEN_SIZE), jnp.float32) ** levels(seeds[18], (WIDTH, HIDDEN_SIZE), ((0, 8), (1, 4)), -0.2, 0.2)), 491.52, 2048.0)
    down_master = scatter_about(seeds[19], (HIDDEN_SIZE, WIDTH), HIDDEN_SIZE ** -0.5, 0.125, ((0, 32),), jnp.float32)
    down_first = scatter_about(seeds[20], (HIDDEN_SIZE, WIDTH), (0.5 * NODES ** 0.5), 256.0, ((0, 32),), jnp.float32)
    down_second = jnp.clip(jnp.exp(math.log(8192.0) - 1.3862944 * jax.random.uniform(seeds[21], (HIDDEN_SIZE, WIDTH), jnp.float32) ** levels(seeds[21], (HIDDEN_SIZE, WIDTH), ((0, 32),), -0.2, 0.2)), 2048.0, 8192.0)
    return {"node_input": node_input, "cotangent": cotangent, "sigma_embed": sigma_embed, "neighbours": neighbours, "neighbour_valid": neighbour_valid, "batch_counts": batch_counts, "step_count": step_count, "ada_master": ada_master, "ada_first": ada_first, "ada_second": ada_second, "qkv_master": qkv_master, "qkv_first": qkv_first, "qkv_second": qkv_second, "out_master": out_master, "out_first": out_first, "out_second": out_second, "up_master": up_master, "up_first": up_first, "up_second": up_second, "down_master": down_master, "down_first": down_first, "down_second": down_second}


@jax.custom_vjp
def low(v):
    return lax.optimization_barrier(v.astype(jnp.bfloat16)).astype(jnp.float32)

@jax.custom_vjp
def low_back(v):
    return v

def low_keep(v):
    return (low(v), None)

def low_pass(kept, grad):
    return (grad,)

def back_keep(v):
    return (v, None)

def back_low(kept, grad):
    return (low(grad),)
low.defvjp(low_keep, low_pass)
low_back.defvjp(back_keep, back_low)
norm_eps = 1e-06
beta_rate = 0.5
adam_eps = 1e-08
weight_decay = 0.1
highest = lax.Precision.HIGHEST

def normalize(values):
    centred = values - lax.optimization_barrier(jnp.mean(values, axis=1, keepdims=True))
    spread = lax.optimization_barrier(jnp.mean(centred * centred, axis=1, keepdims=True))
    return centred * lax.rsqrt(spread + norm_eps)

def batch_onehot(batch_counts):
    limits = jnp.cumsum(batch_counts)[:BATCHES - 1].astype(jnp.int32)
    positions = jnp.arange(NODES, dtype=jnp.int32)
    member = lax.optimization_barrier(jnp.sum((positions[:, None] >= limits[None, :]).astype(jnp.int32), axis=1))
    return (member[:, None] == jnp.arange(BATCHES, dtype=jnp.int32)[None, :]).astype(jnp.float32)

def attend(queries, key_rows, value_rows, neighbours, validity):
    score_scale = HEAD_DIM ** (-0.5)
    block_rows = min(NODES, 4096)

    def one_block(position):
        first_row = position * block_rows
        query_part = lax.dynamic_slice_in_dim(queries, first_row, block_rows, 0)
        key_part = lax.dynamic_slice_in_dim(key_rows, first_row, block_rows, 0)
        value_part = lax.dynamic_slice_in_dim(value_rows, first_row, block_rows, 0)
        link_part = lax.dynamic_slice_in_dim(neighbours, first_row, block_rows, 0)
        valid_part = lax.dynamic_slice_in_dim(validity, first_row, block_rows, 0)
        near_keys = key_rows[link_part]
        near_values = value_rows[link_part]
        self_score = lax.optimization_barrier(jnp.sum(query_part * key_part, axis=2)) * score_scale
        near_score = jnp.einsum('rhd,rkhd->rhk', query_part, near_keys, precision=highest) * score_scale
        near_score = jnp.where(valid_part[:, None, :] > 0, near_score, -1e+30)
        row_max = jnp.maximum(lax.optimization_barrier(jnp.max(near_score, axis=2)), self_score)
        self_exp = jnp.exp(self_score - row_max)
        near_exp = jnp.exp(near_score - row_max[:, :, None])
        denominator = self_exp + lax.optimization_barrier(jnp.sum(near_exp, axis=2))
        self_prob = self_exp / denominator
        near_prob = near_exp / denominator[:, :, None]
        return self_prob[:, :, None] * value_part + jnp.einsum('rhk,rkhd->rhd', near_prob, near_values, precision=highest)
    blocks_out = lax.map(jax.checkpoint(one_block), jnp.arange(NODES // block_rows, dtype=jnp.int32))
    return blocks_out.reshape(NODES, HEADS, HEAD_DIM)

def forward(node_input, ada_weight, qkv_weight, out_weight, up_weight, down_weight, sigma_embed, onehot, neighbours, validity):
    modulation = jnp.dot(sigma_embed, ada_weight, precision=highest)
    per_node = jnp.dot(onehot, modulation, precision=highest)
    scale_one = per_node[:, :WIDTH]
    shift_one = per_node[:, WIDTH:2 * WIDTH]
    scale_two = per_node[:, 2 * WIDTH:3 * WIDTH]
    shift_two = per_node[:, 3 * WIDTH:]
    normed_one = low(normalize(node_input) * (1.0 + scale_one) + shift_one)
    projected = low_back(low(jnp.dot(normed_one, qkv_weight, precision=highest)))
    projected = projected.reshape(NODES, HEADS, 3, HEAD_DIM)
    mixed = attend(projected[:, :, 0], projected[:, :, 1], projected[:, :, 2], neighbours, validity)
    heads_out = low_back(low(mixed.reshape(NODES, WIDTH)))
    branch = low_back(jnp.dot(heads_out, out_weight, precision=highest))
    middle = node_input + branch
    normed_two = low(normalize(middle) * (1.0 + scale_two) + shift_two)
    hidden_pre = low_back(jnp.dot(normed_two, up_weight, precision=highest))
    activated = low(hidden_pre * jax.nn.sigmoid(hidden_pre))
    return middle + jnp.dot(activated, down_weight, precision=highest)

def adamw_update(master, first, second, grad, rate, count_value):
    first_new = beta_rate * first + (1.0 - beta_rate) * grad
    second_new = beta_rate * second + (1.0 - beta_rate) * grad * grad
    correct = 1.0 - jnp.power(jnp.float32(beta_rate), count_value)
    normed_step = first_new / correct / (jnp.sqrt(second_new / correct) + adam_eps)
    master_new = master - rate * (normed_step + weight_decay * master)
    return (master_new, first_new, second_new)

def reference(node_input, cotangent, sigma_embed, neighbours, neighbour_valid, batch_counts, step_count, ada_master, ada_first, ada_second, qkv_master, qkv_first, qkv_second, out_master, out_first, out_second, up_master, up_first, up_second, down_master, down_first, down_second):
    onehot = batch_onehot(batch_counts)
    embed_values = sigma_embed.astype(jnp.float32)
    copies = [low(ada_master), low(qkv_master), low(out_master), low(up_master), low(down_master)]

    def layer(values, ada_weight, qkv_weight, out_weight, up_weight, down_weight):
        return forward(values, ada_weight, qkv_weight, out_weight, up_weight, down_weight, embed_values, onehot, neighbours, neighbour_valid)
    result, pullback = jax.vjp(layer, node_input.astype(jnp.float32), *copies)
    grads = pullback(cotangent.astype(jnp.float32))
    count_value = step_count[0].astype(jnp.float32)
    rates = [(4 * COND) ** (-0.5), (WIDTH // 2) ** (-0.5), (WIDTH // 4) ** (-0.5), WIDTH ** (-0.5), HIDDEN_SIZE ** (-0.5)]
    masters = [ada_master, qkv_master, out_master, up_master, down_master]
    firsts = [ada_first, qkv_first, out_first, up_first, down_first]
    seconds = [ada_second, qkv_second, out_second, up_second, down_second]
    updated = [adamw_update(masters[pos], firsts[pos], seconds[pos], grads[pos + 1], rates[pos], count_value) for pos in range(5)]
    return (result.astype(jnp.bfloat16), grads[0], updated[0][0], updated[0][1], updated[0][2], updated[1][0], updated[1][1], updated[1][2], updated[2][0], updated[2][1], updated[2][2], updated[3][0], updated[3][1], updated[3][2], updated[4][0], updated[4][1], updated[4][2])
```

```python
import functools
import math

import jax
import jax.numpy as jnp
from jax import lax
from jax.experimental import pallas as pl
from jax.experimental.pallas import tpu as pltpu
from jax.sharding import PartitionSpec as P


WIDTH = 512
HIDDEN_SIZE = 2048
COND = 512


norm_eps = 1e-06
beta_rate = 0.5
adam_eps = 1e-08
weight_decay = 0.1
highest = lax.Precision.HIGHEST


def passed_along(block, axis, distance):
    devices = range(lax.axis_size(axis))
    route = [((i - distance) % len(devices), i) for i in devices]
    return lax.ppermute(block, axis, route)


def norm_parts(values):
    centred = values - jnp.mean(values, axis=1, keepdims=True)
    inverse = lax.rsqrt(jnp.mean(centred * centred, axis=1, keepdims=True) + norm_eps)
    return (centred * inverse, inverse)


def norm_back(grad_normed, normed, inverse):
    first_mean = jnp.mean(grad_normed, axis=1, keepdims=True)
    second_mean = jnp.mean(grad_normed * normed, axis=1, keepdims=True)
    return inverse * (grad_normed - first_mean - normed * second_mean)


def adamw_update(master, first, second, grad, rate, count_value):
    first_new = beta_rate * first + (1.0 - beta_rate) * grad
    second_new = beta_rate * second + (1.0 - beta_rate) * grad * grad
    correct = 1.0 - jnp.power(jnp.float32(beta_rate), count_value)
    normed_step = first_new / correct / (jnp.sqrt(second_new / correct) + adam_eps)
    master_new = master - rate * (normed_step + weight_decay * master)
    return (master_new, first_new, second_new)


f32=jnp.float32; bf16=jnp.bfloat16
NT=(((1,),(1,)),((),()))
SPAN=256

def count_groups(cnt, hik, lok, rows):
    steps=hik.shape[0]
    parts=rows//SPAN
    total=5*parts*16
    rowid=lax.broadcasted_iota(jnp.int32,(total,1),0)
    rowkey=lax.div(rowid,16)*16+lax.rem(rowid,16)
    spot=lax.broadcasted_iota(jnp.int32,(SPAN,1),0)
    def body(g,_):
        keys=hik[pl.ds(g,1),:]
        low=lok[pl.ds(g,1),:]
        left=jnp.where(rowkey==keys,1.0,0.0).astype(bf16)
        right=jnp.where(spot==low,1.0,0.0).astype(bf16)
        made=lax.dot_general(left,right,NT,preferred_element_type=f32).astype(bf16)
        at=pl.multiple_of(g*16,16)
        for b in range(5):
            for p in range(parts):
                r=(b*parts+p)*16
                cnt[b,pl.ds(at,16),p*SPAN:(p+1)*SPAN]=made[r:r+16,:]
        return 0
    lax.fori_loop(0,steps,body,0)

def add_self(cnt, block, rows):
    eye=(lax.broadcasted_iota(jnp.int32,(SPAN,SPAN),0)==lax.broadcasted_iota(jnp.int32,(SPAN,SPAN),1))
    one=jnp.where(eye,1.0,0.0).astype(bf16)
    for p in range(rows//SPAN):
        s=slice(p*SPAN,(p+1)*SPAN)
        cnt[block,s,s]=cnt[block,s,s]+one

def attend_block(b, first, q, keys, vals, cnt, e, m, l, acc, fac, chunk, scale):
    rows=q.shape[0]
    lane=lax.broadcasted_iota(jnp.int32,(chunk,128),1)
    def body(i,_):
        at=pl.ds(pl.multiple_of(i*chunk,chunk),chunk)
        s=lax.dot_general(q[at,:],keys,NT,preferred_element_type=f32)*scale
        c=cnt[b,at,:].astype(f32)
        s=jnp.where(c>0,s,-1e30)
        top=jnp.max(s,axis=1,keepdims=True)
        if not first:
            old=m[at,0:1]
            top=jnp.maximum(top,old)
        w=(jnp.exp2(s-top)*c)
        total=jnp.sum(w,axis=1,keepdims=True)
        w=w.astype(bf16)
        e[b,at,:]=w
        out=jnp.dot(w,vals,preferred_element_type=f32)
        if first:
            acc[at,:]=out; l[at,:]=jnp.broadcast_to(total,(chunk,128))
            fac[at,:]=jnp.where(lane==b,top,0.0)
        else:
            shrink=jnp.exp2(old-top)
            acc[at,:]=acc[at,:]*shrink+out
            l[at,:]=l[at,:]*shrink+total
            fac[at,:]=jnp.where(lane==b,top,fac[at,:])
        m[at,:]=jnp.broadcast_to(top,(chunk,128))
        return 0
    lax.fori_loop(0,rows//chunk,body,0)

def fwd_kernel(order, self_block, scale, q, kv, hik, lok, att, e, fac, cnt, m, l):
    rows=q.shape[0]
    count_groups(cnt,hik,lok,rows)
    add_self(cnt,self_block,rows)
    for t,b in enumerate(order):
        attend_block(b,t==0,q,kv[b,:,:128],kv[b,:,128:],cnt,e,m,l,att,fac,256,scale)
    inv=1.0/l[...]
    att[...]=att[...]*inv
    fac[...]=jnp.exp2(fac[...]-m[...])*inv

def attention_fwd(q,kv,hik,lok,scale):
    rows=q.shape[0]
    V=pltpu.VMEM
    full=pl.BlockSpec(memory_space=V)
    return pl.pallas_call(functools.partial(fwd_kernel,(2,1,3,0,4),2,scale*math.log2(math.e)),
        out_shape=(jax.ShapeDtypeStruct((rows,128),f32),jax.ShapeDtypeStruct((5,rows,rows),bf16),jax.ShapeDtypeStruct((rows,128),f32)),
        in_specs=[full]*4,out_specs=(full,)*3,
        scratch_shapes=[V((5,rows,rows),bf16),V((rows,128),f32),V((rows,128),f32)],
        compiler_params=pltpu.CompilerParams(vmem_limit_bytes=60<<20),name="attend_fwd")(q,kv,hik,lok)

def back_block(b, q_t, do, fac, delta, kv, e, dq, dkv, first, chunk, keyscale):
    rows=do.shape[0]
    f=fac[:,b:b+1]
    dob=(do*f)
    dobh=dob.astype(bf16)
    d=-(delta*f)
    h=d.astype(bf16); r=d-h.astype(f32); h2=r.astype(bf16); h3=(r-h2.astype(f32)).astype(bf16)
    lane=lax.broadcasted_iota(jnp.int32,(rows,128),1)
    zero=jnp.zeros((rows,128),bf16)
    dcol=jnp.where(lane==0,h.astype(f32),jnp.where(lane==1,h2.astype(f32),jnp.where(lane==2,h3.astype(f32),0.0))).astype(bf16)
    left=jnp.concatenate([dobh,dcol],axis=1)
    dob_t=dobh.T
    ones=jnp.ones((chunk,128),bf16)
    for i in range(kv.shape[1]//chunk):
        s=slice(i*chunk,(i+1)*chunk)
        right=jnp.concatenate([kv[b,s,128:],ones],axis=1)
        dp=lax.dot_general(left,right,NT,preferred_element_type=f32)
        w=e[b,:,s]
        ds=(dp*w.astype(f32)).astype(bf16)
        dkv[b,:128,s]=jnp.dot(q_t,ds,preferred_element_type=f32)*keyscale
        dkv[b,128:,s]=jnp.dot(dob_t,w,preferred_element_type=f32)
        out=jnp.dot(ds,kv[b,s,:128],preferred_element_type=f32)
        if first and i==0: dq[...]=out
        else: dq[...]+=out

def bwd_kernel(scale, q, do, att, fac, kv, e, dq, dkv, ):
    q_t=q[...].T
    dof=do[...].astype(f32)
    delta=jnp.sum(dof*att[...],axis=1,keepdims=True)
    for t,b in enumerate((0,4,1,3,2)):
        back_block(b,q_t,dof,fac,delta,kv,e,dq,dkv,t==0,512,scale)
    dq[...]=dq[...]*scale

def attention_bwd(q,do,att,fac,kv,e,scale):
    rows=q.shape[0]
    V=pltpu.VMEM
    full=pl.BlockSpec(memory_space=V)
    return pl.pallas_call(functools.partial(bwd_kernel,scale),
        out_shape=(jax.ShapeDtypeStruct((rows,128),f32),jax.ShapeDtypeStruct((5,256,rows),f32)),
        in_specs=[full]*6,out_specs=(full,)*2,
        compiler_params=pltpu.CompilerParams(vmem_limit_bytes=60<<20),name="attend_bwd")(q,do,att,fac,kv,e)

def tables(slot_index, valid, rows):
    parts=rows//SPAN
    flat=slot_index.reshape(-1,256)
    ok=(valid>0).reshape(-1,256)
    node=lax.broadcasted_iota(jnp.int32,flat.shape,1)//16
    hi=jnp.where(ok,(flat//SPAN)*16+node,-1)
    lo=flat%SPAN
    return hi,lo


def per_device(
    node_input,
    cotangent,
    sigma_embed,
    neighbours,
    neighbour_valid,
    batch_counts,
    step_count,
    ada_master,
    ada_first,
    ada_second,
    qkv_master,
    qkv_first,
    qkv_second,
    out_master,
    out_first,
    out_second,
    up_master,
    up_first,
    up_second,
    down_master,
    down_first,
    down_second,
):
    f32 = jnp.float32
    bf16 = jnp.bfloat16
    node_rows = node_input.shape[0]
    model_width = node_input.shape[1]
    head_dim = qkv_master.shape[1] // 3
    score_scale = head_dim ** (-0.5)
    node_index = lax.axis_index("node")
    total_nodes = node_rows * lax.axis_size("node")
    qkv_full, out_full, up_full, down_full = (
        lax.all_gather(qkv_master.astype(bf16), "node", axis=0, tiled=True),
        lax.all_gather(out_master.astype(bf16), "node", axis=0, tiled=True),
        lax.all_gather(up_master.astype(bf16), "node", axis=0, tiled=True),
        lax.all_gather(down_master.astype(bf16), "node", axis=0, tiled=True),
    )
    cond_rows = ada_master.shape[0]
    sigma_part = lax.dynamic_slice_in_dim(sigma_embed, node_index * cond_rows, cond_rows, 1)
    limits = jnp.cumsum(batch_counts)[:-1]
    positions = node_index * node_rows + jnp.arange(node_rows, dtype=jnp.int32)
    member = jnp.sum((positions[:, None] >= limits[None, :]).astype(jnp.int32), axis=1)
    onehot = (
        member[:, None] == jnp.arange(batch_counts.shape[0], dtype=jnp.int32)[None, :]
    ).astype(f32)
    modulation = lax.psum(
        jnp.dot(sigma_part, ada_master.astype(bf16), preferred_element_type=f32), "node"
    )
    per_node = jnp.dot(onehot, modulation, precision=highest)
    scale_one = per_node[:, :model_width]
    shift_one = per_node[:, model_width : 2 * model_width]
    scale_two = per_node[:, 2 * model_width : 3 * model_width]
    shift_two = per_node[:, 3 * model_width :]
    normed_one, inverse_one = norm_parts(node_input.astype(f32))
    xn_one = (normed_one * (1.0 + scale_one) + shift_one).astype(bf16)
    projected = jnp.dot(xn_one, qkv_full, preferred_element_type=f32).astype(bf16)
    queries = projected[:, :head_dim]
    keys_values = projected[:, head_dim:]
    offsets = (-2, -1, 1, 2)
    fetched = {0: keys_values}
    for offset in offsets:
        fetched[offset] = passed_along(keys_values, "node", -offset)
    table = jnp.stack([fetched[offset] for offset in (-2, -1, 0, 1, 2)], axis=0)
    slot_index = jnp.mod(neighbours - (node_index - 2) * node_rows, total_nodes)
    high_keys, low_keys = tables(slot_index, neighbour_valid, node_rows)
    mixed, weights, factors = attention_fwd(queries, table, high_keys, low_keys, score_scale)
    heads_out = mixed.astype(bf16)
    branch = lax.psum(
        jnp.dot(heads_out, out_full, preferred_element_type=f32).astype(jnp.bfloat16), "head"
    ).astype(jnp.float32)
    middle = node_input.astype(f32) + branch
    normed_two, inverse_two = norm_parts(middle)
    xn_two = (normed_two * (1.0 + scale_two) + shift_two).astype(bf16)
    hidden_pre = jnp.dot(xn_two, up_full, preferred_element_type=f32)
    gate_sig = jax.nn.sigmoid(hidden_pre)
    activated = (hidden_pre * gate_sig).astype(bf16)
    mlp_sum = lax.psum(
        jnp.dot(activated, down_full, preferred_element_type=f32).astype(jnp.bfloat16), "head"
    ).astype(jnp.float32)
    node_output = (middle + mlp_sum).astype(bf16)
    down_grad = jnp.einsum("nf,nd->fd", activated, cotangent, preferred_element_type=f32)
    act_grad = jnp.einsum("nd,fd->nf", cotangent, down_full, preferred_element_type=f32)
    pre_grad = (act_grad * gate_sig * (1.0 + hidden_pre * (1.0 - gate_sig))).astype(bf16)
    up_grad = jnp.einsum("nw,nf->wf", xn_two, pre_grad, preferred_element_type=f32)
    normed_two_grad = lax.psum(
        jnp.einsum("nf,wf->nw", pre_grad, up_full, preferred_element_type=f32).astype(jnp.bfloat16),
        "head",
    ).astype(jnp.float32)
    middle_grad = cotangent.astype(f32) + norm_back(
        normed_two_grad * (1.0 + scale_two), normed_two, inverse_two
    )
    branch_grad = middle_grad.astype(bf16)
    out_grad = jnp.einsum("nh,nd->hd", heads_out, branch_grad, preferred_element_type=f32)
    mixed_grad = jnp.einsum("nd,hd->nh", branch_grad, out_full, preferred_element_type=f32).astype(
        bf16
    )
    query_grad, pair_sums = attention_bwd(
        queries, mixed_grad, mixed, factors, table, weights, score_scale
    )
    remote_terms = pair_sums[2]
    for offset in offsets:
        remote_terms = remote_terms + passed_along(
            pair_sums[offset + 2].astype(bf16), "node", offset
        ).astype(f32)
    key_value_grad = remote_terms.T
    projected_grad = jnp.concatenate([query_grad, key_value_grad], axis=1).astype(bf16)
    qkv_grad = jnp.einsum("nw,nc->wc", xn_one, projected_grad, preferred_element_type=f32)
    normed_one_grad = lax.psum(
        jnp.einsum("nc,wc->nw", projected_grad, qkv_full, preferred_element_type=f32).astype(
            jnp.bfloat16
        ),
        "head",
    ).astype(jnp.float32)
    input_grad = middle_grad + norm_back(
        normed_one_grad * (1.0 + scale_one), normed_one, inverse_one
    )
    rows_grad = jnp.concatenate(
        [
            normed_one_grad * normed_one,
            normed_one_grad,
            normed_two_grad * normed_two,
            normed_two_grad,
        ],
        axis=1,
    )
    batch_grad = jnp.dot(onehot.T, rows_grad, precision=highest)
    batch_grad = lax.psum(batch_grad, "node")
    ada_sum = jnp.dot(sigma_part.astype(f32).T, batch_grad, precision=highest)
    qkv_sum, out_sum, up_sum, down_sum = (
        lax.psum_scatter(qkv_grad, "node", scatter_dimension=0, tiled=True),
        lax.psum_scatter(out_grad, "node", scatter_dimension=0, tiled=True),
        lax.psum_scatter(up_grad, "node", scatter_dimension=0, tiled=True),
        lax.psum_scatter(down_grad, "node", scatter_dimension=0, tiled=True),
    )
    count_value = step_count[0].astype(f32)
    ada_res = adamw_update(
        ada_master, ada_first, ada_second, ada_sum, (4 * COND) ** (-0.5), count_value
    )
    qkv_res = adamw_update(
        qkv_master, qkv_first, qkv_second, qkv_sum, (WIDTH // 2) ** (-0.5), count_value
    )
    out_res = adamw_update(
        out_master, out_first, out_second, out_sum, (WIDTH // 4) ** (-0.5), count_value
    )
    up_res = adamw_update(up_master, up_first, up_second, up_sum, WIDTH ** (-0.5), count_value)
    down_res = adamw_update(
        down_master, down_first, down_second, down_sum, HIDDEN_SIZE ** (-0.5), count_value
    )
    return (
        node_output,
        input_grad,
        ada_res[0],
        ada_res[1],
        ada_res[2],
        qkv_res[0],
        qkv_res[1],
        qkv_res[2],
        out_res[0],
        out_res[1],
        out_res[2],
        up_res[0],
        up_res[1],
        up_res[2],
        down_res[0],
        down_res[1],
        down_res[2],
    )


def solution(mesh):
    placed = (
        P("node", None),
        P("node", None),
        P(),
        P("node", None),
        P("node", None),
        P(),
        P(),
        P("node", None),
        P("node", None),
        P("node", None),
        P("node", "head"),
        P("node", "head"),
        P("node", "head"),
        P(("head", "node"), None),
        P(("head", "node"), None),
        P(("head", "node"), None),
        P("node", "head"),
        P("node", "head"),
        P("node", "head"),
        P(("head", "node"), None),
        P(("head", "node"), None),
        P(("head", "node"), None),
    )
    return jax.shard_map(
        per_device,
        mesh=mesh,
        in_specs=placed,
        out_specs=(
            P("node", None),
            P("node", None),
            P("node", None),
            P("node", None),
            P("node", None),
            P("node", "head"),
            P("node", "head"),
            P("node", "head"),
            P(("head", "node"), None),
            P(("head", "node"), None),
            P(("head", "node"), None),
            P("node", "head"),
            P("node", "head"),
            P("node", "head"),
            P(("head", "node"), None),
            P(("head", "node"), None),
            P(("head", "node"), None),
        ),
        check_vma=False,
    )
```

```python
import functools
import math

import jax
import jax.numpy as jnp
from jax import lax
from jax.experimental import pallas as pl
from jax.experimental.pallas import tpu as pltpu
from jax.sharding import PartitionSpec as P

WIDTH = 512
HIDDEN_SIZE = 2048
COND = 512


norm_eps = 1e-06
beta_rate = 0.5
adam_eps = 1e-08
weight_decay = 0.1
highest = lax.Precision.HIGHEST


def passed_along(block, axis, distance):
    devices = range(lax.axis_size(axis))
    route = [((i - distance) % len(devices), i) for i in devices]
    return lax.ppermute(block, axis, route)


def norm_parts(values):
    centred = values - jnp.mean(values, axis=1, keepdims=True)
    inverse = lax.rsqrt(jnp.mean(centred * centred, axis=1, keepdims=True) + norm_eps)
    return (centred * inverse, inverse)


def norm_back(grad_normed, normed, inverse):
    first_mean = jnp.mean(grad_normed, axis=1, keepdims=True)
    second_mean = jnp.mean(grad_normed * normed, axis=1, keepdims=True)
    return inverse * (grad_normed - first_mean - normed * second_mean)


def adamw_update(master, first, second, grad, rate, count_value):
    first_new = beta_rate * first + (1.0 - beta_rate) * grad
    second_new = beta_rate * second + (1.0 - beta_rate) * grad * grad
    correct = 1.0 - jnp.power(jnp.float32(beta_rate), count_value)
    normed_step = first_new / correct / (jnp.sqrt(second_new / correct) + adam_eps)
    master_new = master - rate * (normed_step + weight_decay * master)
    return (master_new, first_new, second_new)


f32=jnp.float32; bf16=jnp.bfloat16
NT=(((1,),(1,)),((),()))
SPAN=256

def count_groups(cnt, hik, lok, rows, start, stop):
    parts=rows//SPAN
    total=5*parts*16
    rowid=lax.broadcasted_iota(jnp.int32,(total,1),0)
    spot=lax.broadcasted_iota(jnp.int32,(SPAN,1),0)
    def body(g,_):
        keys=hik[pl.ds(g,1),:]
        low=lok[pl.ds(g,1),:]
        left=jnp.where(rowid==keys,1.0,0.0).astype(bf16)
        right=jnp.where(spot==low,1.0,0.0).astype(bf16)
        made=lax.dot_general(left,right,NT,preferred_element_type=f32).astype(bf16)
        at=pl.multiple_of(g*16,16)
        for b in range(5):
            for p in range(parts):
                r=(b*parts+p)*16
                cnt[b,pl.ds(at,16),p*SPAN:(p+1)*SPAN]=made[r:r+16,:]
        return 0
    lax.fori_loop(start,stop,body,0)

def add_self(cnt, block, rows):
    eye=(lax.broadcasted_iota(jnp.int32,(SPAN,SPAN),0)==lax.broadcasted_iota(jnp.int32,(SPAN,SPAN),1))
    one=jnp.where(eye,1.0,0.0).astype(bf16)
    for p in range(rows//SPAN):
        s=slice(p*SPAN,(p+1)*SPAN)
        cnt[block,s,s]=cnt[block,s,s]+one

def attend_block(b, first, q, keys, vals, cnt, e, m, l, acc, fac, chunk, scale):
    rows=q.shape[0]
    lane=lax.broadcasted_iota(jnp.int32,(chunk,128),1)
    def body(i,_):
        at=pl.ds(pl.multiple_of(i*chunk,chunk),chunk)
        s=lax.dot_general(q[at,:],keys,NT,preferred_element_type=f32)*scale
        c=cnt[b,at,:].astype(f32)
        s=jnp.where(c>0,s,-1e30)
        top=jnp.max(s,axis=1,keepdims=True)
        if not first:
            old=m[at,0:1]
            top=jnp.maximum(top,old)
        w=(jnp.exp2(s-top)*c)
        total=jnp.sum(w,axis=1,keepdims=True)
        w=w.astype(bf16)
        e[b,at,:]=w
        out=jnp.dot(w,vals,preferred_element_type=f32)
        if first:
            acc[at,:]=out; l[at,:]=jnp.broadcast_to(total,(chunk,128))
            fac[at,:]=jnp.where(lane==b,top,0.0)
        else:
            shrink=jnp.exp2(old-top)
            acc[at,:]=acc[at,:]*shrink+out
            l[at,:]=l[at,:]*shrink+total
            fac[at,:]=jnp.where(lane==b,top,fac[at,:])
        m[at,:]=jnp.broadcast_to(top,(chunk,128))
        return 0
    lax.fori_loop(0,rows//chunk,body,0)

def fwd_kernel(order, self_block, scale, q, kv, hik, lok, att, e, fac, cnt, m, l):
    rows=q.shape[0]
    count_groups(cnt,hik,lok,rows,0,hik.shape[0])
    add_self(cnt,self_block,rows)
    for t,b in enumerate(order):
        attend_block(b,t==0,q,kv[b,:,:128],kv[b,:,128:],cnt,e,m,l,att,fac,256,scale)
    inv=1.0/l[...]
    att[...]=att[...]*inv
    fac[...]=jnp.exp2(fac[...]-m[...])*inv

def attention_fwd(q,kv,hik,lok,scale):
    rows=q.shape[0]
    V=pltpu.VMEM
    full=pl.BlockSpec(memory_space=V)
    return pl.pallas_call(functools.partial(fwd_kernel,(2,1,3,0,4),2,scale*math.log2(math.e)),
        out_shape=(jax.ShapeDtypeStruct((rows,128),f32),jax.ShapeDtypeStruct((5,rows,rows),bf16),jax.ShapeDtypeStruct((rows,128),f32)),
        in_specs=[full]*4,out_specs=(full,)*3,
        scratch_shapes=[V((5,rows,rows),bf16),V((rows,128),f32),V((rows,128),f32)],
        compiler_params=pltpu.CompilerParams(vmem_limit_bytes=60<<20),name="attend_fwd")(q,kv,hik,lok)

def back_block(b, q_t, do, fac, delta, kv, e, dq, write, first, chunk, keyscale):
    rows=do.shape[0]
    f=fac[:,b:b+1]
    dobh=(do*f).astype(bf16)
    d=-(delta*f)
    h=d.astype(bf16); r=d-h.astype(f32); h2=r.astype(bf16); h3=(r-h2.astype(f32)).astype(bf16)
    lane=lax.broadcasted_iota(jnp.int32,(rows,128),1)
    dcol=jnp.where(lane==0,h.astype(f32),jnp.where(lane==1,h2.astype(f32),jnp.where(lane==2,h3.astype(f32),0.0))).astype(bf16)
    left=jnp.concatenate([dobh,dcol],axis=1)
    dob_t=dobh.T
    ones=jnp.ones((chunk,128),bf16)
    for i in range(kv.shape[1]//chunk):
        s=slice(i*chunk,(i+1)*chunk)
        right=jnp.concatenate([kv[b,s,128:],ones],axis=1)
        dp=lax.dot_general(left,right,NT,preferred_element_type=f32)
        w=e[b,:,s]
        ds=(dp*w.astype(f32)).astype(bf16)
        write(slice(0,128),s,jnp.dot(q_t,ds,preferred_element_type=f32)*keyscale)
        write(slice(128,256),s,jnp.dot(dob_t,w,preferred_element_type=f32))
        out=jnp.dot(ds,kv[b,s,:128],preferred_element_type=f32)
        if first and i==0: dq[...]=out
        else: dq[...]+=out

def bwd_kernel(scale, q, do, att, fac, kv, e, dq, dkv, ):
    q_t=q[...].T
    dof=do[...].astype(f32)
    delta=jnp.sum(dof*att[...],axis=1,keepdims=True)
    for t,b in enumerate((0,4,1,3,2)):
        def write(r,s,v,b=b): dkv[b,r,s]=v
        back_block(b,q_t,dof,fac,delta,kv,e,dq,write,t==0,512,scale)
    dq[...]=dq[...]*scale

def attention_bwd(q,do,att,fac,kv,e,scale):
    rows=q.shape[0]
    V=pltpu.VMEM
    full=pl.BlockSpec(memory_space=V)
    return pl.pallas_call(functools.partial(bwd_kernel,scale),
        out_shape=(jax.ShapeDtypeStruct((rows,128),f32),jax.ShapeDtypeStruct((5,256,rows),f32)),
        in_specs=[full]*6,out_specs=(full,)*2,
        compiler_params=pltpu.CompilerParams(vmem_limit_bytes=60<<20),name="attend_bwd")(q,do,att,fac,kv,e)

def tables(slot_index, valid, rows):
    parts=rows//SPAN
    flat=slot_index.reshape(-1,256)
    ok=(valid>0).reshape(-1,256)
    node=lax.broadcasted_iota(jnp.int32,flat.shape,1)//16
    hi=jnp.where(ok,(flat//SPAN)*16+node,-1)
    lo=flat%SPAN
    return hi,lo


def by_batch(pos, limits, table, row, lanes):
    pick=[table[row+b:row+b+1,lanes] for b in range(4)]
    out=jnp.where(pos>=limits[0],pick[1],pick[0])
    out=jnp.where(pos>=limits[1],pick[2],out)
    return jnp.where(pos>=limits[2],pick[3],out)


def batch_limits(counts):
    return (counts[0],counts[0]+counts[1],counts[0]+counts[1]+counts[2])


class Links:
    def __init__(self, send, recv):
        self.send, self.recv, self.used = send, recv, 0

    def copy(self, src, dst, head, node):
        made=pltpu.make_async_remote_copy(src_ref=src,dst_ref=dst,send_sem=self.send.at[self.used],recv_sem=self.recv.at[self.used],
            device_id=(head,node),device_id_type=pl.DeviceIdType.MESH)
        self.used+=1
        return made


def meet(peers):
    barrier=pltpu.get_barrier_semaphore()
    for head,node in peers:
        pl.semaphore_signal(barrier,inc=1,device_id=(head,node),device_id_type=pl.DeviceIdType.MESH)
    pl.semaphore_wait(barrier,len(peers))


def front_kernel(scale, node_input, sigma, ada, qkv, out, up, down, counts, hik, lok,
        att, fac, queries, table, xn_one, modulation, qkv_full, out_full, up_full, down_full, e_out,
        e, cnt, m, l, normed, modp, modbuf, send, recv, store):
    head=lax.axis_index("head"); node=lax.axis_index("node")
    rows=node_input.shape[0]
    chunk=rows//4
    links=Links(send,recv)
    meet([(head,node^k) for k in range(1,8)]+[(head^k,node) for k in range(1,4)])
    limits=batch_limits(counts)
    own=pl.ds(pl.multiple_of(node*64,64),64)
    qkv_full[own,:]=qkv[...].astype(bf16)
    part=jnp.dot(sigma[...],ada[...].astype(bf16),preferred_element_type=f32)
    modp[0:4,:]=part[:,:1024]
    modp[4:8,:]=part[:,1024:]
    first=[]
    for k in range(1,8):
        first.append(links.copy(modp,modbuf.at[node],head,node^k)); first[-1].start()
        first.append(links.copy(qkv_full.at[own],qkv_full.at[own],head,node^k)); first[-1].start()
    cols=pl.ds(pl.multiple_of(head*512,512),512)
    own_out=pl.ds(pl.multiple_of(node*16,16),16)
    up_full[own,cols]=up[...].astype(bf16)
    down_full[head,own,:]=down[...].astype(bf16)
    out_full[head,own_out,:]=out[...].astype(bf16)
    along=[]
    for k in range(1,4):
        for ref in (up_full.at[own,cols],down_full.at[head,own],out_full.at[head,own_out]):
            along.append(links.copy(ref,ref,head^k,node)); along[-1].start()
    modbuf[node,:,:]=modp[...]
    def norm(i,_):
        at=pl.ds(pl.multiple_of(i*128,128),128)
        v=node_input[at,:].astype(f32)
        centred=v-jnp.mean(v,axis=1,keepdims=True)
        normed[at,:]=centred*lax.rsqrt(jnp.mean(centred*centred,axis=1,keepdims=True)+norm_eps)
        return 0
    lax.fori_loop(0,rows//128,norm,0)
    for c in first: c.wait()
    mod=modbuf[0]
    for k in range(1,8): mod=mod+modbuf[k]
    modulation[...]=mod
    across=[]; paired=[]
    for i in range(4):
        at=slice(i*chunk,(i+1)*chunk)
        pos=node*rows+i*chunk+lax.broadcasted_iota(jnp.int32,(chunk,1),0)
        xn=(normed[at,:]*(1.0+by_batch(pos,limits,modulation,0,slice(0,512)))+by_batch(pos,limits,modulation,0,slice(512,1024))).astype(bf16)
        xn_one[at,:]=xn
        proj=jnp.dot(xn,qkv_full[...],preferred_element_type=f32).astype(bf16)
        queries[at,:]=proj[:,:128]
        table[0,at,:]=proj[:,128:]
        across.append(links.copy(table.at[0,at],table.at[2,at],head,node^2)); across[-1].start()
        paired.append(links.copy(table.at[0,at],table.at[1,at],head,node^1)); paired[-1].start()
    onward=[]
    steps=hik.shape[0]
    def column(which):
        at=pl.ds(pl.multiple_of((node^which)*64,64),64); at_out=pl.ds(pl.multiple_of((node^which)*16,16),16)
        return [up_full.at[at],down_full.at[:,at],out_full.at[:,at_out]]
    for i in range(4):
        count_groups(cnt,hik,lok,rows,i*steps//4,(i+1)*steps//4)
        across[i].wait_recv()
        at=slice(i*chunk,(i+1)*chunk)
        onward.append(links.copy(table.at[2,at],table.at[3,at],head,node^4)); onward[-1].start()
        if i==2:
            for c in along: c.wait()
            mine=column(0)
            to_pair=[links.copy(r,r,head,node^1) for r in mine]
            to_x=[links.copy(r,r,head,node^2) for r in mine]
            to_y=[links.copy(r,r,head,node^4) for r in mine]
            for c in to_x+to_y+to_pair: c.start()
    add_self(cnt,0,rows)
    for c in across: c.wait_send()
    saved=[]
    def block(b,t):
        attend_block(b,t==0,queries,table[b,:,:128],table[b,:,128:],cnt,e,m,l,att,fac,256,scale)
        saved.append(pltpu.make_async_copy(e.at[b],e_out.at[b],store.at[b])); saved[-1].start()
    block(0,0)
    for c in paired: c.wait()
    block(1,1)
    for c in to_x: c.wait()
    for c in to_y: c.wait()
    from_x=column(2); from_y=column(4)
    cross=[links.copy(from_x[0],from_x[0],head,node^4)]+[links.copy(r,r,head,node^2) for r in from_y[1:]]
    for c in cross: c.start()
    hand=[links.copy(r,r,head,node^1) for r in from_x+from_y]
    for c in hand: c.start()
    for c in onward: c.wait()
    x_at=(node//2)%2; core=node%2
    fifth=links.copy(table.at[jnp.where(x_at==core,2,3)],table.at[4],head,node^1)
    fifth.start()
    block(2,2)
    block(3,3)
    for c in cross: c.wait()
    last=[links.copy(r,r,head,node^1) for r in column(6)]
    for c in last: c.start()
    fifth.wait()
    block(4,4)
    inv=1.0/l[...]
    att[...]=att[...]*inv
    fac[...]=jnp.exp2(fac[...]-m[...])*inv
    for c in to_pair+hand+last: c.wait()
    for c in saved: c.wait()


def front(node_input,sigma,ada,qkv,out,up,down,counts,hik,lok,scale):
    rows=node_input.shape[0]
    V=pltpu.VMEM
    full=pl.BlockSpec(memory_space=V)
    S=jax.ShapeDtypeStruct
    copies=14+9+8+4+9+9+1+3
    return pl.pallas_call(functools.partial(front_kernel,scale*math.log2(math.e)),
        out_shape=(S((rows,128),f32),S((rows,128),f32),S((rows,128),bf16),S((5,rows,256),bf16),S((rows,512),bf16),S((8,1024),f32),
            S((512,384),bf16),S((4,128,512),bf16),S((512,2048),bf16),S((4,512,512),bf16),S((5,rows,rows),bf16)),
        in_specs=[full]*7+[pl.BlockSpec(memory_space=pltpu.SMEM)]+[full]*2,
        out_specs=(full,)*10+(pl.BlockSpec(memory_space=pl.ANY),),
        scratch_shapes=[V((5,rows,rows),bf16),V((5,rows,rows),bf16),V((rows,128),f32),V((rows,128),f32),V((rows,512),f32),
            V((8,1024),f32),V((8,8,1024),f32),pltpu.SemaphoreType.DMA((copies,)),pltpu.SemaphoreType.DMA((copies,)),pltpu.SemaphoreType.DMA((5,))],
        compiler_params=pltpu.CompilerParams(vmem_limit_bytes=62<<20,collective_id=1,has_side_effects=True),
        name="front")(node_input,sigma,ada,qkv,out,up,down,counts,hik,lok)


def slots(neighbours, valid, node, rows):
    flat=neighbours.reshape(-1,256)
    ok=(valid>0).reshape(-1,256)
    which=(flat//rows)^node
    slot=jnp.where(which==6,3,jnp.where((which==3)|(which==7),4,which))
    local=flat%rows
    spot=lax.broadcasted_iota(jnp.int32,flat.shape,1)//16
    hi=jnp.where(ok,(slot*(rows//SPAN)+local//SPAN)*16+spot,-1)
    return hi,local%SPAN


def batch_sums(pos, limits, values):
    lane=lax.broadcasted_iota(jnp.int32,(pos.shape[0],8),1)
    member=(pos>=limits[0]).astype(jnp.int32)+(pos>=limits[1]).astype(jnp.int32)+(pos>=limits[2]).astype(jnp.int32)
    onehot=jnp.where(lane==member,1.0,0.0).astype(f32)
    return lax.dot_general(onehot,values,(((0,),(0,)),((),())),precision=highest,preferred_element_type=f32)[0:4,:]


def middle_kernel(node_input, cotangent, att, modulation, counts, out_full, up_full, down_full,
        do, dy, out_rows, up_grad, down_grad, out_grad, dmod,
        mixed, heads, do_rows, act, pre, send, recv):
    head=lax.axis_index("head"); node=lax.axis_index("node")
    rows=node_input.shape[0]
    part=rows//4
    links=Links(send,recv)
    mixed[...]=att[...].astype(bf16)
    meet([(head^k,node) for k in range(1,4)])
    lanes=pl.ds(pl.multiple_of(head*128,128),128)
    mine=pl.ds(pl.multiple_of(head*part,part),part)
    moved=[]
    for k in range(1,4):
        moved.append(links.copy(mixed.at[pl.ds(pl.multiple_of((head^k)*part,part),part)],heads.at[:,lanes],head^k,node)); moved[-1].start()
    heads[:,lanes]=mixed[mine,:]
    limits=batch_limits(counts)
    pos=node*rows+head*part+lax.broadcasted_iota(jnp.int32,(part,1),0)
    scale_two=1.0+by_batch(pos,limits,modulation,4,slice(0,512))
    shift_two=by_batch(pos,limits,modulation,4,slice(512,1024))
    g=cotangent[mine,:]
    for c in moved: c.wait()
    out_all=out_full[...].reshape(512,512)
    y=node_input[mine,:].astype(f32)+jnp.dot(heads[...],out_all,preferred_element_type=f32)
    n_two,inv_two=norm_parts(y)
    xn=(n_two*scale_two+shift_two).astype(bf16)
    mlp=jnp.zeros((part,512),f32); dxn=jnp.zeros((part,512),f32)
    for j in range(4):
        s=slice(j*512,(j+1)*512)
        h=jnp.dot(xn,up_full[:,s],preferred_element_type=f32)
        sig=1.0/(1.0+jnp.exp(-h))
        u=(h*sig).astype(bf16)
        act[:,s]=u
        mlp+=jnp.dot(u,down_full[j],preferred_element_type=f32)
        du=lax.dot_general(g,down_full[j],NT,preferred_element_type=f32)
        d=(du*sig*(1.0+h*(1.0-sig))).astype(bf16)
        pre[:,s]=d
        dxn+=lax.dot_general(d,up_full[:,s],NT,preferred_element_type=f32)
    dyv=g.astype(f32)+norm_back(dxn*scale_two,n_two,inv_two)
    dy[...]=dyv
    da=dyv.astype(bf16)
    do_rows[...]=lax.dot_general(da,out_all,NT,preferred_element_type=f32).astype(bf16)
    back=[]
    for k in range(1,4):
        back.append(links.copy(do_rows.at[:,pl.ds(pl.multiple_of((head^k)*128,128),128)],do.at[mine],head^k,node)); back[-1].start()
    do[mine,:]=do_rows[:,lanes]
    out_rows[...]=(y+mlp).astype(bf16)
    dmod[0:4,:]=jnp.zeros((4,1024),f32)
    dmod[4:8,0:512]=batch_sums(pos,limits,dxn*n_two)
    dmod[4:8,512:1024]=batch_sums(pos,limits,dxn)
    xn_t=xn.T
    heads_t=heads[...].T
    out_grad[...]=jnp.dot(heads_t,da,preferred_element_type=f32).astype(bf16).reshape(4,128,512)
    for j in range(4):
        s=slice(j*512,(j+1)*512)
        up_grad[:,s]=jnp.dot(xn_t,pre[:,s],preferred_element_type=f32).astype(bf16)
        down_grad[j]=jnp.dot(act[:,s].T,g,preferred_element_type=f32).astype(bf16)
    for c in back: c.wait()


def middle(node_input,cotangent,att,modulation,counts,out_full,up_full,down_full):
    rows=node_input.shape[0]
    part=rows//4
    V=pltpu.VMEM
    full=pl.BlockSpec(memory_space=V)
    S=jax.ShapeDtypeStruct
    return pl.pallas_call(middle_kernel,
        out_shape=(S((rows,128),bf16),S((part,512),f32),S((part,512),bf16),S((512,2048),bf16),S((4,512,512),bf16),S((4,128,512),bf16),S((8,1024),f32)),
        in_specs=[full]*4+[pl.BlockSpec(memory_space=pltpu.SMEM)]+[full]*3,
        out_specs=(full,)*7,
        scratch_shapes=[V((rows,128),bf16),V((part,512),bf16),V((part,512),bf16),V((part,2048),bf16),V((part,2048),bf16),
            pltpu.SemaphoreType.DMA((6,)),pltpu.SemaphoreType.DMA((6,))],
        compiler_params=pltpu.CompilerParams(vmem_limit_bytes=62<<20,collective_id=2,has_side_effects=True),
        name="middle")(node_input,cotangent,att,modulation,counts,out_full,up_full,down_full)


def back_kernel(scale, queries, do, att, fac, table, xn_one, qkv_full, dy, node_input, modulation, counts, out_rows,
        up_grad, down_grad, out_grad, dmod, e_in,
        node_output, input_grad, up_sum, down_sum, out_sum, qkv_sum, dmod_sum,
        e, dq, dkv, near, got_pair, got_y, got_x, got_one, proj_grad, partial, got_partial, rows_grad, row_all,
        up1, down1, out1, up2, down2, out2, up3, down3, out3, up_z, down_z, out_z, qkv_grad, qkv_got, dm_z, dm_own, dm_n,
        send, recv, load):
    head=lax.axis_index("head"); node=lax.axis_index("node")
    y_at=node//4; x_at=(node//2)%2; core=node%2
    rows=queries.shape[0]
    part=rows//4
    links=Links(send,recv)
    loads=[pltpu.make_async_copy(e_in.at[b],e.at[b],load.at[b]) for b in range(5)]
    order=(4,3,2,1,0)
    for b in order: loads[b].start()
    meet([(head,node^k) for k in range(1,8)]+[(head^k,node) for k in range(1,4)])
    mine=pl.ds(pl.multiple_of(head*part,part),part)
    shown=[]
    for k in range(1,4):
        shown.append(links.copy(out_rows,node_output.at[mine],head^k,node)); shown[-1].start()
    node_output[mine,:]=out_rows[...]
    stage1=[links.copy(up_grad.at[:,1-core],up1,head,node^1),links.copy(down_grad.at[:,:,1-core],down1,head,node^1),links.copy(out_grad.at[:,:,1-core],out1,head,node^1)]
    for c in stage1: c.start()
    q_t=queries[...].T
    dof=do[...].astype(f32)
    delta=jnp.sum(dof*att[...],axis=1,keepdims=True)
    def block(b):
        loads[b].wait()
        def write(r,s,v):
            if b==0: dkv[r,s]=v
            else: near[b,r,s]=v.astype(bf16)
        back_block(b,q_t,dof,fac,delta,table,e,dq,write,b==order[0],512,scale)
    block(4)
    give=links.copy(near.at[4],got_pair,head,node^1); give.start()
    block(3)
    give.wait()
    @pl.when(x_at!=core)
    def _(): near[3]=(near[3].astype(f32)+got_pair[...].astype(f32)).astype(bf16)
    via_y=[]
    for i in range(4):
        s=slice(i*part,(i+1)*part)
        via_y.append(links.copy(near.at[3,:,s],got_y.at[:,s],head,node^4)); via_y[-1].start()
    for c in stage1: c.wait()
    for i in range(4):
        up1[i]=(up1[i].astype(f32)+up_grad[i,core].astype(f32)).astype(bf16)
        down1[i]=(down1[i].astype(f32)+down_grad[i,:,core].astype(f32)).astype(bf16)
        out1[i]=(out1[i].astype(f32)+out_grad[i,:,core].astype(f32)).astype(bf16)
    stage2=[]
    for i in range(2):
        stage2.append(links.copy(up1.at[i*2+1-x_at],up2.at[i],head,node^2))
    there=pl.ds((1-y_at)*2,2)
    stage2+=[links.copy(down1.at[:,there],down2,head,node^4),links.copy(out1.at[:,there],out2,head,node^4)]
    for c in stage2: c.start()
    block(2)
    @pl.when(x_at==core)
    def _(): near[2]=(near[2].astype(f32)+got_pair[...].astype(f32)).astype(bf16)
    via_x=[]
    def pass_on(i):
        s=slice(i*part,(i+1)*part)
        via_y[i].wait()
        near[2,:,s]=(near[2,:,s].astype(f32)+got_y[:,s].astype(f32)).astype(bf16)
        via_x.append(links.copy(near.at[2,:,s],got_x.at[:,s],head,node^2)); via_x[-1].start()
    pass_on(0)
    block(1)
    one=links.copy(near.at[1],got_one,head,node^1); one.start()
    pass_on(1)
    pass_on(2)
    block(0)
    pass_on(3)
    for c in stage2: c.wait()
    for i in range(2):
        up2[i]=(up2[i].astype(f32)+up1[i*2+x_at].astype(f32)).astype(bf16)
    here=pl.ds(y_at*2,2)
    down2[...]=(down2[...].astype(f32)+down1[:,here].astype(f32)).astype(bf16)
    out2[...]=(out2[...].astype(f32)+out1[:,here].astype(f32)).astype(bf16)
    stage3=[links.copy(up2.at[1-y_at],up3,head,node^4),links.copy(down2.at[:,1-x_at],down3,head,node^2),links.copy(out2.at[:,1-x_at],out3,head,node^2)]
    for c in stage3: c.start()
    xn_t=xn_one[...].T
    one.wait()
    for i in range(4):
        s=slice(i*part,(i+1)*part)
        via_x[i].wait()
        total=dkv[:,s]+got_one[:,s].astype(f32)+got_x[:,s].astype(f32)
        proj_grad[s,128:]=total.T.astype(bf16)
        proj_grad[s,:128]=(dq[s,:]*scale).astype(bf16)
        partial[i]=lax.dot_general(proj_grad[s,:],qkv_full[...],NT,preferred_element_type=f32).astype(bf16)
    reduce=[]
    for k in range(1,4):
        reduce.append(links.copy(partial.at[head^k],got_partial.at[k-1],head^k,node)); reduce[-1].start()
    made=jnp.dot(xn_t,proj_grad[...],preferred_element_type=f32).astype(bf16)
    qkv_grad[...]=made.reshape(8,64,384)
    qkv_moves=[]
    for k in range(1,8):
        qkv_moves.append(links.copy(qkv_grad.at[node^k],qkv_got.at[k-1],head,node^k)); qkv_moves[-1].start()
    for c in stage3: c.wait()
    up3[...]=(up3[...].astype(f32)+up2[y_at].astype(f32)).astype(bf16)
    down3[...]=(down3[...].astype(f32)+down2[:,x_at].astype(f32)).astype(bf16)
    out3[...]=(out3[...].astype(f32)+out2[:,x_at].astype(f32)).astype(bf16)
    stage4=[]
    for k in range(1,4):
        cols=pl.ds(pl.multiple_of((head^k)*512,512),512)
        stage4+=[links.copy(up3.at[:,cols],up_z.at[k-1],head^k,node),links.copy(down3.at[head^k],down_z.at[k-1],head^k,node),links.copy(out3.at[head^k],out_z.at[k-1],head^k,node)]
    limits=batch_limits(counts)
    pos=node*rows+head*part+lax.broadcasted_iota(jnp.int32,(part,1),0)
    scale_one=1.0+by_batch(pos,limits,modulation,0,slice(0,512))
    n_one,inv_one=norm_parts(node_input[mine,:].astype(f32))
    for c in reduce: c.wait()
    dxn=partial[head].astype(f32)
    for k in range(3): dxn=dxn+got_partial[k].astype(f32)
    rows_grad[...]=(dy[...]+norm_back(dxn*scale_one,n_one,inv_one)).astype(bf16)
    spread=[]
    for k in range(1,4):
        spread.append(links.copy(rows_grad,row_all.at[head],head^k,node)); spread[-1].start()
    row_all[head,:,:]=rows_grad[...]
    dm_own[0:4,0:512]=batch_sums(pos,limits,dxn*n_one)
    dm_own[0:4,512:1024]=batch_sums(pos,limits,dxn)
    dm_own[4:8,:]=dmod[4:8,:]
    dm_moves=[]
    for k in range(1,4):
        dm_moves.append(links.copy(dm_own,dm_z.at[head],head^k,node)); dm_moves[-1].start()
    dm_z[head,:,:]=dm_own[...]
    for c in stage4: c.start()
    for c in dm_moves: c.wait()
    dm_own[...]=dm_z[0]+dm_z[1]+dm_z[2]+dm_z[3]
    dm_last=[]
    for k in range(1,8):
        dm_last.append(links.copy(dm_own,dm_n.at[node],head,node^k)); dm_last[-1].start()
    dm_n[node,:,:]=dm_own[...]
    for c in qkv_moves: c.wait()
    total=qkv_grad[node].astype(f32)
    for k in range(7): total=total+qkv_got[k].astype(f32)
    qkv_sum[...]=total
    for c in dm_last: c.wait()
    total=dm_n[0]
    for k in range(1,8): total=total+dm_n[k]
    dmod_sum[...]=total
    for c in stage4: c.wait()
    cols=pl.ds(pl.multiple_of(head*512,512),512)
    up_sum[...]=up3[:,cols].astype(f32)+up_z[0].astype(f32)+up_z[1].astype(f32)+up_z[2].astype(f32)
    down_sum[...]=down3[head].astype(f32)+down_z[0].astype(f32)+down_z[1].astype(f32)+down_z[2].astype(f32)
    out_sum[...]=out3[head].astype(f32)+out_z[0].astype(f32)+out_z[1].astype(f32)+out_z[2].astype(f32)
    for c in spread: c.wait()
    for i in range(4):
        input_grad[i*part:(i+1)*part,:]=row_all[i].astype(f32)
    for c in shown: c.wait()


def back(queries,do,att,fac,table,xn_one,qkv_full,dy,node_input,modulation,counts,out_rows,up_grad,down_grad,out_grad,dmod,e,scale):
    rows=queries.shape[0]
    part=rows//4
    V=pltpu.VMEM
    full=pl.BlockSpec(memory_space=V)
    S=jax.ShapeDtypeStruct
    copies=3+3+1+4+4+4+1+3+3+7+9+3+3+7
    return pl.pallas_call(functools.partial(back_kernel,scale),
        out_shape=(S((rows,512),bf16),S((rows,512),f32),S((64,512),f32),S((64,512),f32),S((16,512),f32),S((64,384),f32),S((8,1024),f32)),
        in_specs=[full]*10+[pl.BlockSpec(memory_space=pltpu.SMEM)]+[full]*5+[pl.BlockSpec(memory_space=pl.ANY)],
        out_specs=(full,)*7,
        scratch_shapes=[V((5,rows,rows),bf16),V((rows,128),f32),V((256,rows),f32),V((5,256,rows),bf16),
            V((256,rows),bf16),V((256,rows),bf16),V((256,rows),bf16),V((256,rows),bf16),
            V((rows,384),bf16),V((4,part,512),bf16),V((3,part,512),bf16),V((part,512),bf16),V((4,part,512),bf16),
            V((4,64,2048),bf16),V((4,4,64,512),bf16),V((4,4,16,512),bf16),
            V((2,64,2048),bf16),V((4,2,64,512),bf16),V((4,2,16,512),bf16),
            V((64,2048),bf16),V((4,64,512),bf16),V((4,16,512),bf16),
            V((3,64,512),bf16),V((3,64,512),bf16),V((3,16,512),bf16),
            V((8,64,384),bf16),V((7,64,384),bf16),V((4,8,1024),f32),V((8,1024),f32),V((8,8,1024),f32),
            pltpu.SemaphoreType.DMA((copies,)),pltpu.SemaphoreType.DMA((copies,)),pltpu.SemaphoreType.DMA((5,))],
        compiler_params=pltpu.CompilerParams(vmem_limit_bytes=62<<20,collective_id=3,has_side_effects=True),
        name="back")(queries,do,att,fac,table,xn_one,qkv_full,dy,node_input,modulation,counts,out_rows,
            up_grad.reshape(4,2,64,2048),down_grad.reshape(4,4,2,64,512),out_grad.reshape(4,4,2,16,512),dmod,e)


def per_device_near(
    node_input, cotangent, sigma_embed, neighbours, neighbour_valid, batch_counts, step_count,
    ada_master, ada_first, ada_second, qkv_master, qkv_first, qkv_second, out_master, out_first, out_second,
    up_master, up_first, up_second, down_master, down_first, down_second,
):
    rows=node_input.shape[0]
    node=lax.axis_index("node")
    scale=128**-0.5
    sigma_part=lax.dynamic_slice_in_dim(sigma_embed,node*64,64,1)
    hik,lok=slots(neighbours,neighbour_valid,node,rows)
    att,fac,queries,table,xn_one,modulation,qkv_full,out_full,up_full,down_full,e=front(
        node_input,sigma_part,ada_master,qkv_master,out_master,up_master,down_master,batch_counts,hik,lok,scale)
    do,dy,out_rows,up_grad,down_grad,out_grad,dmod=middle(
        node_input,cotangent,att,modulation,batch_counts,out_full,up_full,down_full)
    node_output,input_grad,up_sum,down_sum,out_sum,qkv_sum,dmod_sum=back(
        queries,do,att,fac,table,xn_one,qkv_full,dy,node_input,modulation,batch_counts,out_rows,up_grad,down_grad,out_grad,dmod,e,scale)
    batch_grad=jnp.concatenate([dmod_sum[:4],dmod_sum[4:]],axis=1)
    ada_sum=jnp.dot(sigma_part.astype(f32).T,batch_grad,precision=highest)
    count_value=step_count[0].astype(f32)
    ada_res=adamw_update(ada_master,ada_first,ada_second,ada_sum,(4*COND)**(-0.5),count_value)
    qkv_res=adamw_update(qkv_master,qkv_first,qkv_second,qkv_sum,(WIDTH//2)**(-0.5),count_value)
    out_res=adamw_update(out_master,out_first,out_second,out_sum,(WIDTH//4)**(-0.5),count_value)
    up_res=adamw_update(up_master,up_first,up_second,up_sum,WIDTH**(-0.5),count_value)
    down_res=adamw_update(down_master,down_first,down_second,down_sum,HIDDEN_SIZE**(-0.5),count_value)
    return (node_output,input_grad)+ada_res+qkv_res+out_res+up_res+down_res


def per_device(
    node_input,
    cotangent,
    sigma_embed,
    neighbours,
    neighbour_valid,
    batch_counts,
    step_count,
    ada_master,
    ada_first,
    ada_second,
    qkv_master,
    qkv_first,
    qkv_second,
    out_master,
    out_first,
    out_second,
    up_master,
    up_first,
    up_second,
    down_master,
    down_first,
    down_second,
):
    f32 = jnp.float32
    bf16 = jnp.bfloat16
    node_rows = node_input.shape[0]
    model_width = node_input.shape[1]
    head_dim = qkv_master.shape[1] // 3
    score_scale = head_dim ** (-0.5)
    node_index = lax.axis_index("node")
    total_nodes = node_rows * lax.axis_size("node")
    qkv_full, out_full, up_full, down_full = (
        lax.all_gather(qkv_master.astype(bf16), "node", axis=0, tiled=True),
        lax.all_gather(out_master.astype(bf16), "node", axis=0, tiled=True),
        lax.all_gather(up_master.astype(bf16), "node", axis=0, tiled=True),
        lax.all_gather(down_master.astype(bf16), "node", axis=0, tiled=True),
    )
    cond_rows = ada_master.shape[0]
    sigma_part = lax.dynamic_slice_in_dim(sigma_embed, node_index * cond_rows, cond_rows, 1)
    limits = jnp.cumsum(batch_counts)[:-1]
    positions = node_index * node_rows + jnp.arange(node_rows, dtype=jnp.int32)
    member = jnp.sum((positions[:, None] >= limits[None, :]).astype(jnp.int32), axis=1)
    onehot = (
        member[:, None] == jnp.arange(batch_counts.shape[0], dtype=jnp.int32)[None, :]
    ).astype(f32)
    modulation = lax.psum(
        jnp.dot(sigma_part, ada_master.astype(bf16), preferred_element_type=f32), "node"
    )
    per_node = jnp.dot(onehot, modulation, precision=highest)
    scale_one = per_node[:, :model_width]
    shift_one = per_node[:, model_width : 2 * model_width]
    scale_two = per_node[:, 2 * model_width : 3 * model_width]
    shift_two = per_node[:, 3 * model_width :]
    normed_one, inverse_one = norm_parts(node_input.astype(f32))
    xn_one = (normed_one * (1.0 + scale_one) + shift_one).astype(bf16)
    projected = jnp.dot(xn_one, qkv_full, preferred_element_type=f32).astype(bf16)
    queries = projected[:, :head_dim]
    keys_values = projected[:, head_dim:]
    offsets = (-2, -1, 1, 2)
    fetched = {0: keys_values}
    for offset in offsets:
        fetched[offset] = passed_along(keys_values, "node", -offset)
    table = jnp.stack([fetched[offset] for offset in (-2, -1, 0, 1, 2)], axis=0)
    slot_index = jnp.mod(neighbours - (node_index - 2) * node_rows, total_nodes)
    high_keys, low_keys = tables(slot_index, neighbour_valid, node_rows)
    mixed, weights, factors = attention_fwd(queries, table, high_keys, low_keys, score_scale)
    heads_out = mixed.astype(bf16)
    branch = lax.psum(
        jnp.dot(heads_out, out_full, preferred_element_type=f32).astype(jnp.bfloat16), "head"
    ).astype(jnp.float32)
    middle = node_input.astype(f32) + branch
    normed_two, inverse_two = norm_parts(middle)
    xn_two = (normed_two * (1.0 + scale_two) + shift_two).astype(bf16)
    hidden_pre = jnp.dot(xn_two, up_full, preferred_element_type=f32)
    gate_sig = jax.nn.sigmoid(hidden_pre)
    activated = (hidden_pre * gate_sig).astype(bf16)
    mlp_sum = lax.psum(
        jnp.dot(activated, down_full, preferred_element_type=f32).astype(jnp.bfloat16), "head"
    ).astype(jnp.float32)
    node_output = (middle + mlp_sum).astype(bf16)
    down_grad = jnp.einsum("nf,nd->fd", activated, cotangent, preferred_element_type=f32)
    act_grad = jnp.einsum("nd,fd->nf", cotangent, down_full, preferred_element_type=f32)
    pre_grad = (act_grad * gate_sig * (1.0 + hidden_pre * (1.0 - gate_sig))).astype(bf16)
    up_grad = jnp.einsum("nw,nf->wf", xn_two, pre_grad, preferred_element_type=f32)
    normed_two_grad = lax.psum(
        jnp.einsum("nf,wf->nw", pre_grad, up_full, preferred_element_type=f32).astype(jnp.bfloat16),
        "head",
    ).astype(jnp.float32)
    middle_grad = cotangent.astype(f32) + norm_back(
        normed_two_grad * (1.0 + scale_two), normed_two, inverse_two
    )
    branch_grad = middle_grad.astype(bf16)
    out_grad = jnp.einsum("nh,nd->hd", heads_out, branch_grad, preferred_element_type=f32)
    mixed_grad = jnp.einsum("nd,hd->nh", branch_grad, out_full, preferred_element_type=f32).astype(
        bf16
    )
    query_grad, pair_sums = attention_bwd(
        queries, mixed_grad, mixed, factors, table, weights, score_scale
    )
    remote_terms = pair_sums[2]
    for offset in offsets:
        remote_terms = remote_terms + passed_along(
            pair_sums[offset + 2].astype(bf16), "node", offset
        ).astype(f32)
    key_value_grad = remote_terms.T
    projected_grad = jnp.concatenate([query_grad, key_value_grad], axis=1).astype(bf16)
    qkv_grad = jnp.einsum("nw,nc->wc", xn_one, projected_grad, preferred_element_type=f32)
    normed_one_grad = lax.psum(
        jnp.einsum("nc,wc->nw", projected_grad, qkv_full, preferred_element_type=f32).astype(
            jnp.bfloat16
        ),
        "head",
    ).astype(jnp.float32)
    input_grad = middle_grad + norm_back(
        normed_one_grad * (1.0 + scale_one), normed_one, inverse_one
    )
    rows_grad = jnp.concatenate(
        [
            normed_one_grad * normed_one,
            normed_one_grad,
            normed_two_grad * normed_two,
            normed_two_grad,
        ],
        axis=1,
    )
    batch_grad = jnp.dot(onehot.T, rows_grad, precision=highest)
    batch_grad = lax.psum(batch_grad, "node")
    ada_sum = jnp.dot(sigma_part.astype(f32).T, batch_grad, precision=highest)
    qkv_sum, out_sum, up_sum, down_sum = (
        lax.psum_scatter(qkv_grad, "node", scatter_dimension=0, tiled=True),
        lax.psum_scatter(out_grad, "node", scatter_dimension=0, tiled=True),
        lax.psum_scatter(up_grad, "node", scatter_dimension=0, tiled=True),
        lax.psum_scatter(down_grad, "node", scatter_dimension=0, tiled=True),
    )
    count_value = step_count[0].astype(f32)
    ada_res = adamw_update(
        ada_master, ada_first, ada_second, ada_sum, (4 * COND) ** (-0.5), count_value
    )
    qkv_res = adamw_update(
        qkv_master, qkv_first, qkv_second, qkv_sum, (WIDTH // 2) ** (-0.5), count_value
    )
    out_res = adamw_update(
        out_master, out_first, out_second, out_sum, (WIDTH // 4) ** (-0.5), count_value
    )
    up_res = adamw_update(up_master, up_first, up_second, up_sum, WIDTH ** (-0.5), count_value)
    down_res = adamw_update(
        down_master, down_first, down_second, down_sum, HIDDEN_SIZE ** (-0.5), count_value
    )
    return (
        node_output,
        input_grad,
        ada_res[0],
        ada_res[1],
        ada_res[2],
        qkv_res[0],
        qkv_res[1],
        qkv_res[2],
        out_res[0],
        out_res[1],
        out_res[2],
        up_res[0],
        up_res[1],
        up_res[2],
        down_res[0],
        down_res[1],
        down_res[2],
    )


def solution(mesh):
    chosen = per_device_near if mesh.shape["node"] == 8 and mesh.shape["head"] == 4 else per_device
    placed = (
        P("node", None),
        P("node", None),
        P(),
        P("node", None),
        P("node", None),
        P(),
        P(),
        P("node", None),
        P("node", None),
        P("node", None),
        P("node", "head"),
        P("node", "head"),
        P("node", "head"),
        P(("head", "node"), None),
        P(("head", "node"), None),
        P(("head", "node"), None),
        P("node", "head"),
        P("node", "head"),
        P("node", "head"),
        P(("head", "node"), None),
        P(("head", "node"), None),
        P(("head", "node"), None),
    )
    return jax.shard_map(
        chosen,
        mesh=mesh,
        in_specs=placed,
        out_specs=(
            P("node", None),
            P("node", None),
            P("node", None),
            P("node", None),
            P("node", None),
            P("node", "head"),
            P("node", "head"),
            P("node", "head"),
            P(("head", "node"), None),
            P(("head", "node"), None),
            P(("head", "node"), None),
            P("node", "head"),
            P("node", "head"),
            P("node", "head"),
            P(("head", "node"), None),
            P(("head", "node"), None),
            P(("head", "node"), None),
        ),
        check_vma=False,
    )
```

```python
import functools
import math

import jax
import jax.numpy as jnp
from jax import lax
from jax.experimental import pallas as pl
from jax.experimental.pallas import tpu as pltpu
from jax.sharding import PartitionSpec as P


WIDTH = 512
HIDDEN_SIZE = 2048
COND = 512


norm_eps = 1e-06
beta_rate = 0.5
adam_eps = 1e-08
weight_decay = 0.1
highest = lax.Precision.HIGHEST


def passed_along(block, axis, distance):
    devices = range(lax.axis_size(axis))
    route = [((i - distance) % len(devices), i) for i in devices]
    return lax.ppermute(block, axis, route)


def norm_parts(values):
    centred = values - jnp.mean(values, axis=1, keepdims=True)
    inverse = lax.rsqrt(jnp.mean(centred * centred, axis=1, keepdims=True) + norm_eps)
    return (centred * inverse, inverse)


def norm_back(grad_normed, normed, inverse):
    first_mean = jnp.mean(grad_normed, axis=1, keepdims=True)
    second_mean = jnp.mean(grad_normed * normed, axis=1, keepdims=True)
    return inverse * (grad_normed - first_mean - normed * second_mean)


def adamw_update(master, first, second, grad, rate, count_value):
    first_new = beta_rate * first + (1.0 - beta_rate) * grad
    second_new = beta_rate * second + (1.0 - beta_rate) * grad * grad
    correct = 1.0 - jnp.power(jnp.float32(beta_rate), count_value)
    normed_step = first_new / correct / (jnp.sqrt(second_new / correct) + adam_eps)
    master_new = master - rate * (normed_step + weight_decay * master)
    return (master_new, first_new, second_new)


f32=jnp.float32; bf16=jnp.bfloat16
NT=(((1,),(1,)),((),()))
SPAN=256

def count_groups(cnt, code, rows, start, stop, step):
    parts=rows//SPAN
    total=5*parts*16
    short=jnp.int16
    rowid=lax.broadcasted_iota(jnp.int32,(total,SPAN),0).astype(short)
    spot=lax.broadcasted_iota(jnp.int32,(SPAN,SPAN),0).astype(short)
    one=bf16(1); zero=bf16(0)
    def group(g):
        both=code[pl.ds(g,1),:]
        keys=lax.shift_right_arithmetic(both,8).astype(short)
        low=lax.bitwise_and(both,255).astype(short)
        left=jnp.where(rowid==jnp.broadcast_to(keys,(total,SPAN)),one,zero)
        right=jnp.where(spot==jnp.broadcast_to(low,(SPAN,SPAN)),one,zero)
        made=lax.dot_general(left,right,NT,preferred_element_type=f32).astype(bf16)
        at=pl.multiple_of(g*16,16)
        for b in range(5):
            for p in range(parts):
                r=(b*parts+p)*16
                cnt[b,pl.ds(at,16),p*SPAN:(p+1)*SPAN]=made[r:r+16,:]
    def body(g,_):
        for u in range(step): group(g*step+u)
        return 0
    lax.fori_loop(start//step,stop//step,body,0)

def add_self(cnt, block, rows):
    eye=(lax.broadcasted_iota(jnp.int32,(SPAN,SPAN),0)==lax.broadcasted_iota(jnp.int32,(SPAN,SPAN),1))
    one=jnp.where(eye,1.0,0.0).astype(bf16)
    for p in range(rows//SPAN):
        s=slice(p*SPAN,(p+1)*SPAN)
        cnt[block,s,s]=cnt[block,s,s]+one

def attend_rows(b, first, at, q, table, e, m, l, acc, fac, scale):
    size=at.stop-at.start
    lane=lax.broadcasted_iota(jnp.int32,(size,128),1)
    s=lax.dot_general(q[at,:],table[b,:,0:128],NT,preferred_element_type=f32)*scale
    c=e[b,at,:].astype(f32)
    s=jnp.where(c>0,s,-1e30)
    top=jnp.max(s,axis=1,keepdims=True)
    if not first:
        old=m[at,0:1]
        top=jnp.maximum(top,old)
    w=(jnp.exp2(s-top)*c).astype(bf16)
    e[b,at,:]=w
    out=jnp.dot(w,table[b,:,128:384],preferred_element_type=f32)
    if first:
        acc[at,:]=out[:,:128]; l[at,:]=out[:,128:]
        fac[at,:]=jnp.where(lane==b,top,0.0)
    else:
        shrink=jnp.exp2(old-top)
        acc[at,:]=acc[at,:]*shrink+out[:,:128]
        l[at,:]=l[at,:]*shrink+out[:,128:]
        fac[at,:]=jnp.where(lane==b,top,fac[at,:])
    m[at,:]=jnp.broadcast_to(top,(size,128))

def back_block(b, q_t, dof, fac, delta, table, e, dq, write, first, chunk, keyscale):
    rows=dof.shape[0]
    f=fac[:,b:b+1]
    dobh=(dof*f).astype(bf16)
    d=-(delta*f)
    h=d.astype(bf16); r=d-h.astype(f32); h2=r.astype(bf16); h3=(r-h2.astype(f32)).astype(bf16)
    lane=lax.broadcasted_iota(jnp.int32,(rows,128),1)
    dcol=jnp.where(lane==0,h.astype(f32),jnp.where(lane==1,h2.astype(f32),jnp.where(lane==2,h3.astype(f32),0.0))).astype(bf16)
    left=jnp.concatenate([dobh,dcol],axis=1)
    dob_t=dobh.T
    for i in range(rows//chunk):
        s=slice(i*chunk,(i+1)*chunk)
        dp=lax.dot_general(left,table[b,s,128:384],NT,preferred_element_type=f32)
        w=e[b,:,s]
        ds=(dp*w.astype(f32)).astype(bf16)
        write(slice(0,128),s,jnp.dot(q_t,ds,preferred_element_type=f32)*keyscale)
        write(slice(128,256),s,jnp.dot(dob_t,w,preferred_element_type=f32))
        out=jnp.dot(ds,table[b,s,0:128],preferred_element_type=f32)
        if first and i==0: dq[...]=out
        else: dq[...]+=out


def by_batch(pos, limits, table, row, lanes):
    pick=[table[row+b:row+b+1,lanes] for b in range(4)]
    out=jnp.where(pos>=limits[0],pick[1],pick[0])
    out=jnp.where(pos>=limits[1],pick[2],out)
    return jnp.where(pos>=limits[2],pick[3],out)


def batch_sums(pos, limits, values):
    lane=lax.broadcasted_iota(jnp.int32,(pos.shape[0],8),1)
    member=(pos>=limits[0]).astype(jnp.int32)+(pos>=limits[1]).astype(jnp.int32)+(pos>=limits[2]).astype(jnp.int32)
    onehot=jnp.where(lane==member,1.0,0.0).astype(f32)
    return lax.dot_general(onehot,values,(((0,),(0,)),((),())),precision=highest,preferred_element_type=f32)[0:4,:]


class Links:
    def __init__(self, send, recv):
        self.send, self.recv, self.used = send, recv, 0

    def copy(self, src, dst, head, node):
        made=pltpu.make_async_remote_copy(src_ref=src,dst_ref=dst,send_sem=self.send.at[self.used],recv_sem=self.recv.at[self.used],
            device_id=(head,node),device_id_type=pl.DeviceIdType.MESH)
        self.used+=1
        return made

    def go(self, src, dst, head, node):
        made=self.copy(src,dst,head,node)
        made.start()
        return made


def meet(peers):
    barrier=pltpu.get_barrier_semaphore()
    for head,node in peers:
        pl.semaphore_signal(barrier,inc=1,device_id=(head,node),device_id_type=pl.DeviceIdType.MESH)
    pl.semaphore_wait(barrier,len(peers))


def wait_all(copies):
    for c in copies: c.wait()


def block_of(index, size):
    return pl.ds(pl.multiple_of(index*size,size),size)


def summed(*refs):
    total=refs[0].astype(f32)
    for r in refs[1:]: total=total+r.astype(f32)
    return total


NAMES=("ada","qkv","out","up","down")


def scratch(rows):
    part=rows//4
    return dict(
        e=((5,rows,rows),bf16),m=((rows,128),f32),l=((rows,128),f32),att=((rows,128),f32),fac=((rows,128),f32),
        queries=((rows,128),bf16),table=((5,rows,384),bf16),xn_one=((rows,512),bf16),
        qkv_full=((512,384),bf16),out_full=((4,128,512),bf16),up_full=((512,2048),bf16),down_full=((4,512,512),bf16),
        modp=((8,1024),f32),modbuf=((8,8,1024),f32),modulation=((8,1024),f32),
        mixed=((rows,128),bf16),heads=((part,512),bf16),do=((rows,128),bf16),do_rows=((part,512),bf16),
        act=((part,2048),bf16),pre=((part,2048),bf16),dy=((part,512),f32),out_rows=((part,512),bf16),
        up_grad=((4,2,64,2048),bf16),down_grad=((4,4,2,64,512),bf16),out_grad=((4,4,2,16,512),bf16),
        dq=((rows,128),f32),dkv=((256,rows),f32),near=((5,256,rows),bf16),
        got_pair=((256,rows),bf16),got_y=((256,rows),bf16),got_x=((256,rows),bf16),got_one=((256,rows),bf16),
        proj_grad=((rows,384),bf16),partial=((4,part,512),bf16),got_partial=((3,part,512),bf16),rows_grad=((part,512),bf16),normed=((rows,512),f32),
        up1=((4,64,2048),bf16),down1=((4,4,64,512),bf16),out1=((4,4,16,512),bf16),
        up2=((2,64,2048),bf16),down2=((4,2,64,512),bf16),out2=((4,2,16,512),bf16),
        up3=((64,2048),bf16),down3=((4,64,512),bf16),out3=((4,16,512),bf16),
        up_z=((3,64,512),bf16),down_z=((3,64,512),bf16),out_z=((3,16,512),bf16),
        qkv_grad=((8,64,384),bf16),qkv_got=((7,64,384),bf16),dm_own=((8,1024),f32),dm_z=((4,8,1024),f32),dm_n=((8,8,1024),f32),
    )


class Bag:
    pass


COPIES=14+9+8+4+9+9+1+3+6+55


def layer_kernel(scale, names, *refs):
    refs=list(refs)
    take=lambda n: [refs.pop(0) for _ in range(n)]
    node_input,cotangent,sigma,code,counts=take(5)
    w={n:refs.pop(0) for n in NAMES}
    node_output,row_all,qkv_sum,out_sum,up_sum,down_sum,mod_sum=take(7)
    k=Bag()
    for n in names: setattr(k,n,refs.pop(0))
    send,recv=take(2)
    head=lax.axis_index("head"); node=lax.axis_index("node")
    y_at=node//4; x_at=(node//2)%2; core=node%2
    rows=node_input.shape[0]
    part=rows//4
    links=Links(send,recv)
    go=links.go
    normed=k.normed
    quarter=[slice(i*part,(i+1)*part) for i in range(4)]
    limits=(counts[0],counts[0]+counts[1],counts[0]+counts[1]+counts[2])
    mine=block_of(head,part)
    head_cols=block_of(head,512)
    own_pos=node*rows+head*part+lax.broadcasted_iota(jnp.int32,(part,1),0)

    own=block_of(node,64); own_out=block_of(node,16)
    k.qkv_full[own,:]=w["qkv"][...].astype(bf16)
    sig=sigma[:,0:64]
    for i in range(1,8): sig=jnp.where(node==i,sigma[:,i*64:(i+1)*64],sig)
    made=jnp.dot(sig,w["ada"][...].astype(bf16),preferred_element_type=f32)
    k.modp[0:4,:]=made[:,:1024]
    k.modp[4:8,:]=made[:,1024:]
    k.up_full[own,head_cols]=w["up"][...].astype(bf16)
    k.down_full[head,own,:]=w["down"][...].astype(bf16)
    k.out_full[head,own_out,:]=w["out"][...].astype(bf16)
    meet([(head,node^i) for i in range(1,8)]+[(head^i,node) for i in range(1,4)])
    first=[]
    for i in range(1,8):
        first.append(go(k.modp,k.modbuf.at[node],head,node^i))
        first.append(go(k.qkv_full.at[own],k.qkv_full.at[own],head,node^i))
    along=[]
    for i in range(1,4):
        for ref in (k.up_full.at[own,head_cols],k.down_full.at[head,own],k.out_full.at[head,own_out]):
            along.append(go(ref,ref,head^i,node))
    k.modbuf[node,:,:]=k.modp[...]
    for b in range(5): k.table[b,:,256:384]=jnp.ones((rows,128),bf16)
    def norm(i,_):
        at=block_of(i,256)
        v=node_input[at,:].astype(f32)
        centred=v-jnp.mean(v,axis=1,keepdims=True)
        normed[at,:]=centred*lax.rsqrt(jnp.mean(centred*centred,axis=1,keepdims=True)+norm_eps)
        return 0
    lax.fori_loop(0,rows//256,norm,0)
    groups=code.shape[0]
    half=groups//2
    count_groups(k.e,code,rows,0,half,8)
    wait_all(first)
    mod=k.modbuf[0]
    for i in range(1,8): mod=mod+k.modbuf[i]
    k.modulation[...]=mod

    kv=slice(0,256)
    across=[]; paired=[]
    for at in quarter:
        pos=node*rows+at.start+lax.broadcasted_iota(jnp.int32,(part,1),0)
        xn=(normed[at,:]*(1.0+by_batch(pos,limits,k.modulation,0,slice(0,512)))+by_batch(pos,limits,k.modulation,0,slice(512,1024))).astype(bf16)
        k.xn_one[at,:]=xn
        proj=jnp.dot(xn,k.qkv_full[...],preferred_element_type=f32).astype(bf16)
        k.queries[at,:]=proj[:,:128]
        k.table[0,at,kv]=proj[:,128:]
        across.append(go(k.table.at[0,at,kv],k.table.at[2,at,kv],head,node^2))
        paired.append(go(k.table.at[0,at,kv],k.table.at[1,at,kv],head,node^1))
    count_groups(k.e,code,rows,half,groups,8)
    add_self(k.e,0,rows)

    onward=[]
    def pass_keys(i):
        at=quarter[i]
        across[i].wait_recv()
        onward.append(go(k.table.at[2,at,kv],k.table.at[3,at,kv],head,node^4))
    def attend(b,at):
        attend_rows(b,b==0,at,k.queries,k.table,k.e,k.m,k.l,k.att,k.fac,scale*math.log2(math.e))
    def column(which):
        at=block_of(node^which,64)
        return [k.up_full.at[at],k.down_full.at[:,at],k.out_full.at[:,block_of(node^which,16)]]
    pass_keys(0)
    for at in quarter: attend(0,at)
    pass_keys(1)
    wait_all(paired)
    for at in quarter: attend(1,at)
    pass_keys(2)
    pass_keys(3)
    wait_all(along)
    own_column=column(0)
    to_x=[go(r,r,head,node^2) for r in own_column]
    to_y=[go(r,r,head,node^4) for r in own_column]
    to_pair=[go(r,r,head,node^1) for r in own_column]
    for at in quarter: attend(2,at)
    wait_all(onward)
    fifth=go(k.table.at[jnp.where(x_at==core,2,3),:,kv],k.table.at[4,:,kv],head,node^1)
    for at in quarter: attend(3,at)
    fifth.wait()
    lanes=block_of(head,128)
    moved=[]
    for i in range(4):
        at=quarter[i]
        attend(4,at)
        inv=1.0/k.l[at,:]
        o=k.att[at,:]*inv
        k.att[at,:]=o
        k.fac[at,:]=jnp.exp2(k.fac[at,:]-k.m[at,:])*inv
        k.mixed[at,:]=o.astype(bf16)
    for i in range(1,4):
        moved.append(go(k.mixed.at[block_of(head^i,part)],k.heads.at[:,lanes],head^i,node))
    k.heads[:,lanes]=k.mixed[mine,:]
    for c in across: c.wait_send()
    wait_all(to_x+to_y)
    from_x=column(2); from_y=column(4)
    cross=[go(from_x[0],from_x[0],head,node^4)]+[go(r,r,head,node^2) for r in from_y[1:]]
    hand=[go(r,r,head,node^1) for r in from_x+from_y]
    wait_all(cross)
    last=[go(r,r,head,node^1) for r in column(6)]
    scale_two=1.0+by_batch(own_pos,limits,k.modulation,4,slice(0,512))
    shift_two=by_batch(own_pos,limits,k.modulation,4,slice(512,1024))
    g=cotangent[mine,:]
    wait_all(moved)
    wait_all(to_pair+hand+last)

    out_all=k.out_full[...].reshape(512,512)
    y=node_input[mine,:].astype(f32)+jnp.dot(k.heads[...],out_all,preferred_element_type=f32)
    n_two,inv_two=norm_parts(y)
    xn=(n_two*scale_two+shift_two).astype(bf16)
    mlp=jnp.zeros((part,512),f32); dxn=jnp.zeros((part,512),f32)
    for j in range(4):
        s=slice(j*512,(j+1)*512)
        h=jnp.dot(xn,k.up_full[:,s],preferred_element_type=f32)
        gate=1.0/(1.0+jnp.exp(-h))
        u=(h*gate).astype(bf16)
        k.act[:,s]=u
        mlp+=jnp.dot(u,k.down_full[j],preferred_element_type=f32)
        du=lax.dot_general(g,k.down_full[j],NT,preferred_element_type=f32)
        d=(du*gate*(1.0+h*(1.0-gate))).astype(bf16)
        k.pre[:,s]=d
        dxn+=lax.dot_general(d,k.up_full[:,s],NT,preferred_element_type=f32)
    dyv=g.astype(f32)+norm_back(dxn*scale_two,n_two,inv_two)
    k.dy[...]=dyv
    da=dyv.astype(bf16)
    k.do_rows[...]=lax.dot_general(da,out_all,NT,preferred_element_type=f32).astype(bf16)
    returned=[]
    for i in range(1,4):
        returned.append(go(k.do_rows.at[:,block_of(head^i,128)],k.do.at[mine],head^i,node))
    k.do[mine,:]=k.do_rows[:,lanes]
    k.out_rows[...]=(y+mlp).astype(bf16)
    xn_t=xn.T
    heads_t=k.heads[...].T
    k.out_grad[...]=jnp.dot(heads_t,da,preferred_element_type=f32).astype(bf16).reshape(4,4,2,16,512)
    for j in range(4):
        s=slice(j*512,(j+1)*512)
        k.up_grad[:,:,:,s]=jnp.dot(xn_t,k.pre[:,s],preferred_element_type=f32).astype(bf16).reshape(4,2,64,512)
        k.down_grad[j]=jnp.dot(k.act[:,s].T,g,preferred_element_type=f32).astype(bf16).reshape(4,2,64,512)
    stage1=[go(k.up_grad.at[:,1-core],k.up1,head,node^1),go(k.down_grad.at[:,:,1-core],k.down1,head,node^1),go(k.out_grad.at[:,:,1-core],k.out1,head,node^1)]
    k.dm_own[4:8,0:512]=batch_sums(own_pos,limits,dxn*n_two)
    k.dm_own[4:8,512:1024]=batch_sums(own_pos,limits,dxn)
    wait_all(returned)
    shown=[go(k.out_rows,node_output.at[mine],head^i,node) for i in range(1,4)]
    node_output[mine,:]=k.out_rows[...]

    q_t=k.queries[...].T
    dof=k.do[...].astype(f32)
    delta=jnp.sum(dof*k.att[...],axis=1,keepdims=True)
    def block(b):
        def write(r,s,v):
            if b==0: k.dkv[r,s]=v
            else: k.near[b,r,s]=v.astype(bf16)
        back_block(b,q_t,dof,k.fac,delta,k.table,k.e,k.dq,write,b==4,512,scale)
    near=k.near
    block(4)
    give=go(near.at[4],k.got_pair,head,node^1)
    block(3)
    give.wait()
    @pl.when(x_at!=core)
    def _(): near[3]=summed(near[3],k.got_pair[...]).astype(bf16)
    via_y=[go(near.at[3,:,s],k.got_y.at[:,s],head,node^4) for s in quarter]
    block(2)
    @pl.when(x_at==core)
    def _(): near[2]=summed(near[2],k.got_pair[...]).astype(bf16)
    via_x=[]
    def pass_on(i):
        s=quarter[i]
        via_y[i].wait()
        near[2,:,s]=summed(near[2,:,s],k.got_y[:,s]).astype(bf16)
        via_x.append(go(near.at[2,:,s],k.got_x.at[:,s],head,node^2))
    pass_on(0)
    block(1)
    one=go(near.at[1],k.got_one,head,node^1)
    pass_on(1)
    pass_on(2)
    block(0)
    pass_on(3)
    wait_all(stage1)
    for i in range(4):
        k.up1[i]=summed(k.up1[i],k.up_grad[i,core]).astype(bf16)
        k.down1[i]=summed(k.down1[i],k.down_grad[i,:,core]).astype(bf16)
        k.out1[i]=summed(k.out1[i],k.out_grad[i,:,core]).astype(bf16)
    stage2=[go(k.up1.at[i*2+1-x_at],k.up2.at[i],head,node^2) for i in range(2)]
    there=pl.ds((1-y_at)*2,2)
    stage2+=[go(k.down1.at[:,there],k.down2,head,node^4),go(k.out1.at[:,there],k.out2,head,node^4)]
    xn_t=k.xn_one[...].T
    one.wait()
    for i in range(4):
        s=quarter[i]
        via_x[i].wait()
        total=k.dkv[:,s]+k.got_one[:,s].astype(f32)+k.got_x[:,s].astype(f32)
        k.proj_grad[s,128:]=total.T.astype(bf16)
        k.proj_grad[s,:128]=(k.dq[s,:]*scale).astype(bf16)
        k.partial[i]=lax.dot_general(k.proj_grad[s,:],k.qkv_full[...],NT,preferred_element_type=f32).astype(bf16)
    reduce=[go(k.partial.at[head^i],k.got_partial.at[i-1],head^i,node) for i in range(1,4)]
    k.qkv_grad[...]=jnp.dot(xn_t,k.proj_grad[...],preferred_element_type=f32).astype(bf16).reshape(8,64,384)
    qkv_moves=[go(k.qkv_grad.at[node^i],k.qkv_got.at[i-1],head,node^i) for i in range(1,8)]
    wait_all(stage2)
    for i in range(2):
        k.up2[i]=summed(k.up2[i],k.up1[i*2+x_at]).astype(bf16)
    here=pl.ds(y_at*2,2)
    k.down2[...]=summed(k.down2[...],k.down1[:,here]).astype(bf16)
    k.out2[...]=summed(k.out2[...],k.out1[:,here]).astype(bf16)
    stage3=[go(k.up2.at[1-y_at],k.up3,head,node^4),go(k.down2.at[:,1-x_at],k.down3,head,node^2),go(k.out2.at[:,1-x_at],k.out3,head,node^2)]
    scale_one=1.0+by_batch(own_pos,limits,k.modulation,0,slice(0,512))
    n_one,inv_one=norm_parts(node_input[mine,:].astype(f32))
    wait_all(qkv_moves)
    qkv_sum[...]=summed(k.qkv_grad[node],*[k.qkv_got[i] for i in range(7)])
    wait_all(stage3)
    k.up3[...]=summed(k.up3[...],k.up2[y_at]).astype(bf16)
    k.down3[...]=summed(k.down3[...],k.down2[:,x_at]).astype(bf16)
    k.out3[...]=summed(k.out3[...],k.out2[:,x_at]).astype(bf16)
    wait_all(reduce)
    dxn=summed(k.partial[head],*[k.got_partial[i] for i in range(3)])
    k.rows_grad[...]=(k.dy[...]+norm_back(dxn*scale_one,n_one,inv_one)).astype(bf16)
    spread=[go(k.rows_grad,row_all.at[head],head^i,node) for i in range(1,4)]
    row_all[head,:,:]=k.rows_grad[...]
    k.dm_own[0:4,0:512]=batch_sums(own_pos,limits,dxn*n_one)
    k.dm_own[0:4,512:1024]=batch_sums(own_pos,limits,dxn)
    dm_moves=[go(k.dm_own,k.dm_z.at[head],head^i,node) for i in range(1,4)]
    k.dm_z[head,:,:]=k.dm_own[...]
    stage4=[]
    for i in range(1,4):
        stage4+=[go(k.up3.at[:,block_of(head^i,512)],k.up_z.at[i-1],head^i,node),go(k.down3.at[head^i],k.down_z.at[i-1],head^i,node),go(k.out3.at[head^i],k.out_z.at[i-1],head^i,node)]
    wait_all(dm_moves)
    k.modp[...]=k.dm_z[0]+k.dm_z[1]+k.dm_z[2]+k.dm_z[3]
    dm_last=[go(k.modp,k.dm_n.at[node],head,node^i) for i in range(1,8)]
    k.dm_n[node,:,:]=k.modp[...]
    wait_all(dm_last)
    total=k.dm_n[0]
    for i in range(1,8): total=total+k.dm_n[i]
    mod_sum[...]=total
    wait_all(stage4)
    up_sum[...]=summed(k.up3[:,head_cols],*[k.up_z[i] for i in range(3)])
    down_sum[...]=summed(k.down3[head],*[k.down_z[i] for i in range(3)])
    out_sum[...]=summed(k.out3[head],*[k.out_z[i] for i in range(3)])
    wait_all(spread)
    wait_all(shown)


def finish_kernel(sigma, step_count, *refs):
    sources=refs[:22]; results=refs[22:39]; held=refs[39:62]; load,store=refs[62:]
    loads=[pltpu.make_async_copy(sources[i],held[i],load.at[i]) for i in range(22)]
    for i in (0,1)+tuple(range(7,22))+tuple(range(2,7)): loads[i].start()
    node=lax.axis_index("node")
    stores=[]
    def keep(ref, result):
        stores.append(pltpu.make_async_copy(ref,results[result],store.at[result])); stores[-1].start()
    loads[0].wait()
    keep(held[0],0)
    loads[1].wait()
    wide=held[22]
    rows=wide.shape[0]
    for i in range(4): wide[i*rows//4:(i+1)*rows//4,:]=held[1][i].astype(f32)
    keep(wide,1)
    count=jnp.full((8,128),step_count[0],jnp.int32).astype(f32)
    correct=(1.0-jnp.exp2(-count))[0:1,0:1]
    sig=sigma[:,0:64]
    for i in range(1,8): sig=jnp.where(node==i,sigma[:,i*64:(i+1)*64],sig)
    rates=((4*COND)**-0.5,(WIDTH//2)**-0.5,(WIDTH//4)**-0.5,WIDTH**-0.5,HIDDEN_SIZE**-0.5)
    for w in (0,3,4,1,2):
        at=7+3*w
        for i in range(3): loads[at+i].wait()
        if w==0:
            loads[6].wait()
            total=held[6]
            batch_grad=jnp.concatenate([total[0:4,:],total[4:8,:]],axis=1)
            grad=lax.dot_general(sig.astype(f32),batch_grad,(((0,),(0,)),((),())),precision=highest,preferred_element_type=f32)
        else:
            loads[1+w].wait()
            grad=held[1+w][...]
        master,first,second=held[at:at+3]
        first_new=beta_rate*first[...]+(1.0-beta_rate)*grad
        second_new=beta_rate*second[...]+(1.0-beta_rate)*grad*grad
        step=first_new/correct/(jnp.sqrt(second_new/correct)+adam_eps)
        old=master[...]
        master[...]=old-rates[w]*(step+weight_decay*old)
        first[...]=first_new
        second[...]=second_new
        for i in range(3): keep(held[at+i],2+3*w+i)
    for c in stores: c.wait()


def slots(neighbours, valid, node, rows):
    which=(neighbours//rows)^node
    slot=jnp.where(which==6,3,jnp.where((which==3)|(which==7),4,which))
    local=neighbours%rows
    spot=lax.broadcasted_iota(jnp.int32,neighbours.shape,0)%16
    hi=(slot*(rows//SPAN)+local//SPAN)*16+spot
    return jnp.where(valid>0,hi*256+local%SPAN,-1).reshape(-1,256)


def per_device_near(
    node_input, cotangent, sigma_embed, neighbours, neighbour_valid, batch_counts, step_count,
    ada_master, ada_first, ada_second, qkv_master, qkv_first, qkv_second, out_master, out_first, out_second,
    up_master, up_first, up_second, down_master, down_first, down_second,
):
    rows=node_input.shape[0]
    code=slots(neighbours,neighbour_valid,lax.axis_index("node"),rows)
    masters=(ada_master,qkv_master,out_master,up_master,down_master)
    firsts=(ada_first,qkv_first,out_first,up_first,down_first)
    seconds=(ada_second,qkv_second,out_second,up_second,down_second)
    V=pltpu.VMEM
    full=pl.BlockSpec(memory_space=V); few=pl.BlockSpec(memory_space=pltpu.SMEM); hbm=pl.BlockSpec(memory_space=pl.ANY)
    S=jax.ShapeDtypeStruct
    held=scratch(rows)
    sums=pl.pallas_call(functools.partial(layer_kernel,128**-0.5,tuple(held)),
        out_shape=(S((rows,512),bf16),S((4,rows//4,512),bf16))+tuple(S(a.shape,f32) for a in masters[1:])+(S((8,1024),f32),),
        in_specs=[full]*4+[few]+[full]*5,
        out_specs=(full,)*7,
        scratch_shapes=[V(*v) for v in held.values()]+[pltpu.SemaphoreType.DMA((COPIES,))]*2,
        compiler_params=pltpu.CompilerParams(vmem_limit_bytes=67043328,collective_id=1,has_side_effects=True),
        name="layer")(node_input,cotangent,sigma_embed,code,batch_counts,*masters)
    news=tuple(S(a.shape,f32) for a in masters for _ in range(3))
    inner=[V(a.shape,a.dtype) for a in sums]+[V(a.shape,f32) for a in masters for _ in range(3)]+[V((rows,512),f32)]
    return pl.pallas_call(finish_kernel,
        out_shape=(S((rows,512),bf16),S((rows,512),f32))+news,
        in_specs=[full,few]+[hbm]*(7+15),
        out_specs=(hbm,)*17,
        scratch_shapes=inner+[pltpu.SemaphoreType.DMA((22,)),pltpu.SemaphoreType.DMA((17,))],
        compiler_params=pltpu.CompilerParams(vmem_limit_bytes=48<<20),
        name="finish")(sigma_embed,step_count,*sums,*[a for three in zip(masters,firsts,seconds) for a in three])


def wide_count_groups(cnt, hik, lok, rows):
    steps=hik.shape[0]
    parts=rows//SPAN
    total=5*parts*16
    rowid=lax.broadcasted_iota(jnp.int32,(total,1),0)
    rowkey=lax.div(rowid,16)*16+lax.rem(rowid,16)
    spot=lax.broadcasted_iota(jnp.int32,(SPAN,1),0)
    def body(g,_):
        keys=hik[pl.ds(g,1),:]
        low=lok[pl.ds(g,1),:]
        left=jnp.where(rowkey==keys,1.0,0.0).astype(bf16)
        right=jnp.where(spot==low,1.0,0.0).astype(bf16)
        made=lax.dot_general(left,right,NT,preferred_element_type=f32).astype(bf16)
        at=pl.multiple_of(g*16,16)
        for b in range(5):
            for p in range(parts):
                r=(b*parts+p)*16
                cnt[b,pl.ds(at,16),p*SPAN:(p+1)*SPAN]=made[r:r+16,:]
        return 0
    lax.fori_loop(0,steps,body,0)

def wide_add_self(cnt, block, rows):
    eye=(lax.broadcasted_iota(jnp.int32,(SPAN,SPAN),0)==lax.broadcasted_iota(jnp.int32,(SPAN,SPAN),1))
    one=jnp.where(eye,1.0,0.0).astype(bf16)
    for p in range(rows//SPAN):
        s=slice(p*SPAN,(p+1)*SPAN)
        cnt[block,s,s]=cnt[block,s,s]+one

def wide_attend_block(b, first, q, keys, vals, cnt, e, m, l, acc, fac, chunk, scale):
    rows=q.shape[0]
    lane=lax.broadcasted_iota(jnp.int32,(chunk,128),1)
    def body(i,_):
        at=pl.ds(pl.multiple_of(i*chunk,chunk),chunk)
        s=lax.dot_general(q[at,:],keys,NT,preferred_element_type=f32)*scale
        c=cnt[b,at,:].astype(f32)
        s=jnp.where(c>0,s,-1e30)
        top=jnp.max(s,axis=1,keepdims=True)
        if not first:
            old=m[at,0:1]
            top=jnp.maximum(top,old)
        w=(jnp.exp2(s-top)*c)
        total=jnp.sum(w,axis=1,keepdims=True)
        w=w.astype(bf16)
        e[b,at,:]=w
        out=jnp.dot(w,vals,preferred_element_type=f32)
        if first:
            acc[at,:]=out; l[at,:]=jnp.broadcast_to(total,(chunk,128))
            fac[at,:]=jnp.where(lane==b,top,0.0)
        else:
            shrink=jnp.exp2(old-top)
            acc[at,:]=acc[at,:]*shrink+out
            l[at,:]=l[at,:]*shrink+total
            fac[at,:]=jnp.where(lane==b,top,fac[at,:])
        m[at,:]=jnp.broadcast_to(top,(chunk,128))
        return 0
    lax.fori_loop(0,rows//chunk,body,0)

def wide_fwd_kernel(order, self_block, scale, q, kv, hik, lok, att, e, fac, cnt, m, l):
    rows=q.shape[0]
    wide_count_groups(cnt,hik,lok,rows)
    wide_add_self(cnt,self_block,rows)
    for t,b in enumerate(order):
        wide_attend_block(b,t==0,q,kv[b,:,:128],kv[b,:,128:],cnt,e,m,l,att,fac,256,scale)
    inv=1.0/l[...]
    att[...]=att[...]*inv
    fac[...]=jnp.exp2(fac[...]-m[...])*inv

def wide_attention_fwd(q,kv,hik,lok,scale):
    rows=q.shape[0]
    V=pltpu.VMEM
    full=pl.BlockSpec(memory_space=V)
    return pl.pallas_call(functools.partial(wide_fwd_kernel,(2,1,3,0,4),2,scale*math.log2(math.e)),
        out_shape=(jax.ShapeDtypeStruct((rows,128),f32),jax.ShapeDtypeStruct((5,rows,rows),bf16),jax.ShapeDtypeStruct((rows,128),f32)),
        in_specs=[full]*4,out_specs=(full,)*3,
        scratch_shapes=[V((5,rows,rows),bf16),V((rows,128),f32),V((rows,128),f32)],
        compiler_params=pltpu.CompilerParams(vmem_limit_bytes=60<<20),name="attend_fwd")(q,kv,hik,lok)

def wide_back_block(b, q_t, do, fac, delta, kv, e, dq, dkv, first, chunk, keyscale):
    rows=do.shape[0]
    f=fac[:,b:b+1]
    dob=(do*f)
    dobh=dob.astype(bf16)
    d=-(delta*f)
    h=d.astype(bf16); r=d-h.astype(f32); h2=r.astype(bf16); h3=(r-h2.astype(f32)).astype(bf16)
    lane=lax.broadcasted_iota(jnp.int32,(rows,128),1)
    zero=jnp.zeros((rows,128),bf16)
    dcol=jnp.where(lane==0,h.astype(f32),jnp.where(lane==1,h2.astype(f32),jnp.where(lane==2,h3.astype(f32),0.0))).astype(bf16)
    left=jnp.concatenate([dobh,dcol],axis=1)
    dob_t=dobh.T
    ones=jnp.ones((chunk,128),bf16)
    for i in range(kv.shape[1]//chunk):
        s=slice(i*chunk,(i+1)*chunk)
        right=jnp.concatenate([kv[b,s,128:],ones],axis=1)
        dp=lax.dot_general(left,right,NT,preferred_element_type=f32)
        w=e[b,:,s]
        ds=(dp*w.astype(f32)).astype(bf16)
        dkv[b,:128,s]=jnp.dot(q_t,ds,preferred_element_type=f32)*keyscale
        dkv[b,128:,s]=jnp.dot(dob_t,w,preferred_element_type=f32)
        out=jnp.dot(ds,kv[b,s,:128],preferred_element_type=f32)
        if first and i==0: dq[...]=out
        else: dq[...]+=out

def wide_bwd_kernel(scale, q, do, att, fac, kv, e, dq, dkv, ):
    q_t=q[...].T
    dof=do[...].astype(f32)
    delta=jnp.sum(dof*att[...],axis=1,keepdims=True)
    for t,b in enumerate((0,4,1,3,2)):
        wide_back_block(b,q_t,dof,fac,delta,kv,e,dq,dkv,t==0,512,scale)
    dq[...]=dq[...]*scale

def wide_attention_bwd(q,do,att,fac,kv,e,scale):
    rows=q.shape[0]
    V=pltpu.VMEM
    full=pl.BlockSpec(memory_space=V)
    return pl.pallas_call(functools.partial(wide_bwd_kernel,scale),
        out_shape=(jax.ShapeDtypeStruct((rows,128),f32),jax.ShapeDtypeStruct((5,256,rows),f32)),
        in_specs=[full]*6,out_specs=(full,)*2,
        compiler_params=pltpu.CompilerParams(vmem_limit_bytes=60<<20),name="attend_bwd")(q,do,att,fac,kv,e)

def wide_tables(slot_index, valid, rows):
    parts=rows//SPAN
    flat=slot_index.reshape(-1,256)
    ok=(valid>0).reshape(-1,256)
    node=lax.broadcasted_iota(jnp.int32,flat.shape,1)//16
    hi=jnp.where(ok,(flat//SPAN)*16+node,-1)
    lo=flat%SPAN
    return hi,lo


def per_device(
    node_input,
    cotangent,
    sigma_embed,
    neighbours,
    neighbour_valid,
    batch_counts,
    step_count,
    ada_master,
    ada_first,
    ada_second,
    qkv_master,
    qkv_first,
    qkv_second,
    out_master,
    out_first,
    out_second,
    up_master,
    up_first,
    up_second,
    down_master,
    down_first,
    down_second,
):
    f32 = jnp.float32
    bf16 = jnp.bfloat16
    node_rows = node_input.shape[0]
    model_width = node_input.shape[1]
    head_dim = qkv_master.shape[1] // 3
    score_scale = head_dim ** (-0.5)
    node_index = lax.axis_index("node")
    total_nodes = node_rows * lax.axis_size("node")
    qkv_full, out_full, up_full, down_full = (
        lax.all_gather(qkv_master.astype(bf16), "node", axis=0, tiled=True),
        lax.all_gather(out_master.astype(bf16), "node", axis=0, tiled=True),
        lax.all_gather(up_master.astype(bf16), "node", axis=0, tiled=True),
        lax.all_gather(down_master.astype(bf16), "node", axis=0, tiled=True),
    )
    cond_rows = ada_master.shape[0]
    sigma_part = lax.dynamic_slice_in_dim(sigma_embed, node_index * cond_rows, cond_rows, 1)
    limits = jnp.cumsum(batch_counts)[:-1]
    positions = node_index * node_rows + jnp.arange(node_rows, dtype=jnp.int32)
    member = jnp.sum((positions[:, None] >= limits[None, :]).astype(jnp.int32), axis=1)
    onehot = (
        member[:, None] == jnp.arange(batch_counts.shape[0], dtype=jnp.int32)[None, :]
    ).astype(f32)
    modulation = lax.psum(
        jnp.dot(sigma_part, ada_master.astype(bf16), preferred_element_type=f32), "node"
    )
    per_node = jnp.dot(onehot, modulation, precision=highest)
    scale_one = per_node[:, :model_width]
    shift_one = per_node[:, model_width : 2 * model_width]
    scale_two = per_node[:, 2 * model_width : 3 * model_width]
    shift_two = per_node[:, 3 * model_width :]
    normed_one, inverse_one = norm_parts(node_input.astype(f32))
    xn_one = (normed_one * (1.0 + scale_one) + shift_one).astype(bf16)
    projected = jnp.dot(xn_one, qkv_full, preferred_element_type=f32).astype(bf16)
    queries = projected[:, :head_dim]
    keys_values = projected[:, head_dim:]
    offsets = (-2, -1, 1, 2)
    fetched = {0: keys_values}
    for offset in offsets:
        fetched[offset] = passed_along(keys_values, "node", -offset)
    table = jnp.stack([fetched[offset] for offset in (-2, -1, 0, 1, 2)], axis=0)
    slot_index = jnp.mod(neighbours - (node_index - 2) * node_rows, total_nodes)
    high_keys, low_keys = wide_tables(slot_index, neighbour_valid, node_rows)
    mixed, weights, factors = wide_attention_fwd(queries, table, high_keys, low_keys, score_scale)
    heads_out = mixed.astype(bf16)
    branch = lax.psum(
        jnp.dot(heads_out, out_full, preferred_element_type=f32).astype(jnp.bfloat16), "head"
    ).astype(jnp.float32)
    middle = node_input.astype(f32) + branch
    normed_two, inverse_two = norm_parts(middle)
    xn_two = (normed_two * (1.0 + scale_two) + shift_two).astype(bf16)
    hidden_pre = jnp.dot(xn_two, up_full, preferred_element_type=f32)
    gate_sig = jax.nn.sigmoid(hidden_pre)
    activated = (hidden_pre * gate_sig).astype(bf16)
    mlp_sum = lax.psum(
        jnp.dot(activated, down_full, preferred_element_type=f32).astype(jnp.bfloat16), "head"
    ).astype(jnp.float32)
    node_output = (middle + mlp_sum).astype(bf16)
    down_grad = jnp.einsum("nf,nd->fd", activated, cotangent, preferred_element_type=f32)
    act_grad = jnp.einsum("nd,fd->nf", cotangent, down_full, preferred_element_type=f32)
    pre_grad = (act_grad * gate_sig * (1.0 + hidden_pre * (1.0 - gate_sig))).astype(bf16)
    up_grad = jnp.einsum("nw,nf->wf", xn_two, pre_grad, preferred_element_type=f32)
    normed_two_grad = lax.psum(
        jnp.einsum("nf,wf->nw", pre_grad, up_full, preferred_element_type=f32).astype(jnp.bfloat16),
        "head",
    ).astype(jnp.float32)
    middle_grad = cotangent.astype(f32) + norm_back(
        normed_two_grad * (1.0 + scale_two), normed_two, inverse_two
    )
    branch_grad = middle_grad.astype(bf16)
    out_grad = jnp.einsum("nh,nd->hd", heads_out, branch_grad, preferred_element_type=f32)
    mixed_grad = jnp.einsum("nd,hd->nh", branch_grad, out_full, preferred_element_type=f32).astype(
        bf16
    )
    query_grad, pair_sums = wide_attention_bwd(
        queries, mixed_grad, mixed, factors, table, weights, score_scale
    )
    remote_terms = pair_sums[2]
    for offset in offsets:
        remote_terms = remote_terms + passed_along(
            pair_sums[offset + 2].astype(bf16), "node", offset
        ).astype(f32)
    key_value_grad = remote_terms.T
    projected_grad = jnp.concatenate([query_grad, key_value_grad], axis=1).astype(bf16)
    qkv_grad = jnp.einsum("nw,nc->wc", xn_one, projected_grad, preferred_element_type=f32)
    normed_one_grad = lax.psum(
        jnp.einsum("nc,wc->nw", projected_grad, qkv_full, preferred_element_type=f32).astype(
            jnp.bfloat16
        ),
        "head",
    ).astype(jnp.float32)
    input_grad = middle_grad + norm_back(
        normed_one_grad * (1.0 + scale_one), normed_one, inverse_one
    )
    rows_grad = jnp.concatenate(
        [
            normed_one_grad * normed_one,
            normed_one_grad,
            normed_two_grad * normed_two,
            normed_two_grad,
        ],
        axis=1,
    )
    batch_grad = jnp.dot(onehot.T, rows_grad, precision=highest)
    batch_grad = lax.psum(batch_grad, "node")
    ada_sum = jnp.dot(sigma_part.astype(f32).T, batch_grad, precision=highest)
    qkv_sum, out_sum, up_sum, down_sum = (
        lax.psum_scatter(qkv_grad, "node", scatter_dimension=0, tiled=True),
        lax.psum_scatter(out_grad, "node", scatter_dimension=0, tiled=True),
        lax.psum_scatter(up_grad, "node", scatter_dimension=0, tiled=True),
        lax.psum_scatter(down_grad, "node", scatter_dimension=0, tiled=True),
    )
    count_value = step_count[0].astype(f32)
    ada_res = adamw_update(
        ada_master, ada_first, ada_second, ada_sum, (4 * COND) ** (-0.5), count_value
    )
    qkv_res = adamw_update(
        qkv_master, qkv_first, qkv_second, qkv_sum, (WIDTH // 2) ** (-0.5), count_value
    )
    out_res = adamw_update(
        out_master, out_first, out_second, out_sum, (WIDTH // 4) ** (-0.5), count_value
    )
    up_res = adamw_update(up_master, up_first, up_second, up_sum, WIDTH ** (-0.5), count_value)
    down_res = adamw_update(
        down_master, down_first, down_second, down_sum, HIDDEN_SIZE ** (-0.5), count_value
    )
    return (
        node_output,
        input_grad,
        ada_res[0],
        ada_res[1],
        ada_res[2],
        qkv_res[0],
        qkv_res[1],
        qkv_res[2],
        out_res[0],
        out_res[1],
        out_res[2],
        up_res[0],
        up_res[1],
        up_res[2],
        down_res[0],
        down_res[1],
        down_res[2],
    )


def solution(mesh):
    chosen = per_device_near if mesh.shape["node"] == 8 and mesh.shape["head"] == 4 else per_device
    placed = (
        P("node", None),
        P("node", None),
        P(),
        P("node", None),
        P("node", None),
        P(),
        P(),
        P("node", None),
        P("node", None),
        P("node", None),
        P("node", "head"),
        P("node", "head"),
        P("node", "head"),
        P(("head", "node"), None),
        P(("head", "node"), None),
        P(("head", "node"), None),
        P("node", "head"),
        P("node", "head"),
        P("node", "head"),
        P(("head", "node"), None),
        P(("head", "node"), None),
        P(("head", "node"), None),
    )
    return jax.shard_map(
        chosen,
        mesh=mesh,
        in_specs=placed,
        out_specs=(
            P("node", None),
            P("node", None),
            P("node", None),
            P("node", None),
            P("node", None),
            P("node", "head"),
            P("node", "head"),
            P("node", "head"),
            P(("head", "node"), None),
            P(("head", "node"), None),
            P(("head", "node"), None),
            P("node", "head"),
            P("node", "head"),
            P("node", "head"),
            P(("head", "node"), None),
            P(("head", "node"), None),
            P(("head", "node"), None),
        ),
        check_vma=False,
    )
```

```python
import functools
import math

import jax
import jax.numpy as jnp
from jax import lax
from jax.experimental import pallas as pl
from jax.experimental.pallas import tpu as pltpu
from jax.sharding import PartitionSpec as P


WIDTH = 512
HIDDEN_SIZE = 2048
COND = 512


norm_eps = 1e-06
beta_rate = 0.5
adam_eps = 1e-08
weight_decay = 0.1
highest = lax.Precision.HIGHEST


def passed_along(block, axis, distance):
    devices = range(lax.axis_size(axis))
    route = [((i - distance) % len(devices), i) for i in devices]
    return lax.ppermute(block, axis, route)


def norm_parts(values):
    centred = values - jnp.mean(values, axis=1, keepdims=True)
    inverse = lax.rsqrt(jnp.mean(centred * centred, axis=1, keepdims=True) + norm_eps)
    return (centred * inverse, inverse)


def norm_back(grad_normed, normed, inverse):
    first_mean = jnp.mean(grad_normed, axis=1, keepdims=True)
    second_mean = jnp.mean(grad_normed * normed, axis=1, keepdims=True)
    return inverse * (grad_normed - first_mean - normed * second_mean)


def adamw_update(master, first, second, grad, rate, count_value):
    first_new = beta_rate * first + (1.0 - beta_rate) * grad
    second_new = beta_rate * second + (1.0 - beta_rate) * grad * grad
    correct = 1.0 - jnp.power(jnp.float32(beta_rate), count_value)
    normed_step = first_new / correct / (jnp.sqrt(second_new / correct) + adam_eps)
    master_new = master - rate * (normed_step + weight_decay * master)
    return (master_new, first_new, second_new)


f32=jnp.float32; bf16=jnp.bfloat16
NT=(((1,),(1,)),((),()))
SPAN=256

def count_groups(cnt, code, rows, start, stop, step):
    parts=rows//SPAN
    total=5*parts*16
    short=jnp.int16
    rowid=lax.broadcasted_iota(jnp.int32,(total,SPAN),0).astype(short)
    spot=lax.broadcasted_iota(jnp.int32,(SPAN,SPAN),0).astype(short)
    one=bf16(1); zero=bf16(0)
    def group(g):
        both=code[pl.ds(g,1),:]
        keys=lax.shift_right_arithmetic(both,8).astype(short)
        low=lax.bitwise_and(both,255).astype(short)
        left=jnp.where(rowid==jnp.broadcast_to(keys,(total,SPAN)),one,zero)
        right=jnp.where(spot==jnp.broadcast_to(low,(SPAN,SPAN)),one,zero)
        made=lax.dot_general(left,right,NT,preferred_element_type=f32).astype(bf16)
        at=pl.multiple_of(g*16,16)
        for b in range(5):
            for p in range(parts):
                r=(b*parts+p)*16
                cnt[b,pl.ds(at,16),p*SPAN:(p+1)*SPAN]=made[r:r+16,:]
    def body(g,_):
        for u in range(step): group(g*step+u)
        return 0
    lax.fori_loop(start//step,stop//step,body,0)

def add_self(cnt, block, rows):
    eye=(lax.broadcasted_iota(jnp.int32,(SPAN,SPAN),0)==lax.broadcasted_iota(jnp.int32,(SPAN,SPAN),1))
    one=jnp.where(eye,1.0,0.0).astype(bf16)
    for p in range(rows//SPAN):
        s=slice(p*SPAN,(p+1)*SPAN)
        cnt[block,s,s]=cnt[block,s,s]+one

def attend_rows(b, first, at, q, table, e, m, l, acc, fac, scale):
    size=at.stop-at.start
    lane=lax.broadcasted_iota(jnp.int32,(size,128),1)
    s=lax.dot_general(q[at,:],table[b,:,0:128],NT,preferred_element_type=f32)*scale
    c=e[b,at,:].astype(f32)
    s=jnp.where(c>0,s,-1e30)
    top=jnp.max(s,axis=1,keepdims=True)
    if not first:
        old=m[at,0:1]
        top=jnp.maximum(top,old)
    w=(jnp.exp2(s-top)*c).astype(bf16)
    e[b,at,:]=w
    out=jnp.dot(w,table[b,:,128:384],preferred_element_type=f32)
    if first:
        acc[at,:]=out[:,:128]; l[at,:]=out[:,128:]
        fac[at,:]=jnp.where(lane==b,top,0.0)
    else:
        shrink=jnp.exp2(old-top)
        acc[at,:]=acc[at,:]*shrink+out[:,:128]
        l[at,:]=l[at,:]*shrink+out[:,128:]
        fac[at,:]=jnp.where(lane==b,top,fac[at,:])
    m[at,:]=jnp.broadcast_to(top,(size,128))

def back_block(b, q_t, dof, fac, delta, table, e, dq, write, first, chunk, keyscale):
    rows=dof.shape[0]
    f=fac[:,b:b+1]
    dobh=(dof*f).astype(bf16)
    d=-(delta*f)
    h=d.astype(bf16); r=d-h.astype(f32); h2=r.astype(bf16); h3=(r-h2.astype(f32)).astype(bf16)
    lane=lax.broadcasted_iota(jnp.int32,(rows,128),1)
    dcol=jnp.where(lane==0,h.astype(f32),jnp.where(lane==1,h2.astype(f32),jnp.where(lane==2,h3.astype(f32),0.0))).astype(bf16)
    left=jnp.concatenate([dobh,dcol],axis=1)
    dob_t=dobh.T
    for i in range(rows//chunk):
        s=slice(i*chunk,(i+1)*chunk)
        dp=lax.dot_general(left,table[b,s,128:384],NT,preferred_element_type=f32)
        w=e[b,:,s]
        ds=(dp*w.astype(f32)).astype(bf16)
        write(slice(0,128),s,jnp.dot(q_t,ds,preferred_element_type=f32)*keyscale)
        write(slice(128,256),s,jnp.dot(dob_t,w,preferred_element_type=f32))
        out=jnp.dot(ds,table[b,s,0:128],preferred_element_type=f32)
        if first and i==0: dq[...]=out
        else: dq[...]+=out


def by_batch(pos, limits, table, row, lanes):
    pick=[table[row+b:row+b+1,lanes] for b in range(4)]
    out=jnp.where(pos>=limits[0],pick[1],pick[0])
    out=jnp.where(pos>=limits[1],pick[2],out)
    return jnp.where(pos>=limits[2],pick[3],out)


def batch_sums(pos, limits, values):
    lane=lax.broadcasted_iota(jnp.int32,(pos.shape[0],8),1)
    member=(pos>=limits[0]).astype(jnp.int32)+(pos>=limits[1]).astype(jnp.int32)+(pos>=limits[2]).astype(jnp.int32)
    onehot=jnp.where(lane==member,1.0,0.0).astype(f32)
    return lax.dot_general(onehot,values,(((0,),(0,)),((),())),precision=highest,preferred_element_type=f32)[0:4,:]


class Links:
    def __init__(self, send, recv):
        self.send, self.recv, self.used = send, recv, 0

    def copy(self, src, dst, head, node):
        made=pltpu.make_async_remote_copy(src_ref=src,dst_ref=dst,send_sem=self.send.at[self.used],recv_sem=self.recv.at[self.used],
            device_id=(head,node),device_id_type=pl.DeviceIdType.MESH)
        self.used+=1
        return made

    def go(self, src, dst, head, node):
        made=self.copy(src,dst,head,node)
        made.start()
        return made


def meet(peers):
    barrier=pltpu.get_barrier_semaphore()
    for head,node in peers:
        pl.semaphore_signal(barrier,inc=1,device_id=(head,node),device_id_type=pl.DeviceIdType.MESH)
    pl.semaphore_wait(barrier,len(peers))


def wait_all(copies):
    for c in copies: c.wait()


def block_of(index, size):
    return pl.ds(pl.multiple_of(index*size,size),size)


def summed(*refs):
    total=refs[0].astype(f32)
    for r in refs[1:]: total=total+r.astype(f32)
    return total


NAMES=("ada","qkv","out","up","down")


def scratch(rows):
    part=rows//4
    return dict(
        e=((5,rows,rows),bf16),m=((rows,128),f32),l=((rows,128),f32),att=((rows,128),f32),fac=((rows,128),f32),
        queries=((rows,128),bf16),table=((5,rows,384),bf16),xn_one=((rows,512),bf16),
        qkv_full=((512,384),bf16),out_full=((4,128,512),bf16),up_full=((512,2048),bf16),down_full=((4,512,512),bf16),
        modp=((8,1024),f32),modbuf=((8,8,1024),f32),modulation=((8,1024),f32),
        mixed=((rows,128),bf16),heads=((part,512),bf16),do=((rows,128),bf16),do_rows=((part,512),bf16),
        act=((part,2048),bf16),pre=((part,2048),bf16),dy=((part,512),f32),out_rows=((part,512),bf16),
        up_grad=((4,2,64,2048),bf16),down_grad=((4,4,2,64,512),bf16),out_grad=((4,4,2,16,512),bf16),
        dq=((rows,128),f32),dkv=((256,rows),f32),near=((5,256,rows),bf16),
        got_pair=((256,rows),bf16),got_y=((256,rows),bf16),got_x=((256,rows),bf16),got_one=((256,rows),bf16),
        proj_grad=((rows,384),bf16),partial=((4,part,512),bf16),got_partial=((3,part,512),bf16),rows_grad=((part,512),bf16),normed=((rows,512),f32),
        up1=((4,64,2048),bf16),down1=((4,4,64,512),bf16),out1=((4,4,16,512),bf16),
        up2=((2,64,2048),bf16),down2=((4,2,64,512),bf16),out2=((4,2,16,512),bf16),
        up3=((64,2048),bf16),down3=((4,64,512),bf16),out3=((4,16,512),bf16),
        up_z=((3,64,512),bf16),down_z=((3,64,512),bf16),out_z=((3,16,512),bf16),
        qkv_grad=((8,64,384),bf16),qkv_got=((7,64,384),bf16),dm_own=((8,1024),f32),dm_z=((4,8,1024),f32),dm_n=((8,8,1024),f32),
    )


class Bag:
    pass


COPIES=14+9+8+4+9+9+1+3+6+55


def layer_kernel(scale, names, *refs):
    refs=list(refs)
    take=lambda n: [refs.pop(0) for _ in range(n)]
    node_input,cotangent,sigma,code,counts=take(5)
    w={n:refs.pop(0) for n in NAMES}
    node_output,row_all,qkv_sum,out_sum,up_sum,down_sum,mod_sum=take(7)
    k=Bag()
    for n in names: setattr(k,n,refs.pop(0))
    send,recv=take(2)
    head=lax.axis_index("head"); node=lax.axis_index("node")
    y_at=node//4; x_at=(node//2)%2; core=node%2
    rows=node_input.shape[0]
    part=rows//4
    links=Links(send,recv)
    go=links.go
    normed=k.normed
    quarter=[slice(i*part,(i+1)*part) for i in range(4)]
    limits=(counts[0],counts[0]+counts[1],counts[0]+counts[1]+counts[2])
    mine=block_of(head,part)
    head_cols=block_of(head,512)
    own_pos=node*rows+head*part+lax.broadcasted_iota(jnp.int32,(part,1),0)

    own=block_of(node,64); own_out=block_of(node,16)
    k.qkv_full[own,:]=w["qkv"][...].astype(bf16)
    sig=sigma[:,0:64]
    for i in range(1,8): sig=jnp.where(node==i,sigma[:,i*64:(i+1)*64],sig)
    made=jnp.dot(sig,w["ada"][...].astype(bf16),preferred_element_type=f32)
    k.modp[0:4,:]=made[:,:1024]
    k.modp[4:8,:]=made[:,1024:]
    k.up_full[own,head_cols]=w["up"][...].astype(bf16)
    k.down_full[head,own,:]=w["down"][...].astype(bf16)
    k.out_full[head,own_out,:]=w["out"][...].astype(bf16)
    meet([(head,node^i) for i in range(1,8)]+[(head^i,node) for i in range(1,4)])
    first=[]
    for i in range(1,8):
        first.append(go(k.modp,k.modbuf.at[node],head,node^i))
        first.append(go(k.qkv_full.at[own],k.qkv_full.at[own],head,node^i))
    along=[]
    for i in range(1,4):
        for ref in (k.up_full.at[own,head_cols],k.down_full.at[head,own],k.out_full.at[head,own_out]):
            along.append(go(ref,ref,head^i,node))
    k.modbuf[node,:,:]=k.modp[...]
    for b in range(5): k.table[b,:,256:384]=jnp.ones((rows,128),bf16)
    def norm(i,_):
        at=block_of(i,256)
        v=node_input[at,:].astype(f32)
        centred=v-jnp.mean(v,axis=1,keepdims=True)
        normed[at,:]=centred*lax.rsqrt(jnp.mean(centred*centred,axis=1,keepdims=True)+norm_eps)
        return 0
    lax.fori_loop(0,rows//256,norm,0)
    groups=code.shape[0]
    half=groups//2
    count_groups(k.e,code,rows,0,half,8)
    wait_all(first)
    mod=k.modbuf[0]
    for i in range(1,8): mod=mod+k.modbuf[i]
    k.modulation[...]=mod

    kv=slice(0,256)
    across=[]; paired=[]
    for at in quarter:
        pos=node*rows+at.start+lax.broadcasted_iota(jnp.int32,(part,1),0)
        xn=(normed[at,:]*(1.0+by_batch(pos,limits,k.modulation,0,slice(0,512)))+by_batch(pos,limits,k.modulation,0,slice(512,1024))).astype(bf16)
        k.xn_one[at,:]=xn
        proj=jnp.dot(xn,k.qkv_full[...],preferred_element_type=f32).astype(bf16)
        k.queries[at,:]=proj[:,:128]
        k.table[0,at,kv]=proj[:,128:]
        across.append(go(k.table.at[0,at,kv],k.table.at[2,at,kv],head,node^2))
        paired.append(go(k.table.at[0,at,kv],k.table.at[1,at,kv],head,node^1))
    count_groups(k.e,code,rows,half,groups,8)
    add_self(k.e,0,rows)

    onward=[]
    def pass_keys(i):
        at=quarter[i]
        across[i].wait_recv()
        onward.append(go(k.table.at[2,at,kv],k.table.at[3,at,kv],head,node^4))
    def attend(b,at):
        attend_rows(b,b==0,at,k.queries,k.table,k.e,k.m,k.l,k.att,k.fac,scale*math.log2(math.e))
    def column(which):
        at=block_of(node^which,64)
        return [k.up_full.at[at],k.down_full.at[:,at],k.out_full.at[:,block_of(node^which,16)]]
    pass_keys(0)
    for at in quarter: attend(0,at)
    pass_keys(1)
    wait_all(paired)
    for at in quarter: attend(1,at)
    pass_keys(2)
    pass_keys(3)
    wait_all(along)
    own_column=column(0)
    to_x=[go(r,r,head,node^2) for r in own_column]
    to_y=[go(r,r,head,node^4) for r in own_column]
    to_pair=[go(r,r,head,node^1) for r in own_column]
    for at in quarter: attend(2,at)
    wait_all(onward)
    fifth=go(k.table.at[jnp.where(x_at==core,2,3),:,kv],k.table.at[4,:,kv],head,node^1)
    for at in quarter: attend(3,at)
    fifth.wait()
    lanes=block_of(head,128)
    moved=[]
    for i in range(4):
        at=quarter[i]
        attend(4,at)
        inv=1.0/k.l[at,:]
        o=k.att[at,:]*inv
        k.att[at,:]=o
        k.fac[at,:]=jnp.exp2(k.fac[at,:]-k.m[at,:])*inv
        k.mixed[at,:]=o.astype(bf16)
    for i in range(1,4):
        moved.append(go(k.mixed.at[block_of(head^i,part)],k.heads.at[:,lanes],head^i,node))
    k.heads[:,lanes]=k.mixed[mine,:]
    for c in across: c.wait_send()
    wait_all(to_x+to_y)
    from_x=column(2); from_y=column(4)
    cross=[go(from_x[0],from_x[0],head,node^4)]+[go(r,r,head,node^2) for r in from_y[1:]]
    hand=[go(r,r,head,node^1) for r in from_x+from_y]
    wait_all(cross)
    last=[go(r,r,head,node^1) for r in column(6)]
    scale_two=1.0+by_batch(own_pos,limits,k.modulation,4,slice(0,512))
    shift_two=by_batch(own_pos,limits,k.modulation,4,slice(512,1024))
    g=cotangent[mine,:]
    wait_all(moved)
    wait_all(to_pair+hand+last)

    out_all=k.out_full[...].reshape(512,512)
    y=node_input[mine,:].astype(f32)+jnp.dot(k.heads[...],out_all,preferred_element_type=f32)
    n_two,inv_two=norm_parts(y)
    xn=(n_two*scale_two+shift_two).astype(bf16)
    mlp=jnp.zeros((part,512),f32); dxn=jnp.zeros((part,512),f32)
    for j in range(4):
        s=slice(j*512,(j+1)*512)
        h=jnp.dot(xn,k.up_full[:,s],preferred_element_type=f32)
        gate=1.0/(1.0+jnp.exp(-h))
        u=(h*gate).astype(bf16)
        k.act[:,s]=u
        mlp+=jnp.dot(u,k.down_full[j],preferred_element_type=f32)
        du=lax.dot_general(g,k.down_full[j],NT,preferred_element_type=f32)
        d=(du*gate*(1.0+h*(1.0-gate))).astype(bf16)
        k.pre[:,s]=d
        dxn+=lax.dot_general(d,k.up_full[:,s],NT,preferred_element_type=f32)
    dyv=g.astype(f32)+norm_back(dxn*scale_two,n_two,inv_two)
    k.dy[...]=dyv
    da=dyv.astype(bf16)
    k.do_rows[...]=lax.dot_general(da,out_all,NT,preferred_element_type=f32).astype(bf16)
    returned=[]
    for i in range(1,4):
        returned.append(go(k.do_rows.at[:,block_of(head^i,128)],k.do.at[mine],head^i,node))
    k.do[mine,:]=k.do_rows[:,lanes]
    k.out_rows[...]=(y+mlp).astype(bf16)
    xn_t=xn.T
    heads_t=k.heads[...].T
    k.out_grad[...]=jnp.dot(heads_t,da,preferred_element_type=f32).astype(bf16).reshape(4,4,2,16,512)
    for j in range(4):
        s=slice(j*512,(j+1)*512)
        k.up_grad[:,:,:,s]=jnp.dot(xn_t,k.pre[:,s],preferred_element_type=f32).astype(bf16).reshape(4,2,64,512)
        k.down_grad[j]=jnp.dot(k.act[:,s].T,g,preferred_element_type=f32).astype(bf16).reshape(4,2,64,512)
    stage1=[go(k.up_grad.at[:,1-core],k.up1,head,node^1),go(k.down_grad.at[:,:,1-core],k.down1,head,node^1),go(k.out_grad.at[:,:,1-core],k.out1,head,node^1)]
    k.dm_own[4:8,0:512]=batch_sums(own_pos,limits,dxn*n_two)
    k.dm_own[4:8,512:1024]=batch_sums(own_pos,limits,dxn)
    wait_all(returned)
    shown=[go(k.out_rows,node_output.at[mine],head^i,node) for i in range(1,4)]
    node_output[mine,:]=k.out_rows[...]

    q_t=k.queries[...].T
    dof=k.do[...].astype(f32)
    delta=jnp.sum(dof*k.att[...],axis=1,keepdims=True)
    def block(b):
        def write(r,s,v):
            if b==0: k.dkv[r,s]=v
            else: k.near[b,r,s]=v.astype(bf16)
        back_block(b,q_t,dof,k.fac,delta,k.table,k.e,k.dq,write,b==4,512,scale)
    near=k.near
    block(4)
    give=go(near.at[4],k.got_pair,head,node^1)
    block(3)
    give.wait()
    @pl.when(x_at!=core)
    def _(): near[3]=summed(near[3],k.got_pair[...]).astype(bf16)
    via_y=[go(near.at[3,:,s],k.got_y.at[:,s],head,node^4) for s in quarter]
    block(2)
    @pl.when(x_at==core)
    def _(): near[2]=summed(near[2],k.got_pair[...]).astype(bf16)
    via_x=[]
    def pass_on(i):
        s=quarter[i]
        via_y[i].wait()
        near[2,:,s]=summed(near[2,:,s],k.got_y[:,s]).astype(bf16)
        via_x.append(go(near.at[2,:,s],k.got_x.at[:,s],head,node^2))
    pass_on(0)
    block(1)
    one=go(near.at[1],k.got_one,head,node^1)
    pass_on(1)
    pass_on(2)
    block(0)
    pass_on(3)
    wait_all(stage1)
    for i in range(4):
        k.up1[i]=summed(k.up1[i],k.up_grad[i,core]).astype(bf16)
        k.down1[i]=summed(k.down1[i],k.down_grad[i,:,core]).astype(bf16)
        k.out1[i]=summed(k.out1[i],k.out_grad[i,:,core]).astype(bf16)
    stage2=[go(k.up1.at[i*2+1-x_at],k.up2.at[i],head,node^2) for i in range(2)]
    there=pl.ds((1-y_at)*2,2)
    stage2+=[go(k.down1.at[:,there],k.down2,head,node^4),go(k.out1.at[:,there],k.out2,head,node^4)]
    xn_t=k.xn_one[...].T
    one.wait()
    for i in range(4):
        s=quarter[i]
        via_x[i].wait()
        total=k.dkv[:,s]+k.got_one[:,s].astype(f32)+k.got_x[:,s].astype(f32)
        k.proj_grad[s,128:]=total.T.astype(bf16)
        k.proj_grad[s,:128]=(k.dq[s,:]*scale).astype(bf16)
        k.partial[i]=lax.dot_general(k.proj_grad[s,:],k.qkv_full[...],NT,preferred_element_type=f32).astype(bf16)
    reduce=[go(k.partial.at[head^i],k.got_partial.at[i-1],head^i,node) for i in range(1,4)]
    k.qkv_grad[...]=jnp.dot(xn_t,k.proj_grad[...],preferred_element_type=f32).astype(bf16).reshape(8,64,384)
    qkv_moves=[go(k.qkv_grad.at[node^i],k.qkv_got.at[i-1],head,node^i) for i in range(1,8)]
    wait_all(stage2)
    for i in range(2):
        k.up2[i]=summed(k.up2[i],k.up1[i*2+x_at]).astype(bf16)
    here=pl.ds(y_at*2,2)
    k.down2[...]=summed(k.down2[...],k.down1[:,here]).astype(bf16)
    k.out2[...]=summed(k.out2[...],k.out1[:,here]).astype(bf16)
    stage3=[go(k.up2.at[1-y_at],k.up3,head,node^4),go(k.down2.at[:,1-x_at],k.down3,head,node^2),go(k.out2.at[:,1-x_at],k.out3,head,node^2)]
    scale_one=1.0+by_batch(own_pos,limits,k.modulation,0,slice(0,512))
    n_one,inv_one=norm_parts(node_input[mine,:].astype(f32))
    wait_all(qkv_moves)
    qkv_sum[...]=summed(k.qkv_grad[node],*[k.qkv_got[i] for i in range(7)])
    wait_all(stage3)
    k.up3[...]=summed(k.up3[...],k.up2[y_at]).astype(bf16)
    k.down3[...]=summed(k.down3[...],k.down2[:,x_at]).astype(bf16)
    k.out3[...]=summed(k.out3[...],k.out2[:,x_at]).astype(bf16)
    wait_all(reduce)
    dxn=summed(k.partial[head],*[k.got_partial[i] for i in range(3)])
    k.rows_grad[...]=(k.dy[...]+norm_back(dxn*scale_one,n_one,inv_one)).astype(bf16)
    spread=[go(k.rows_grad,row_all.at[head],head^i,node) for i in range(1,4)]
    row_all[head,:,:]=k.rows_grad[...]
    k.dm_own[0:4,0:512]=batch_sums(own_pos,limits,dxn*n_one)
    k.dm_own[0:4,512:1024]=batch_sums(own_pos,limits,dxn)
    dm_moves=[go(k.dm_own,k.dm_z.at[head],head^i,node) for i in range(1,4)]
    k.dm_z[head,:,:]=k.dm_own[...]
    stage4=[]
    for i in range(1,4):
        stage4+=[go(k.up3.at[:,block_of(head^i,512)],k.up_z.at[i-1],head^i,node),go(k.down3.at[head^i],k.down_z.at[i-1],head^i,node),go(k.out3.at[head^i],k.out_z.at[i-1],head^i,node)]
    wait_all(dm_moves)
    k.modp[...]=k.dm_z[0]+k.dm_z[1]+k.dm_z[2]+k.dm_z[3]
    dm_last=[go(k.modp,k.dm_n.at[node],head,node^i) for i in range(1,8)]
    k.dm_n[node,:,:]=k.modp[...]
    wait_all(dm_last)
    total=k.dm_n[0]
    for i in range(1,8): total=total+k.dm_n[i]
    mod_sum[...]=total
    wait_all(stage4)
    up_sum[...]=summed(k.up3[:,head_cols],*[k.up_z[i] for i in range(3)])
    down_sum[...]=summed(k.down3[head],*[k.down_z[i] for i in range(3)])
    out_sum[...]=summed(k.out3[head],*[k.out_z[i] for i in range(3)])
    wait_all(spread)
    wait_all(shown)


def finish_kernel(sigma, step_count, *refs):
    sources=refs[:22]; results=refs[22:39]; held=refs[39:62]; load,store=refs[62:]
    loads=[pltpu.make_async_copy(sources[i],held[i],load.at[i]) for i in range(22)]
    for i in (0,1)+tuple(range(7,22))+tuple(range(2,7)): loads[i].start()
    node=lax.axis_index("node")
    stores=[]
    def keep(ref, result):
        stores.append(pltpu.make_async_copy(ref,results[result],store.at[result])); stores[-1].start()
    loads[0].wait()
    keep(held[0],0)
    loads[1].wait()
    wide=held[22]
    rows=wide.shape[0]
    for i in range(4): wide[i*rows//4:(i+1)*rows//4,:]=held[1][i].astype(f32)
    keep(wide,1)
    count=jnp.full((8,128),step_count[0],jnp.int32).astype(f32)
    correct=(1.0-jnp.exp2(-count))[0:1,0:1]
    sig=sigma[:,0:64]
    for i in range(1,8): sig=jnp.where(node==i,sigma[:,i*64:(i+1)*64],sig)
    rates=((4*COND)**-0.5,(WIDTH//2)**-0.5,(WIDTH//4)**-0.5,WIDTH**-0.5,HIDDEN_SIZE**-0.5)
    for w in (0,3,4,1,2):
        at=7+3*w
        for i in range(3): loads[at+i].wait()
        if w==0:
            loads[6].wait()
            total=held[6]
            batch_grad=jnp.concatenate([total[0:4,:],total[4:8,:]],axis=1)
            grad=lax.dot_general(sig.astype(f32),batch_grad,(((0,),(0,)),((),())),precision=highest,preferred_element_type=f32)
        else:
            loads[1+w].wait()
            grad=held[1+w][...]
        master,first,second=held[at:at+3]
        first_new=beta_rate*first[...]+(1.0-beta_rate)*grad
        second_new=beta_rate*second[...]+(1.0-beta_rate)*grad*grad
        step=first_new/correct/(jnp.sqrt(second_new/correct)+adam_eps)
        old=master[...]
        master[...]=old-rates[w]*(step+weight_decay*old)
        first[...]=first_new
        second[...]=second_new
        for i in range(3): keep(held[at+i],2+3*w+i)
    for c in stores: c.wait()


def slots(neighbours, valid, node, rows):
    which=(neighbours//rows)^node
    slot=jnp.where(which==6,3,jnp.where((which==3)|(which==7),4,which))
    local=neighbours%rows
    spot=lax.broadcasted_iota(jnp.int32,neighbours.shape,0)%16
    hi=(slot*(rows//SPAN)+local//SPAN)*16+spot
    return jnp.where(valid>0,hi*256+local%SPAN,-1).reshape(-1,256)


def per_device_near(
    node_input, cotangent, sigma_embed, neighbours, neighbour_valid, batch_counts, step_count,
    ada_master, ada_first, ada_second, qkv_master, qkv_first, qkv_second, out_master, out_first, out_second,
    up_master, up_first, up_second, down_master, down_first, down_second,
):
    rows=node_input.shape[0]
    code=slots(neighbours,neighbour_valid,lax.axis_index("node"),rows)
    masters=(ada_master,qkv_master,out_master,up_master,down_master)
    firsts=(ada_first,qkv_first,out_first,up_first,down_first)
    seconds=(ada_second,qkv_second,out_second,up_second,down_second)
    V=pltpu.VMEM
    full=pl.BlockSpec(memory_space=V); few=pl.BlockSpec(memory_space=pltpu.SMEM); hbm=pl.BlockSpec(memory_space=pltpu.HBM)
    S=jax.ShapeDtypeStruct
    held=scratch(rows)
    sums=pl.pallas_call(functools.partial(layer_kernel,128**-0.5,tuple(held)),
        out_shape=(S((rows,512),bf16),S((4,rows//4,512),bf16))+tuple(S(a.shape,f32) for a in masters[1:])+(S((8,1024),f32),),
        in_specs=[full]*4+[few]+[full]*5,
        out_specs=(full,)*7,
        scratch_shapes=[V(*v) for v in held.values()]+[pltpu.SemaphoreType.DMA((COPIES,))]*2,
        compiler_params=pltpu.CompilerParams(vmem_limit_bytes=67043328,collective_id=1,has_side_effects=True),
        name="layer")(node_input,cotangent,sigma_embed,code,batch_counts,*masters)
    news=tuple(S(a.shape,f32) for a in masters for _ in range(3))
    inner=[V(a.shape,a.dtype) for a in sums]+[V(a.shape,f32) for a in masters for _ in range(3)]+[V((rows,512),f32)]
    return pl.pallas_call(finish_kernel,
        out_shape=(S((rows,512),bf16),S((rows,512),f32))+news,
        in_specs=[full,few]+[hbm]*(7+15),
        out_specs=(hbm,)*17,
        scratch_shapes=inner+[pltpu.SemaphoreType.DMA((22,)),pltpu.SemaphoreType.DMA((17,))],
        compiler_params=pltpu.CompilerParams(vmem_limit_bytes=67043328),
        name="finish")(sigma_embed,step_count,*sums,*[a for three in zip(masters,firsts,seconds) for a in three])


def wide_count_groups(cnt, hik, lok, rows):
    steps=hik.shape[0]
    parts=rows//SPAN
    total=5*parts*16
    rowid=lax.broadcasted_iota(jnp.int32,(total,1),0)
    rowkey=lax.div(rowid,16)*16+lax.rem(rowid,16)
    spot=lax.broadcasted_iota(jnp.int32,(SPAN,1),0)
    def body(g,_):
        keys=hik[pl.ds(g,1),:]
        low=lok[pl.ds(g,1),:]
        left=jnp.where(rowkey==keys,1.0,0.0).astype(bf16)
        right=jnp.where(spot==low,1.0,0.0).astype(bf16)
        made=lax.dot_general(left,right,NT,preferred_element_type=f32).astype(bf16)
        at=pl.multiple_of(g*16,16)
        for b in range(5):
            for p in range(parts):
                r=(b*parts+p)*16
                cnt[b,pl.ds(at,16),p*SPAN:(p+1)*SPAN]=made[r:r+16,:]
        return 0
    lax.fori_loop(0,steps,body,0)

def wide_add_self(cnt, block, rows):
    eye=(lax.broadcasted_iota(jnp.int32,(SPAN,SPAN),0)==lax.broadcasted_iota(jnp.int32,(SPAN,SPAN),1))
    one=jnp.where(eye,1.0,0.0).astype(bf16)
    for p in range(rows//SPAN):
        s=slice(p*SPAN,(p+1)*SPAN)
        cnt[block,s,s]=cnt[block,s,s]+one

def wide_attend_block(b, first, q, keys, vals, cnt, e, m, l, acc, fac, chunk, scale):
    rows=q.shape[0]
    lane=lax.broadcasted_iota(jnp.int32,(chunk,128),1)
    def body(i,_):
        at=pl.ds(pl.multiple_of(i*chunk,chunk),chunk)
        s=lax.dot_general(q[at,:],keys,NT,preferred_element_type=f32)*scale
        c=cnt[b,at,:].astype(f32)
        s=jnp.where(c>0,s,-1e30)
        top=jnp.max(s,axis=1,keepdims=True)
        if not first:
            old=m[at,0:1]
            top=jnp.maximum(top,old)
        w=(jnp.exp2(s-top)*c)
        total=jnp.sum(w,axis=1,keepdims=True)
        w=w.astype(bf16)
        e[b,at,:]=w
        out=jnp.dot(w,vals,preferred_element_type=f32)
        if first:
            acc[at,:]=out; l[at,:]=jnp.broadcast_to(total,(chunk,128))
            fac[at,:]=jnp.where(lane==b,top,0.0)
        else:
            shrink=jnp.exp2(old-top)
            acc[at,:]=acc[at,:]*shrink+out
            l[at,:]=l[at,:]*shrink+total
            fac[at,:]=jnp.where(lane==b,top,fac[at,:])
        m[at,:]=jnp.broadcast_to(top,(chunk,128))
        return 0
    lax.fori_loop(0,rows//chunk,body,0)

def wide_fwd_kernel(order, self_block, scale, q, kv, hik, lok, att, e, fac, cnt, m, l):
    rows=q.shape[0]
    wide_count_groups(cnt,hik,lok,rows)
    wide_add_self(cnt,self_block,rows)
    for t,b in enumerate(order):
        wide_attend_block(b,t==0,q,kv[b,:,:128],kv[b,:,128:],cnt,e,m,l,att,fac,256,scale)
    inv=1.0/l[...]
    att[...]=att[...]*inv
    fac[...]=jnp.exp2(fac[...]-m[...])*inv

def wide_attention_fwd(q,kv,hik,lok,scale):
    rows=q.shape[0]
    V=pltpu.VMEM
    full=pl.BlockSpec(memory_space=V)
    return pl.pallas_call(functools.partial(wide_fwd_kernel,(2,1,3,0,4),2,scale*math.log2(math.e)),
        out_shape=(jax.ShapeDtypeStruct((rows,128),f32),jax.ShapeDtypeStruct((5,rows,rows),bf16),jax.ShapeDtypeStruct((rows,128),f32)),
        in_specs=[full]*4,out_specs=(full,)*3,
        scratch_shapes=[V((5,rows,rows),bf16),V((rows,128),f32),V((rows,128),f32)],
        compiler_params=pltpu.CompilerParams(vmem_limit_bytes=60<<20),name="attend_fwd")(q,kv,hik,lok)

def wide_back_block(b, q_t, do, fac, delta, kv, e, dq, dkv, first, chunk, keyscale):
    rows=do.shape[0]
    f=fac[:,b:b+1]
    dob=(do*f)
    dobh=dob.astype(bf16)
    d=-(delta*f)
    h=d.astype(bf16); r=d-h.astype(f32); h2=r.astype(bf16); h3=(r-h2.astype(f32)).astype(bf16)
    lane=lax.broadcasted_iota(jnp.int32,(rows,128),1)
    zero=jnp.zeros((rows,128),bf16)
    dcol=jnp.where(lane==0,h.astype(f32),jnp.where(lane==1,h2.astype(f32),jnp.where(lane==2,h3.astype(f32),0.0))).astype(bf16)
    left=jnp.concatenate([dobh,dcol],axis=1)
    dob_t=dobh.T
    ones=jnp.ones((chunk,128),bf16)
    for i in range(kv.shape[1]//chunk):
        s=slice(i*chunk,(i+1)*chunk)
        right=jnp.concatenate([kv[b,s,128:],ones],axis=1)
        dp=lax.dot_general(left,right,NT,preferred_element_type=f32)
        w=e[b,:,s]
        ds=(dp*w.astype(f32)).astype(bf16)
        dkv[b,:128,s]=jnp.dot(q_t,ds,preferred_element_type=f32)*keyscale
        dkv[b,128:,s]=jnp.dot(dob_t,w,preferred_element_type=f32)
        out=jnp.dot(ds,kv[b,s,:128],preferred_element_type=f32)
        if first and i==0: dq[...]=out
        else: dq[...]+=out

def wide_bwd_kernel(scale, q, do, att, fac, kv, e, dq, dkv, ):
    q_t=q[...].T
    dof=do[...].astype(f32)
    delta=jnp.sum(dof*att[...],axis=1,keepdims=True)
    for t,b in enumerate((0,4,1,3,2)):
        wide_back_block(b,q_t,dof,fac,delta,kv,e,dq,dkv,t==0,512,scale)
    dq[...]=dq[...]*scale

def wide_attention_bwd(q,do,att,fac,kv,e,scale):
    rows=q.shape[0]
    V=pltpu.VMEM
    full=pl.BlockSpec(memory_space=V)
    return pl.pallas_call(functools.partial(wide_bwd_kernel,scale),
        out_shape=(jax.ShapeDtypeStruct((rows,128),f32),jax.ShapeDtypeStruct((5,256,rows),f32)),
        in_specs=[full]*6,out_specs=(full,)*2,
        compiler_params=pltpu.CompilerParams(vmem_limit_bytes=60<<20),name="attend_bwd")(q,do,att,fac,kv,e)

def wide_tables(slot_index, valid, rows):
    parts=rows//SPAN
    flat=slot_index.reshape(-1,256)
    ok=(valid>0).reshape(-1,256)
    node=lax.broadcasted_iota(jnp.int32,flat.shape,1)//16
    hi=jnp.where(ok,(flat//SPAN)*16+node,-1)
    lo=flat%SPAN
    return hi,lo


def per_device(
    node_input,
    cotangent,
    sigma_embed,
    neighbours,
    neighbour_valid,
    batch_counts,
    step_count,
    ada_master,
    ada_first,
    ada_second,
    qkv_master,
    qkv_first,
    qkv_second,
    out_master,
    out_first,
    out_second,
    up_master,
    up_first,
    up_second,
    down_master,
    down_first,
    down_second,
):
    f32 = jnp.float32
    bf16 = jnp.bfloat16
    node_rows = node_input.shape[0]
    model_width = node_input.shape[1]
    head_dim = qkv_master.shape[1] // 3
    score_scale = head_dim ** (-0.5)
    node_index = lax.axis_index("node")
    total_nodes = node_rows * lax.axis_size("node")
    qkv_full, out_full, up_full, down_full = (
        lax.all_gather(qkv_master.astype(bf16), "node", axis=0, tiled=True),
        lax.all_gather(out_master.astype(bf16), "node", axis=0, tiled=True),
        lax.all_gather(up_master.astype(bf16), "node", axis=0, tiled=True),
        lax.all_gather(down_master.astype(bf16), "node", axis=0, tiled=True),
    )
    cond_rows = ada_master.shape[0]
    sigma_part = lax.dynamic_slice_in_dim(sigma_embed, node_index * cond_rows, cond_rows, 1)
    limits = jnp.cumsum(batch_counts)[:-1]
    positions = node_index * node_rows + jnp.arange(node_rows, dtype=jnp.int32)
    member = jnp.sum((positions[:, None] >= limits[None, :]).astype(jnp.int32), axis=1)
    onehot = (
        member[:, None] == jnp.arange(batch_counts.shape[0], dtype=jnp.int32)[None, :]
    ).astype(f32)
    modulation = lax.psum(
        jnp.dot(sigma_part, ada_master.astype(bf16), preferred_element_type=f32), "node"
    )
    per_node = jnp.dot(onehot, modulation, precision=highest)
    scale_one = per_node[:, :model_width]
    shift_one = per_node[:, model_width : 2 * model_width]
    scale_two = per_node[:, 2 * model_width : 3 * model_width]
    shift_two = per_node[:, 3 * model_width :]
    normed_one, inverse_one = norm_parts(node_input.astype(f32))
    xn_one = (normed_one * (1.0 + scale_one) + shift_one).astype(bf16)
    projected = jnp.dot(xn_one, qkv_full, preferred_element_type=f32).astype(bf16)
    queries = projected[:, :head_dim]
    keys_values = projected[:, head_dim:]
    offsets = (-2, -1, 1, 2)
    fetched = {0: keys_values}
    for offset in offsets:
        fetched[offset] = passed_along(keys_values, "node", -offset)
    table = jnp.stack([fetched[offset] for offset in (-2, -1, 0, 1, 2)], axis=0)
    slot_index = jnp.mod(neighbours - (node_index - 2) * node_rows, total_nodes)
    high_keys, low_keys = wide_tables(slot_index, neighbour_valid, node_rows)
    mixed, weights, factors = wide_attention_fwd(queries, table, high_keys, low_keys, score_scale)
    heads_out = mixed.astype(bf16)
    branch = lax.psum(
        jnp.dot(heads_out, out_full, preferred_element_type=f32).astype(jnp.bfloat16), "head"
    ).astype(jnp.float32)
    middle = node_input.astype(f32) + branch
    normed_two, inverse_two = norm_parts(middle)
    xn_two = (normed_two * (1.0 + scale_two) + shift_two).astype(bf16)
    hidden_pre = jnp.dot(xn_two, up_full, preferred_element_type=f32)
    gate_sig = jax.nn.sigmoid(hidden_pre)
    activated = (hidden_pre * gate_sig).astype(bf16)
    mlp_sum = lax.psum(
        jnp.dot(activated, down_full, preferred_element_type=f32).astype(jnp.bfloat16), "head"
    ).astype(jnp.float32)
    node_output = (middle + mlp_sum).astype(bf16)
    down_grad = jnp.einsum("nf,nd->fd", activated, cotangent, preferred_element_type=f32)
    act_grad = jnp.einsum("nd,fd->nf", cotangent, down_full, preferred_element_type=f32)
    pre_grad = (act_grad * gate_sig * (1.0 + hidden_pre * (1.0 - gate_sig))).astype(bf16)
    up_grad = jnp.einsum("nw,nf->wf", xn_two, pre_grad, preferred_element_type=f32)
    normed_two_grad = lax.psum(
        jnp.einsum("nf,wf->nw", pre_grad, up_full, preferred_element_type=f32).astype(jnp.bfloat16),
        "head",
    ).astype(jnp.float32)
    middle_grad = cotangent.astype(f32) + norm_back(
        normed_two_grad * (1.0 + scale_two), normed_two, inverse_two
    )
    branch_grad = middle_grad.astype(bf16)
    out_grad = jnp.einsum("nh,nd->hd", heads_out, branch_grad, preferred_element_type=f32)
    mixed_grad = jnp.einsum("nd,hd->nh", branch_grad, out_full, preferred_element_type=f32).astype(
        bf16
    )
    query_grad, pair_sums = wide_attention_bwd(
        queries, mixed_grad, mixed, factors, table, weights, score_scale
    )
    remote_terms = pair_sums[2]
    for offset in offsets:
        remote_terms = remote_terms + passed_along(
            pair_sums[offset + 2].astype(bf16), "node", offset
        ).astype(f32)
    key_value_grad = remote_terms.T
    projected_grad = jnp.concatenate([query_grad, key_value_grad], axis=1).astype(bf16)
    qkv_grad = jnp.einsum("nw,nc->wc", xn_one, projected_grad, preferred_element_type=f32)
    normed_one_grad = lax.psum(
        jnp.einsum("nc,wc->nw", projected_grad, qkv_full, preferred_element_type=f32).astype(
            jnp.bfloat16
        ),
        "head",
    ).astype(jnp.float32)
    input_grad = middle_grad + norm_back(
        normed_one_grad * (1.0 + scale_one), normed_one, inverse_one
    )
    rows_grad = jnp.concatenate(
        [
            normed_one_grad * normed_one,
            normed_one_grad,
            normed_two_grad * normed_two,
            normed_two_grad,
        ],
        axis=1,
    )
    batch_grad = jnp.dot(onehot.T, rows_grad, precision=highest)
    batch_grad = lax.psum(batch_grad, "node")
    ada_sum = jnp.dot(sigma_part.astype(f32).T, batch_grad, precision=highest)
    qkv_sum, out_sum, up_sum, down_sum = (
        lax.psum_scatter(qkv_grad, "node", scatter_dimension=0, tiled=True),
        lax.psum_scatter(out_grad, "node", scatter_dimension=0, tiled=True),
        lax.psum_scatter(up_grad, "node", scatter_dimension=0, tiled=True),
        lax.psum_scatter(down_grad, "node", scatter_dimension=0, tiled=True),
    )
    count_value = step_count[0].astype(f32)
    ada_res = adamw_update(
        ada_master, ada_first, ada_second, ada_sum, (4 * COND) ** (-0.5), count_value
    )
    qkv_res = adamw_update(
        qkv_master, qkv_first, qkv_second, qkv_sum, (WIDTH // 2) ** (-0.5), count_value
    )
    out_res = adamw_update(
        out_master, out_first, out_second, out_sum, (WIDTH // 4) ** (-0.5), count_value
    )
    up_res = adamw_update(up_master, up_first, up_second, up_sum, WIDTH ** (-0.5), count_value)
    down_res = adamw_update(
        down_master, down_first, down_second, down_sum, HIDDEN_SIZE ** (-0.5), count_value
    )
    return (
        node_output,
        input_grad,
        ada_res[0],
        ada_res[1],
        ada_res[2],
        qkv_res[0],
        qkv_res[1],
        qkv_res[2],
        out_res[0],
        out_res[1],
        out_res[2],
        up_res[0],
        up_res[1],
        up_res[2],
        down_res[0],
        down_res[1],
        down_res[2],
    )


def solution(mesh):
    chosen = per_device_near if mesh.shape["node"] == 8 and mesh.shape["head"] == 4 else per_device
    placed = (
        P("node", None),
        P("node", None),
        P(),
        P("node", None),
        P("node", None),
        P(),
        P(),
        P("node", None),
        P("node", None),
        P("node", None),
        P("node", "head"),
        P("node", "head"),
        P("node", "head"),
        P(("head", "node"), None),
        P(("head", "node"), None),
        P(("head", "node"), None),
        P("node", "head"),
        P("node", "head"),
        P("node", "head"),
        P(("head", "node"), None),
        P(("head", "node"), None),
        P(("head", "node"), None),
    )
    return jax.shard_map(
        chosen,
        mesh=mesh,
        in_specs=placed,
        out_specs=(
            P("node", None),
            P("node", None),
            P("node", None),
            P("node", None),
            P("node", None),
            P("node", "head"),
            P("node", "head"),
            P("node", "head"),
            P(("head", "node"), None),
            P(("head", "node"), None),
            P(("head", "node"), None),
            P("node", "head"),
            P("node", "head"),
            P("node", "head"),
            P(("head", "node"), None),
            P(("head", "node"), None),
            P(("head", "node"), None),
        ),
        check_vma=False,
    )
```

```python
import functools
import math

import jax
import jax.numpy as jnp
from jax import lax
from jax.experimental import pallas as pl
from jax.experimental.pallas import tpu as pltpu
from jax.sharding import PartitionSpec as P


WIDTH = 512
HIDDEN_SIZE = 2048
COND = 512


norm_eps = 1e-06
beta_rate = 0.5
adam_eps = 1e-08
weight_decay = 0.1
highest = lax.Precision.HIGHEST


def passed_along(block, axis, distance):
    devices = range(lax.axis_size(axis))
    route = [((i - distance) % len(devices), i) for i in devices]
    return lax.ppermute(block, axis, route)


def norm_parts(values):
    centred = values - jnp.mean(values, axis=1, keepdims=True)
    inverse = lax.rsqrt(jnp.mean(centred * centred, axis=1, keepdims=True) + norm_eps)
    return (centred * inverse, inverse)


def norm_back(grad_normed, normed, inverse):
    first_mean = jnp.mean(grad_normed, axis=1, keepdims=True)
    second_mean = jnp.mean(grad_normed * normed, axis=1, keepdims=True)
    return inverse * (grad_normed - first_mean - normed * second_mean)


def adamw_update(master, first, second, grad, rate, count_value):
    first_new = beta_rate * first + (1.0 - beta_rate) * grad
    second_new = beta_rate * second + (1.0 - beta_rate) * grad * grad
    correct = 1.0 - jnp.power(jnp.float32(beta_rate), count_value)
    normed_step = first_new / correct / (jnp.sqrt(second_new / correct) + adam_eps)
    master_new = master - rate * (normed_step + weight_decay * master)
    return (master_new, first_new, second_new)


f32=jnp.float32; bf16=jnp.bfloat16
NT=(((1,),(1,)),((),()))
SPAN=256

def count_groups(cnt, code, rows, start, stop, step):
    parts=rows//SPAN
    total=5*parts*16
    short=jnp.int16
    rowid=lax.broadcasted_iota(jnp.int32,(total,SPAN),0).astype(short)
    spot=lax.broadcasted_iota(jnp.int32,(SPAN,SPAN),0).astype(short)
    one=bf16(1); zero=bf16(0)
    def group(g):
        both=code[pl.ds(g,1),:]
        keys=lax.shift_right_arithmetic(both,8).astype(short)
        low=lax.bitwise_and(both,255).astype(short)
        left=jnp.where(rowid==jnp.broadcast_to(keys,(total,SPAN)),one,zero)
        right=jnp.where(spot==jnp.broadcast_to(low,(SPAN,SPAN)),one,zero)
        made=lax.dot_general(left,right,NT,preferred_element_type=f32).astype(bf16)
        at=pl.multiple_of(g*16,16)
        for b in range(5):
            for p in range(parts):
                r=(b*parts+p)*16
                cnt[b,pl.ds(at,16),p*SPAN:(p+1)*SPAN]=made[r:r+16,:]
    def body(g,_):
        for u in range(step): group(g*step+u)
        return 0
    lax.fori_loop(start//step,stop//step,body,0)

def add_self(cnt, block, rows):
    eye=(lax.broadcasted_iota(jnp.int32,(SPAN,SPAN),0)==lax.broadcasted_iota(jnp.int32,(SPAN,SPAN),1))
    one=jnp.where(eye,1.0,0.0).astype(bf16)
    for p in range(rows//SPAN):
        s=slice(p*SPAN,(p+1)*SPAN)
        cnt[block,s,s]=cnt[block,s,s]+one

def attend_rows(b, first, at, q, table, e, m, l, acc, fac, scale):
    size=at.stop-at.start
    lane=lax.broadcasted_iota(jnp.int32,(size,128),1)
    s=lax.dot_general(q[at,:],table[b,:,0:128],NT,preferred_element_type=f32)*scale
    c=e[b,at,:].astype(f32)
    s=jnp.where(c>0,s,-1e30)
    top=jnp.max(s,axis=1,keepdims=True)
    if not first:
        old=m[at,0:1]
        top=jnp.maximum(top,old)
    w=(jnp.exp2(s-top)*c).astype(bf16)
    e[b,at,:]=w
    out=jnp.dot(w,table[b,:,128:384],preferred_element_type=f32)
    if first:
        acc[at,:]=out[:,:128]; l[at,:]=out[:,128:]
        fac[at,:]=jnp.where(lane==b,top,0.0)
    else:
        shrink=jnp.exp2(old-top)
        acc[at,:]=acc[at,:]*shrink+out[:,:128]
        l[at,:]=l[at,:]*shrink+out[:,128:]
        fac[at,:]=jnp.where(lane==b,top,fac[at,:])
    m[at,:]=jnp.broadcast_to(top,(size,128))

def back_block(b, q_t, dof, fac, delta, table, e, dq, write, first, chunk, keyscale):
    rows=dof.shape[0]
    f=fac[:,b:b+1]
    dobh=(dof*f).astype(bf16)
    d=-(delta*f)
    h=d.astype(bf16); r=d-h.astype(f32); h2=r.astype(bf16); h3=(r-h2.astype(f32)).astype(bf16)
    lane=lax.broadcasted_iota(jnp.int32,(rows,128),1)
    dcol=jnp.where(lane==0,h.astype(f32),jnp.where(lane==1,h2.astype(f32),jnp.where(lane==2,h3.astype(f32),0.0))).astype(bf16)
    left=jnp.concatenate([dobh,dcol],axis=1)
    dob_t=dobh.T
    for i in range(rows//chunk):
        s=slice(i*chunk,(i+1)*chunk)
        dp=lax.dot_general(left,table[b,s,128:384],NT,preferred_element_type=f32)
        w=e[b,:,s]
        ds=(dp*w.astype(f32)).astype(bf16)
        write(slice(0,128),s,jnp.dot(q_t,ds,preferred_element_type=f32)*keyscale)
        write(slice(128,256),s,jnp.dot(dob_t,w,preferred_element_type=f32))
        out=jnp.dot(ds,table[b,s,0:128],preferred_element_type=f32)
        if first and i==0: dq[...]=out
        else: dq[...]+=out


def by_batch(pos, limits, table, row, lanes):
    pick=[table[row+b:row+b+1,lanes] for b in range(4)]
    out=jnp.where(pos>=limits[0],pick[1],pick[0])
    out=jnp.where(pos>=limits[1],pick[2],out)
    return jnp.where(pos>=limits[2],pick[3],out)


def batch_sums(pos, limits, values):
    lane=lax.broadcasted_iota(jnp.int32,(pos.shape[0],8),1)
    member=(pos>=limits[0]).astype(jnp.int32)+(pos>=limits[1]).astype(jnp.int32)+(pos>=limits[2]).astype(jnp.int32)
    onehot=jnp.where(lane==member,1.0,0.0).astype(f32)
    return lax.dot_general(onehot,values,(((0,),(0,)),((),())),precision=highest,preferred_element_type=f32)[0:4,:]


class Links:
    def __init__(self, send, recv):
        self.send, self.recv, self.used = send, recv, 0

    def copy(self, src, dst, head, node):
        made=pltpu.make_async_remote_copy(src_ref=src,dst_ref=dst,send_sem=self.send.at[self.used],recv_sem=self.recv.at[self.used],
            device_id=(head,node),device_id_type=pl.DeviceIdType.MESH)
        self.used+=1
        return made

    def go(self, src, dst, head, node):
        made=self.copy(src,dst,head,node)
        made.start()
        return made


def meet(peers):
    barrier=pltpu.get_barrier_semaphore()
    for head,node in peers:
        pl.semaphore_signal(barrier,inc=1,device_id=(head,node),device_id_type=pl.DeviceIdType.MESH)
    pl.semaphore_wait(barrier,len(peers))


class Shown:
    def __init__(self, links, head, node, place):
        self.end=(head==0)|(head==3)
        own=place(head)
        self.two=links.go(own,own,head^2,node)
        self.one=links.go(own,own,head^1,node)
        self.three=links.copy(own,own,head^3,node)
        pl.when(~self.end)(self.three.start)
        far=place(jnp.where(self.end,head^3,head^2))
        self.pass_copy=links.copy(far,far,head^1,node)

    def onward(self):
        @pl.when(~self.end)
        def _():
            self.two.wait_recv()
            self.pass_copy.start()

    def wait(self):
        self.one.wait()
        self.two.wait_send()
        @pl.when(self.end)
        def _():
            self.two.wait_recv()
            self.pass_copy.wait_recv()
        @pl.when(~self.end)
        def _():
            self.three.wait()
            self.pass_copy.wait_send()


class Added:
    def __init__(self, links, head, node, part, got, relay):
        self.end=(head==0)|(head==3)
        self.relay=relay
        self.far=part(head^2)
        self.zero=links.copy(part(head^3),relay,head^1,node)
        self.two=links.copy(self.far,got(1),head^2,node)
        self.one=links.copy(part(head^1),got(0),head^1,node)
        self.three=links.copy(part(head^3),got(2),head^3,node)
        @pl.when(self.end)
        def _():
            self.zero.start()
            self.two.start()
            self.one.start()
            got(2)[...]=jnp.zeros(relay.shape,bf16)
        @pl.when(~self.end)
        def _():
            self.three.start()
            self.one.start()

    def onward(self):
        @pl.when(~self.end)
        def _():
            self.zero.wait_recv()
            self.far[...]=summed(self.far,self.relay).astype(bf16)
            self.two.start()

    def wait(self):
        pl.when(self.end)(self.zero.wait_send)
        pl.when(~self.end)(self.three.wait)
        self.one.wait()
        self.two.wait()


def wait_all(copies):
    for c in copies: c.wait()


def block_of(index, size):
    return pl.ds(pl.multiple_of(index*size,size),size)


def summed(*refs):
    total=refs[0][...].astype(f32)
    for r in refs[1:]: total=total+r[...].astype(f32)
    return total


NAMES=("ada","qkv","out","up","down")


def scratch(rows):
    part=rows//4
    return dict(
        e=((5,rows,rows),bf16),m=((rows,128),f32),l=((rows,128),f32),att=((rows,128),f32),fac=((rows,128),f32),
        queries=((rows,128),bf16),table=((5,rows,384),bf16),xn_one=((rows,512),bf16),
        qkv_full=((512,384),bf16),out_full=((4,128,512),bf16),up_full=((512,2048),bf16),down_full=((4,512,512),bf16),
        modp=((8,1024),f32),modbuf=((8,8,1024),f32),modulation=((8,1024),f32),
        mixed=((rows,128),bf16),heads=((part,512),bf16),do=((rows,128),bf16),do_rows=((part,512),bf16),
        act=((part,2048),bf16),pre=((part,2048),bf16),dy=((part,512),f32),
        up_grad=((4,2,64,2048),bf16),down_grad=((4,4,2,64,512),bf16),out_grad=((4,4,2,16,512),bf16),
        dq=((rows,128),f32),dkv=((256,rows),f32),near=((5,256,rows),bf16),
        got_pair=((256,rows),bf16),got_y=((256,rows),bf16),got_x=((256,rows),bf16),got_one=((256,rows),bf16),
        proj_grad=((rows,384),bf16),partial=((4,part,512),bf16),got_partial=((3,part,512),bf16),normed=((rows,512),f32),
        up1=((4,64,2048),bf16),down1=((4,4,64,512),bf16),out1=((4,4,16,512),bf16),
        up2=((2,64,2048),bf16),down2=((4,2,64,512),bf16),out2=((4,2,16,512),bf16),
        up3=((64,2048),bf16),down3=((4,64,512),bf16),out3=((4,16,512),bf16),
        up_z=((3,64,512),bf16),down_z=((3,64,512),bf16),out_z=((3,16,512),bf16),
        up_relay=((64,512),bf16),down_relay=((64,512),bf16),out_relay=((16,512),bf16),relay=((part,512),bf16),
        qkv_grad=((8,64,384),bf16),qkv_got=((7,64,384),bf16),dm_own=((8,1024),f32),dm_z=((4,8,1024),f32),dm_n=((8,8,1024),f32),
    )


class Bag:
    pass


COPIES=150


def layer_kernel(scale, names, *refs):
    refs=list(refs)
    take=lambda n: [refs.pop(0) for _ in range(n)]
    node_input,cotangent,sigma,code,counts=take(5)
    w={n:refs.pop(0) for n in NAMES}
    node_output,row_all,qkv_sum,out_sum,up_sum,down_sum,mod_sum=take(7)
    k=Bag()
    for n in names: setattr(k,n,refs.pop(0))
    send,recv=take(2)
    head=lax.axis_index("head"); node=lax.axis_index("node")
    y_at=node//4; x_at=(node//2)%2; core=node%2
    rows=node_input.shape[0]
    part=rows//4
    links=Links(send,recv)
    go=links.go
    normed=k.normed
    quarter=[slice(i*part,(i+1)*part) for i in range(4)]
    limits=(counts[0],counts[0]+counts[1],counts[0]+counts[1]+counts[2])
    mine=block_of(head,part)
    head_cols=block_of(head,512)
    own_pos=node*rows+head*part+lax.broadcasted_iota(jnp.int32,(part,1),0)

    own=block_of(node,64); own_out=block_of(node,16)
    k.qkv_full[own,:]=w["qkv"][...].astype(bf16)
    sig=sigma[:,0:64]
    for i in range(1,8): sig=jnp.where(node==i,sigma[:,i*64:(i+1)*64],sig)
    made=jnp.dot(sig,w["ada"][...].astype(bf16),preferred_element_type=f32)
    k.modp[0:4,:]=made[:,:1024]
    k.modp[4:8,:]=made[:,1024:]
    k.up_full[own,head_cols]=w["up"][...].astype(bf16)
    k.down_full[head,own,:]=w["down"][...].astype(bf16)
    k.out_full[head,own_out,:]=w["out"][...].astype(bf16)
    meet([(head,node^i) for i in range(1,8)]+[(head^i,node) for i in range(1,4)])
    first=[]
    for i in range(1,8):
        first.append(go(k.modp,k.modbuf.at[node],head,node^i))
        first.append(go(k.qkv_full.at[own],k.qkv_full.at[own],head,node^i))
    along=[]
    for place in (lambda h: k.up_full.at[own,block_of(h,512)],lambda h: k.down_full.at[h,own],lambda h: k.out_full.at[h,own_out]):
        along.append(Shown(links,head,node,place))
    k.modbuf[node,:,:]=k.modp[...]
    for b in range(5): k.table[b,:,256:384]=jnp.ones((rows,128),bf16)
    def norm(i,_):
        at=block_of(i,256)
        v=node_input[at,:].astype(f32)
        centred=v-jnp.mean(v,axis=1,keepdims=True)
        normed[at,:]=centred*lax.rsqrt(jnp.mean(centred*centred,axis=1,keepdims=True)+norm_eps)
        return 0
    lax.fori_loop(0,rows//256,norm,0)
    groups=code.shape[0]
    half=groups//2
    count_groups(k.e,code,rows,0,half,4)
    for a in along: a.onward()
    wait_all(first)
    mod=k.modbuf[0]
    for i in range(1,8): mod=mod+k.modbuf[i]
    k.modulation[...]=mod

    kv=slice(0,256)
    across=[]; paired=[]
    for at in quarter:
        pos=node*rows+at.start+lax.broadcasted_iota(jnp.int32,(part,1),0)
        xn=(normed[at,:]*(1.0+by_batch(pos,limits,k.modulation,0,slice(0,512)))+by_batch(pos,limits,k.modulation,0,slice(512,1024))).astype(bf16)
        k.xn_one[at,:]=xn
        proj=jnp.dot(xn,k.qkv_full[...],preferred_element_type=f32).astype(bf16)
        k.queries[at,:]=proj[:,:128]
        k.table[0,at,kv]=proj[:,128:]
        across.append(go(k.table.at[0,at,kv],k.table.at[2,at,kv],head,node^2))
        paired.append(go(k.table.at[0,at,kv],k.table.at[1,at,kv],head,node^1))
    count_groups(k.e,code,rows,half,groups,4)
    add_self(k.e,0,rows)

    onward=[]
    def pass_keys(i):
        at=quarter[i]
        across[i].wait_recv()
        onward.append(go(k.table.at[2,at,kv],k.table.at[3,at,kv],head,node^4))
    def attend(b,at):
        attend_rows(b,b==0,at,k.queries,k.table,k.e,k.m,k.l,k.att,k.fac,scale*math.log2(math.e))
    def column(which):
        at=block_of(node^which,64)
        return [k.up_full.at[at],k.down_full.at[:,at],k.out_full.at[:,block_of(node^which,16)]]
    pass_keys(0)
    for at in quarter: attend(0,at)
    pass_keys(1)
    wait_all(paired)
    for at in quarter: attend(1,at)
    pass_keys(2)
    pass_keys(3)
    wait_all(along)
    own_column=column(0)
    to_x=[go(r,r,head,node^2) for r in own_column]
    to_y=[go(r,r,head,node^4) for r in own_column]
    to_pair=[go(r,r,head,node^1) for r in own_column]
    for at in quarter: attend(2,at)
    wait_all(onward)
    fifth=go(k.table.at[jnp.where(x_at==core,2,3),:,kv],k.table.at[4,:,kv],head,node^1)
    for at in quarter: attend(3,at)
    fifth.wait()
    lanes=block_of(head,128)
    moved=[]
    for i in range(4):
        at=quarter[i]
        attend(4,at)
        inv=1.0/k.l[at,:]
        o=k.att[at,:]*inv
        k.att[at,:]=o
        k.fac[at,:]=jnp.exp2(k.fac[at,:]-k.m[at,:])*inv
        k.mixed[at,:]=o.astype(bf16)
    for i in range(1,4):
        moved.append(go(k.mixed.at[block_of(head^i,part)],k.heads.at[:,lanes],head^i,node))
    k.heads[:,lanes]=k.mixed[mine,:]
    for c in across: c.wait_send()
    wait_all(to_x+to_y)
    from_x=column(2); from_y=column(4)
    cross=[go(from_x[0],from_x[0],head,node^4)]+[go(r,r,head,node^2) for r in from_y[1:]]
    hand=[go(r,r,head,node^1) for r in from_x+from_y]
    wait_all(cross)
    last=[go(r,r,head,node^1) for r in column(6)]
    scale_two=1.0+by_batch(own_pos,limits,k.modulation,4,slice(0,512))
    shift_two=by_batch(own_pos,limits,k.modulation,4,slice(512,1024))
    g=cotangent[mine,:]
    wait_all(moved)
    wait_all(to_pair+hand+last)

    out_all=k.out_full[...].reshape(512,512)
    y=node_input[mine,:].astype(f32)+jnp.dot(k.heads[...],out_all,preferred_element_type=f32)
    n_two,inv_two=norm_parts(y)
    xn=(n_two*scale_two+shift_two).astype(bf16)
    mlp=jnp.zeros((part,512),f32); dxn=jnp.zeros((part,512),f32)
    for j in range(4):
        s=slice(j*512,(j+1)*512)
        h=jnp.dot(xn,k.up_full[:,s],preferred_element_type=f32)
        gate=1.0/(1.0+jnp.exp(-h))
        u=(h*gate).astype(bf16)
        k.act[:,s]=u
        mlp+=jnp.dot(u,k.down_full[j],preferred_element_type=f32)
        du=lax.dot_general(g,k.down_full[j],NT,preferred_element_type=f32)
        d=(du*gate*(1.0+h*(1.0-gate))).astype(bf16)
        k.pre[:,s]=d
        dxn+=lax.dot_general(d,k.up_full[:,s],NT,preferred_element_type=f32)
    dyv=g.astype(f32)+norm_back(dxn*scale_two,n_two,inv_two)
    k.dy[...]=dyv
    da=dyv.astype(bf16)
    k.do_rows[...]=lax.dot_general(da,out_all,NT,preferred_element_type=f32).astype(bf16)
    returned=[]
    for i in range(1,4):
        returned.append(go(k.do_rows.at[:,block_of(head^i,128)],k.do.at[mine],head^i,node))
    k.do[mine,:]=k.do_rows[:,lanes]
    node_output[mine,:]=(y+mlp).astype(bf16)
    xn_t=xn.T
    heads_t=k.heads[...].T
    k.out_grad[...]=jnp.dot(heads_t,da,preferred_element_type=f32).astype(bf16).reshape(4,4,2,16,512)
    for j in range(4):
        s=slice(j*512,(j+1)*512)
        k.up_grad[:,:,:,s]=jnp.dot(xn_t,k.pre[:,s],preferred_element_type=f32).astype(bf16).reshape(4,2,64,512)
        k.down_grad[j]=jnp.dot(k.act[:,s].T,g,preferred_element_type=f32).astype(bf16).reshape(4,2,64,512)
    stage1=[go(k.up_grad.at[:,1-core],k.up1,head,node^1),go(k.down_grad.at[:,:,1-core],k.down1,head,node^1),go(k.out_grad.at[:,:,1-core],k.out1,head,node^1)]
    k.dm_own[4:8,0:512]=batch_sums(own_pos,limits,dxn*n_two)
    k.dm_own[4:8,512:1024]=batch_sums(own_pos,limits,dxn)
    wait_all(returned)
    shown=Shown(links,head,node,lambda h: node_output.at[block_of(h,part)])

    q_t=k.queries[...].T
    dof=k.do[...].astype(f32)
    delta=jnp.sum(dof*k.att[...],axis=1,keepdims=True)
    def block(b):
        def write(r,s,v):
            if b==0: k.dkv[r,s]=v
            else: k.near[b,r,s]=v.astype(bf16)
        back_block(b,q_t,dof,k.fac,delta,k.table,k.e,k.dq,write,b==4,512,scale)
    near=k.near
    block(4)
    give=go(near.at[4],k.got_pair,head,node^1)
    block(3)
    give.wait()
    @pl.when(x_at!=core)
    def _(): near[3]=summed(near[3],k.got_pair[...]).astype(bf16)
    via_y=[go(near.at[3,:,s],k.got_y.at[:,s],head,node^4) for s in quarter]
    block(2)
    @pl.when(x_at==core)
    def _(): near[2]=summed(near[2],k.got_pair[...]).astype(bf16)
    via_x=[]
    def pass_on(i):
        s=quarter[i]
        via_y[i].wait()
        near[2,:,s]=summed(near[2,:,s],k.got_y[:,s]).astype(bf16)
        via_x.append(go(near.at[2,:,s],k.got_x.at[:,s],head,node^2))
    pass_on(0)
    shown.onward()
    block(1)
    one=go(near.at[1],k.got_one,head,node^1)
    pass_on(1)
    pass_on(2)
    block(0)
    pass_on(3)
    wait_all(stage1)
    for i in range(4):
        k.up1[i]=summed(k.up1[i],k.up_grad[i,core]).astype(bf16)
        k.down1[i]=summed(k.down1[i],k.down_grad[i,:,core]).astype(bf16)
        k.out1[i]=summed(k.out1[i],k.out_grad[i,:,core]).astype(bf16)
    stage2=[go(k.up1.at[i*2+1-x_at],k.up2.at[i],head,node^2) for i in range(2)]
    there=pl.ds((1-y_at)*2,2)
    stage2+=[go(k.down1.at[:,there],k.down2,head,node^4),go(k.out1.at[:,there],k.out2,head,node^4)]
    xn_t=k.xn_one[...].T
    one.wait()
    for i in range(4):
        s=quarter[i]
        via_x[i].wait()
        total=k.dkv[:,s]+k.got_one[:,s].astype(f32)+k.got_x[:,s].astype(f32)
        k.proj_grad[s,128:]=total.T.astype(bf16)
        k.proj_grad[s,:128]=(k.dq[s,:]*scale).astype(bf16)
        k.partial[i]=lax.dot_general(k.proj_grad[s,:],k.qkv_full[...],NT,preferred_element_type=f32).astype(bf16)
    reduce=Added(links,head,node,lambda h: k.partial.at[h],lambda i: k.got_partial.at[i],k.relay)
    k.qkv_grad[...]=jnp.dot(xn_t,k.proj_grad[...],preferred_element_type=f32).astype(bf16).reshape(8,64,384)
    qkv_moves=[go(k.qkv_grad.at[node^i],k.qkv_got.at[i-1],head,node^i) for i in range(1,8)]
    reduce.onward()
    wait_all(stage2)
    for i in range(2):
        k.up2[i]=summed(k.up2[i],k.up1[i*2+x_at]).astype(bf16)
    here=pl.ds(y_at*2,2)
    k.down2[...]=summed(k.down2[...],k.down1[:,here]).astype(bf16)
    k.out2[...]=summed(k.out2[...],k.out1[:,here]).astype(bf16)
    stage3=[go(k.up2.at[1-y_at],k.up3,head,node^4),go(k.down2.at[:,1-x_at],k.down3,head,node^2),go(k.out2.at[:,1-x_at],k.out3,head,node^2)]
    scale_one=1.0+by_batch(own_pos,limits,k.modulation,0,slice(0,512))
    n_one,inv_one=norm_parts(node_input[mine,:].astype(f32))
    wait_all(qkv_moves)
    qkv_sum[...]=summed(k.qkv_grad[node],*[k.qkv_got[i] for i in range(7)])
    wait_all(stage3)
    k.up3[...]=summed(k.up3[...],k.up2[y_at]).astype(bf16)
    k.down3[...]=summed(k.down3[...],k.down2[:,x_at]).astype(bf16)
    k.out3[...]=summed(k.out3[...],k.out2[:,x_at]).astype(bf16)
    stage4=[Added(links,head,node,lambda h: k.up3.at[:,block_of(h,512)],lambda i: k.up_z.at[i],k.up_relay),
        Added(links,head,node,lambda h: k.down3.at[h],lambda i: k.down_z.at[i],k.down_relay),
        Added(links,head,node,lambda h: k.out3.at[h],lambda i: k.out_z.at[i],k.out_relay)]
    reduce.wait()
    dxn=summed(k.partial.at[head],*[k.got_partial.at[i] for i in range(3)])
    k.dm_own[0:4,0:512]=batch_sums(own_pos,limits,dxn*n_one)
    k.dm_own[0:4,512:1024]=batch_sums(own_pos,limits,dxn)
    dm_moves=[go(k.dm_own,k.dm_z.at[head],head^i,node) for i in range(1,4)]
    row_all[head,:,:]=(k.dy[...]+norm_back(dxn*scale_one,n_one,inv_one)).astype(bf16)
    spread=Shown(links,head,node,lambda h: row_all.at[h])
    for s in stage4: s.onward()
    k.dm_z[head,:,:]=k.dm_own[...]
    wait_all(dm_moves)
    k.modp[...]=k.dm_z[0]+k.dm_z[1]+k.dm_z[2]+k.dm_z[3]
    dm_last=[go(k.modp,k.dm_n.at[node],head,node^i) for i in range(1,8)]
    k.dm_n[node,:,:]=k.modp[...]
    spread.onward()
    wait_all(dm_last)
    total=k.dm_n[0]
    for i in range(1,8): total=total+k.dm_n[i]
    mod_sum[...]=total
    wait_all(stage4)
    up_sum[...]=summed(k.up3[:,head_cols],*[k.up_z[i] for i in range(3)])
    down_sum[...]=summed(k.down3[head],*[k.down_z[i] for i in range(3)])
    out_sum[...]=summed(k.out3[head],*[k.out_z[i] for i in range(3)])
    spread.wait()
    shown.wait()


def finish_kernel(sigma, step_count, *refs):
    sources=refs[:22]; results=refs[22:39]; held=refs[39:62]; load,store=refs[62:]
    loads=[pltpu.make_async_copy(sources[i],held[i],load.at[i]) for i in range(22)]
    for i in (0,1)+tuple(range(7,22))+tuple(range(2,7)): loads[i].start()
    node=lax.axis_index("node")
    stores=[]
    def keep(ref, result):
        stores.append(pltpu.make_async_copy(ref,results[result],store.at[result])); stores[-1].start()
    loads[0].wait()
    keep(held[0],0)
    loads[1].wait()
    wide=held[22]
    rows=wide.shape[0]
    for i in range(4): wide[i*rows//4:(i+1)*rows//4,:]=held[1][i].astype(f32)
    keep(wide,1)
    count=jnp.full((8,128),step_count[0],jnp.int32).astype(f32)
    correct=(1.0-jnp.exp2(-count))[0:1,0:1]
    sig=sigma[:,0:64]
    for i in range(1,8): sig=jnp.where(node==i,sigma[:,i*64:(i+1)*64],sig)
    rates=((4*COND)**-0.5,(WIDTH//2)**-0.5,(WIDTH//4)**-0.5,WIDTH**-0.5,HIDDEN_SIZE**-0.5)
    for w in (0,3,4,1,2):
        at=7+3*w
        for i in range(3): loads[at+i].wait()
        if w==0:
            loads[6].wait()
            total=held[6]
            batch_grad=jnp.concatenate([total[0:4,:],total[4:8,:]],axis=1)
            grad=lax.dot_general(sig.astype(f32),batch_grad,(((0,),(0,)),((),())),precision=highest,preferred_element_type=f32)
        else:
            loads[1+w].wait()
            grad=held[1+w][...]
        master,first,second=held[at:at+3]
        first_new=beta_rate*first[...]+(1.0-beta_rate)*grad
        second_new=beta_rate*second[...]+(1.0-beta_rate)*grad*grad
        step=first_new/correct/(jnp.sqrt(second_new/correct)+adam_eps)
        old=master[...]
        master[...]=old-rates[w]*(step+weight_decay*old)
        first[...]=first_new
        second[...]=second_new
        for i in range(3): keep(held[at+i],2+3*w+i)
    for c in stores: c.wait()


def slots(neighbours, valid, node, rows):
    which=(neighbours//rows)^node
    slot=jnp.where(which==6,3,jnp.where((which==3)|(which==7),4,which))
    local=neighbours%rows
    spot=lax.broadcasted_iota(jnp.int32,neighbours.shape,0)%16
    hi=(slot*(rows//SPAN)+local//SPAN)*16+spot
    return jnp.where(valid>0,hi*256+local%SPAN,-1).reshape(-1,256)


def per_device_near(
    node_input, cotangent, sigma_embed, neighbours, neighbour_valid, batch_counts, step_count,
    ada_master, ada_first, ada_second, qkv_master, qkv_first, qkv_second, out_master, out_first, out_second,
    up_master, up_first, up_second, down_master, down_first, down_second,
):
    rows=node_input.shape[0]
    code=slots(neighbours,neighbour_valid,lax.axis_index("node"),rows)
    masters=(ada_master,qkv_master,out_master,up_master,down_master)
    firsts=(ada_first,qkv_first,out_first,up_first,down_first)
    seconds=(ada_second,qkv_second,out_second,up_second,down_second)
    V=pltpu.VMEM
    full=pl.BlockSpec(memory_space=V); few=pl.BlockSpec(memory_space=pltpu.SMEM); hbm=pl.BlockSpec(memory_space=pltpu.HBM)
    S=jax.ShapeDtypeStruct
    held=scratch(rows)
    sums=pl.pallas_call(functools.partial(layer_kernel,128**-0.5,tuple(held)),
        out_shape=(S((rows,512),bf16),S((4,rows//4,512),bf16))+tuple(S(a.shape,f32) for a in masters[1:])+(S((8,1024),f32),),
        in_specs=[full]*4+[few]+[full]*5,
        out_specs=(full,)*7,
        scratch_shapes=[V(*v) for v in held.values()]+[pltpu.SemaphoreType.DMA((COPIES,))]*2,
        compiler_params=pltpu.CompilerParams(vmem_limit_bytes=67043328,collective_id=1,has_side_effects=True),
        name="layer")(node_input,cotangent,sigma_embed,code,batch_counts,*masters)
    news=tuple(S(a.shape,f32) for a in masters for _ in range(3))
    inner=[V(a.shape,a.dtype) for a in sums]+[V(a.shape,f32) for a in masters for _ in range(3)]+[V((rows,512),f32)]
    return pl.pallas_call(finish_kernel,
        out_shape=(S((rows,512),bf16),S((rows,512),f32))+news,
        in_specs=[full,few]+[hbm]*(7+15),
        out_specs=(hbm,)*17,
        scratch_shapes=inner+[pltpu.SemaphoreType.DMA((22,)),pltpu.SemaphoreType.DMA((17,))],
        compiler_params=pltpu.CompilerParams(vmem_limit_bytes=67043328),
        name="finish")(sigma_embed,step_count,*sums,*[a for three in zip(masters,firsts,seconds) for a in three])


def wide_count_groups(cnt, hik, lok, rows):
    steps=hik.shape[0]
    parts=rows//SPAN
    total=5*parts*16
    rowid=lax.broadcasted_iota(jnp.int32,(total,1),0)
    rowkey=lax.div(rowid,16)*16+lax.rem(rowid,16)
    spot=lax.broadcasted_iota(jnp.int32,(SPAN,1),0)
    def body(g,_):
        keys=hik[pl.ds(g,1),:]
        low=lok[pl.ds(g,1),:]
        left=jnp.where(rowkey==keys,1.0,0.0).astype(bf16)
        right=jnp.where(spot==low,1.0,0.0).astype(bf16)
        made=lax.dot_general(left,right,NT,preferred_element_type=f32).astype(bf16)
        at=pl.multiple_of(g*16,16)
        for b in range(5):
            for p in range(parts):
                r=(b*parts+p)*16
                cnt[b,pl.ds(at,16),p*SPAN:(p+1)*SPAN]=made[r:r+16,:]
        return 0
    lax.fori_loop(0,steps,body,0)

def wide_add_self(cnt, block, rows):
    eye=(lax.broadcasted_iota(jnp.int32,(SPAN,SPAN),0)==lax.broadcasted_iota(jnp.int32,(SPAN,SPAN),1))
    one=jnp.where(eye,1.0,0.0).astype(bf16)
    for p in range(rows//SPAN):
        s=slice(p*SPAN,(p+1)*SPAN)
        cnt[block,s,s]=cnt[block,s,s]+one

def wide_attend_block(b, first, q, keys, vals, cnt, e, m, l, acc, fac, chunk, scale):
    rows=q.shape[0]
    lane=lax.broadcasted_iota(jnp.int32,(chunk,128),1)
    def body(i,_):
        at=pl.ds(pl.multiple_of(i*chunk,chunk),chunk)
        s=lax.dot_general(q[at,:],keys,NT,preferred_element_type=f32)*scale
        c=cnt[b,at,:].astype(f32)
        s=jnp.where(c>0,s,-1e30)
        top=jnp.max(s,axis=1,keepdims=True)
        if not first:
            old=m[at,0:1]
            top=jnp.maximum(top,old)
        w=(jnp.exp2(s-top)*c)
        total=jnp.sum(w,axis=1,keepdims=True)
        w=w.astype(bf16)
        e[b,at,:]=w
        out=jnp.dot(w,vals,preferred_element_type=f32)
        if first:
            acc[at,:]=out; l[at,:]=jnp.broadcast_to(total,(chunk,128))
            fac[at,:]=jnp.where(lane==b,top,0.0)
        else:
            shrink=jnp.exp2(old-top)
            acc[at,:]=acc[at,:]*shrink+out
            l[at,:]=l[at,:]*shrink+total
            fac[at,:]=jnp.where(lane==b,top,fac[at,:])
        m[at,:]=jnp.broadcast_to(top,(chunk,128))
        return 0
    lax.fori_loop(0,rows//chunk,body,0)

def wide_fwd_kernel(order, self_block, scale, q, kv, hik, lok, att, e, fac, cnt, m, l):
    rows=q.shape[0]
    wide_count_groups(cnt,hik,lok,rows)
    wide_add_self(cnt,self_block,rows)
    for t,b in enumerate(order):
        wide_attend_block(b,t==0,q,kv[b,:,:128],kv[b,:,128:],cnt,e,m,l,att,fac,256,scale)
    inv=1.0/l[...]
    att[...]=att[...]*inv
    fac[...]=jnp.exp2(fac[...]-m[...])*inv

def wide_attention_fwd(q,kv,hik,lok,scale):
    rows=q.shape[0]
    V=pltpu.VMEM
    full=pl.BlockSpec(memory_space=V)
    return pl.pallas_call(functools.partial(wide_fwd_kernel,(2,1,3,0,4),2,scale*math.log2(math.e)),
        out_shape=(jax.ShapeDtypeStruct((rows,128),f32),jax.ShapeDtypeStruct((5,rows,rows),bf16),jax.ShapeDtypeStruct((rows,128),f32)),
        in_specs=[full]*4,out_specs=(full,)*3,
        scratch_shapes=[V((5,rows,rows),bf16),V((rows,128),f32),V((rows,128),f32)],
        compiler_params=pltpu.CompilerParams(vmem_limit_bytes=60<<20),name="attend_fwd")(q,kv,hik,lok)

def wide_back_block(b, q_t, do, fac, delta, kv, e, dq, dkv, first, chunk, keyscale):
    rows=do.shape[0]
    f=fac[:,b:b+1]
    dob=(do*f)
    dobh=dob.astype(bf16)
    d=-(delta*f)
    h=d.astype(bf16); r=d-h.astype(f32); h2=r.astype(bf16); h3=(r-h2.astype(f32)).astype(bf16)
    lane=lax.broadcasted_iota(jnp.int32,(rows,128),1)
    zero=jnp.zeros((rows,128),bf16)
    dcol=jnp.where(lane==0,h.astype(f32),jnp.where(lane==1,h2.astype(f32),jnp.where(lane==2,h3.astype(f32),0.0))).astype(bf16)
    left=jnp.concatenate([dobh,dcol],axis=1)
    dob_t=dobh.T
    ones=jnp.ones((chunk,128),bf16)
    for i in range(kv.shape[1]//chunk):
        s=slice(i*chunk,(i+1)*chunk)
        right=jnp.concatenate([kv[b,s,128:],ones],axis=1)
        dp=lax.dot_general(left,right,NT,preferred_element_type=f32)
        w=e[b,:,s]
        ds=(dp*w.astype(f32)).astype(bf16)
        dkv[b,:128,s]=jnp.dot(q_t,ds,preferred_element_type=f32)*keyscale
        dkv[b,128:,s]=jnp.dot(dob_t,w,preferred_element_type=f32)
        out=jnp.dot(ds,kv[b,s,:128],preferred_element_type=f32)
        if first and i==0: dq[...]=out
        else: dq[...]+=out

def wide_bwd_kernel(scale, q, do, att, fac, kv, e, dq, dkv, ):
    q_t=q[...].T
    dof=do[...].astype(f32)
    delta=jnp.sum(dof*att[...],axis=1,keepdims=True)
    for t,b in enumerate((0,4,1,3,2)):
        wide_back_block(b,q_t,dof,fac,delta,kv,e,dq,dkv,t==0,512,scale)
    dq[...]=dq[...]*scale

def wide_attention_bwd(q,do,att,fac,kv,e,scale):
    rows=q.shape[0]
    V=pltpu.VMEM
    full=pl.BlockSpec(memory_space=V)
    return pl.pallas_call(functools.partial(wide_bwd_kernel,scale),
        out_shape=(jax.ShapeDtypeStruct((rows,128),f32),jax.ShapeDtypeStruct((5,256,rows),f32)),
        in_specs=[full]*6,out_specs=(full,)*2,
        compiler_params=pltpu.CompilerParams(vmem_limit_bytes=60<<20),name="attend_bwd")(q,do,att,fac,kv,e)

def wide_tables(slot_index, valid, rows):
    parts=rows//SPAN
    flat=slot_index.reshape(-1,256)
    ok=(valid>0).reshape(-1,256)
    node=lax.broadcasted_iota(jnp.int32,flat.shape,1)//16
    hi=jnp.where(ok,(flat//SPAN)*16+node,-1)
    lo=flat%SPAN
    return hi,lo


def per_device(
    node_input,
    cotangent,
    sigma_embed,
    neighbours,
    neighbour_valid,
    batch_counts,
    step_count,
    ada_master,
    ada_first,
    ada_second,
    qkv_master,
    qkv_first,
    qkv_second,
    out_master,
    out_first,
    out_second,
    up_master,
    up_first,
    up_second,
    down_master,
    down_first,
    down_second,
):
    f32 = jnp.float32
    bf16 = jnp.bfloat16
    node_rows = node_input.shape[0]
    model_width = node_input.shape[1]
    head_dim = qkv_master.shape[1] // 3
    score_scale = head_dim ** (-0.5)
    node_index = lax.axis_index("node")
    total_nodes = node_rows * lax.axis_size("node")
    qkv_full, out_full, up_full, down_full = (
        lax.all_gather(qkv_master.astype(bf16), "node", axis=0, tiled=True),
        lax.all_gather(out_master.astype(bf16), "node", axis=0, tiled=True),
        lax.all_gather(up_master.astype(bf16), "node", axis=0, tiled=True),
        lax.all_gather(down_master.astype(bf16), "node", axis=0, tiled=True),
    )
    cond_rows = ada_master.shape[0]
    sigma_part = lax.dynamic_slice_in_dim(sigma_embed, node_index * cond_rows, cond_rows, 1)
    limits = jnp.cumsum(batch_counts)[:-1]
    positions = node_index * node_rows + jnp.arange(node_rows, dtype=jnp.int32)
    member = jnp.sum((positions[:, None] >= limits[None, :]).astype(jnp.int32), axis=1)
    onehot = (
        member[:, None] == jnp.arange(batch_counts.shape[0], dtype=jnp.int32)[None, :]
    ).astype(f32)
    modulation = lax.psum(
        jnp.dot(sigma_part, ada_master.astype(bf16), preferred_element_type=f32), "node"
    )
    per_node = jnp.dot(onehot, modulation, precision=highest)
    scale_one = per_node[:, :model_width]
    shift_one = per_node[:, model_width : 2 * model_width]
    scale_two = per_node[:, 2 * model_width : 3 * model_width]
    shift_two = per_node[:, 3 * model_width :]
    normed_one, inverse_one = norm_parts(node_input.astype(f32))
    xn_one = (normed_one * (1.0 + scale_one) + shift_one).astype(bf16)
    projected = jnp.dot(xn_one, qkv_full, preferred_element_type=f32).astype(bf16)
    queries = projected[:, :head_dim]
    keys_values = projected[:, head_dim:]
    offsets = (-2, -1, 1, 2)
    fetched = {0: keys_values}
    for offset in offsets:
        fetched[offset] = passed_along(keys_values, "node", -offset)
    table = jnp.stack([fetched[offset] for offset in (-2, -1, 0, 1, 2)], axis=0)
    slot_index = jnp.mod(neighbours - (node_index - 2) * node_rows, total_nodes)
    high_keys, low_keys = wide_tables(slot_index, neighbour_valid, node_rows)
    mixed, weights, factors = wide_attention_fwd(queries, table, high_keys, low_keys, score_scale)
    heads_out = mixed.astype(bf16)
    branch = lax.psum(
        jnp.dot(heads_out, out_full, preferred_element_type=f32).astype(jnp.bfloat16), "head"
    ).astype(jnp.float32)
    middle = node_input.astype(f32) + branch
    normed_two, inverse_two = norm_parts(middle)
    xn_two = (normed_two * (1.0 + scale_two) + shift_two).astype(bf16)
    hidden_pre = jnp.dot(xn_two, up_full, preferred_element_type=f32)
    gate_sig = jax.nn.sigmoid(hidden_pre)
    activated = (hidden_pre * gate_sig).astype(bf16)
    mlp_sum = lax.psum(
        jnp.dot(activated, down_full, preferred_element_type=f32).astype(jnp.bfloat16), "head"
    ).astype(jnp.float32)
    node_output = (middle + mlp_sum).astype(bf16)
    down_grad = jnp.einsum("nf,nd->fd", activated, cotangent, preferred_element_type=f32)
    act_grad = jnp.einsum("nd,fd->nf", cotangent, down_full, preferred_element_type=f32)
    pre_grad = (act_grad * gate_sig * (1.0 + hidden_pre * (1.0 - gate_sig))).astype(bf16)
    up_grad = jnp.einsum("nw,nf->wf", xn_two, pre_grad, preferred_element_type=f32)
    normed_two_grad = lax.psum(
        jnp.einsum("nf,wf->nw", pre_grad, up_full, preferred_element_type=f32).astype(jnp.bfloat16),
        "head",
    ).astype(jnp.float32)
    middle_grad = cotangent.astype(f32) + norm_back(
        normed_two_grad * (1.0 + scale_two), normed_two, inverse_two
    )
    branch_grad = middle_grad.astype(bf16)
    out_grad = jnp.einsum("nh,nd->hd", heads_out, branch_grad, preferred_element_type=f32)
    mixed_grad = jnp.einsum("nd,hd->nh", branch_grad, out_full, preferred_element_type=f32).astype(
        bf16
    )
    query_grad, pair_sums = wide_attention_bwd(
        queries, mixed_grad, mixed, factors, table, weights, score_scale
    )
    remote_terms = pair_sums[2]
    for offset in offsets:
        remote_terms = remote_terms + passed_along(
            pair_sums[offset + 2].astype(bf16), "node", offset
        ).astype(f32)
    key_value_grad = remote_terms.T
    projected_grad = jnp.concatenate([query_grad, key_value_grad], axis=1).astype(bf16)
    qkv_grad = jnp.einsum("nw,nc->wc", xn_one, projected_grad, preferred_element_type=f32)
    normed_one_grad = lax.psum(
        jnp.einsum("nc,wc->nw", projected_grad, qkv_full, preferred_element_type=f32).astype(
            jnp.bfloat16
        ),
        "head",
    ).astype(jnp.float32)
    input_grad = middle_grad + norm_back(
        normed_one_grad * (1.0 + scale_one), normed_one, inverse_one
    )
    rows_grad = jnp.concatenate(
        [
            normed_one_grad * normed_one,
            normed_one_grad,
            normed_two_grad * normed_two,
            normed_two_grad,
        ],
        axis=1,
    )
    batch_grad = jnp.dot(onehot.T, rows_grad, precision=highest)
    batch_grad = lax.psum(batch_grad, "node")
    ada_sum = jnp.dot(sigma_part.astype(f32).T, batch_grad, precision=highest)
    qkv_sum, out_sum, up_sum, down_sum = (
        lax.psum_scatter(qkv_grad, "node", scatter_dimension=0, tiled=True),
        lax.psum_scatter(out_grad, "node", scatter_dimension=0, tiled=True),
        lax.psum_scatter(up_grad, "node", scatter_dimension=0, tiled=True),
        lax.psum_scatter(down_grad, "node", scatter_dimension=0, tiled=True),
    )
    count_value = step_count[0].astype(f32)
    ada_res = adamw_update(
        ada_master, ada_first, ada_second, ada_sum, (4 * COND) ** (-0.5), count_value
    )
    qkv_res = adamw_update(
        qkv_master, qkv_first, qkv_second, qkv_sum, (WIDTH // 2) ** (-0.5), count_value
    )
    out_res = adamw_update(
        out_master, out_first, out_second, out_sum, (WIDTH // 4) ** (-0.5), count_value
    )
    up_res = adamw_update(up_master, up_first, up_second, up_sum, WIDTH ** (-0.5), count_value)
    down_res = adamw_update(
        down_master, down_first, down_second, down_sum, HIDDEN_SIZE ** (-0.5), count_value
    )
    return (
        node_output,
        input_grad,
        ada_res[0],
        ada_res[1],
        ada_res[2],
        qkv_res[0],
        qkv_res[1],
        qkv_res[2],
        out_res[0],
        out_res[1],
        out_res[2],
        up_res[0],
        up_res[1],
        up_res[2],
        down_res[0],
        down_res[1],
        down_res[2],
    )


def solution(mesh):
    chosen = per_device_near if mesh.shape["node"] == 8 and mesh.shape["head"] == 4 else per_device
    placed = (
        P("node", None),
        P("node", None),
        P(),
        P("node", None),
        P("node", None),
        P(),
        P(),
        P("node", None),
        P("node", None),
        P("node", None),
        P("node", "head"),
        P("node", "head"),
        P("node", "head"),
        P(("head", "node"), None),
        P(("head", "node"), None),
        P(("head", "node"), None),
        P("node", "head"),
        P("node", "head"),
        P("node", "head"),
        P(("head", "node"), None),
        P(("head", "node"), None),
        P(("head", "node"), None),
    )
    return jax.shard_map(
        chosen,
        mesh=mesh,
        in_specs=placed,
        out_specs=(
            P("node", None),
            P("node", None),
            P("node", None),
            P("node", None),
            P("node", None),
            P("node", "head"),
            P("node", "head"),
            P("node", "head"),
            P(("head", "node"), None),
            P(("head", "node"), None),
            P(("head", "node"), None),
            P("node", "head"),
            P("node", "head"),
            P("node", "head"),
            P(("head", "node"), None),
            P(("head", "node"), None),
            P(("head", "node"), None),
        ),
        check_vma=False,
    )
```

```python
import functools
import math

import jax
import jax.numpy as jnp
from jax import lax
from jax.experimental import pallas as pl
from jax.experimental.pallas import tpu as pltpu
from jax.sharding import PartitionSpec as P


WIDTH = 512
HIDDEN_SIZE = 2048
COND = 512


norm_eps = 1e-06
beta_rate = 0.5
adam_eps = 1e-08
weight_decay = 0.1
highest = lax.Precision.HIGHEST


def passed_along(block, axis, distance):
    devices = range(lax.axis_size(axis))
    route = [((i - distance) % len(devices), i) for i in devices]
    return lax.ppermute(block, axis, route)


def norm_parts(values):
    centred = values - jnp.mean(values, axis=1, keepdims=True)
    inverse = lax.rsqrt(jnp.mean(centred * centred, axis=1, keepdims=True) + norm_eps)
    return (centred * inverse, inverse)


def norm_back(grad_normed, normed, inverse):
    first_mean = jnp.mean(grad_normed, axis=1, keepdims=True)
    second_mean = jnp.mean(grad_normed * normed, axis=1, keepdims=True)
    return inverse * (grad_normed - first_mean - normed * second_mean)


def adamw_update(master, first, second, grad, rate, count_value):
    first_new = beta_rate * first + (1.0 - beta_rate) * grad
    second_new = beta_rate * second + (1.0 - beta_rate) * grad * grad
    correct = 1.0 - jnp.power(jnp.float32(beta_rate), count_value)
    normed_step = first_new / correct / (jnp.sqrt(second_new / correct) + adam_eps)
    master_new = master - rate * (normed_step + weight_decay * master)
    return (master_new, first_new, second_new)


f32=jnp.float32; bf16=jnp.bfloat16
NT=(((1,),(1,)),((),()))
SPAN=256

def count_groups(cnt, code, rows, start, stop, step):
    parts=rows//SPAN
    total=5*parts*16
    short=jnp.int16
    rowid=lax.broadcasted_iota(jnp.int32,(total,SPAN),0).astype(short)
    spot=lax.broadcasted_iota(jnp.int32,(SPAN,SPAN),0).astype(short)
    one=bf16(1); zero=bf16(0)
    def group(g):
        both=code[pl.ds(g,1),:]
        keys=lax.shift_right_arithmetic(both,8).astype(short)
        low=lax.bitwise_and(both,255).astype(short)
        left=jnp.where(rowid==jnp.broadcast_to(keys,(total,SPAN)),one,zero)
        right=jnp.where(spot==jnp.broadcast_to(low,(SPAN,SPAN)),one,zero)
        made=lax.dot_general(left,right,NT,preferred_element_type=f32).astype(bf16)
        at=pl.multiple_of(g*16,16)
        for b in range(5):
            for p in range(parts):
                r=(b*parts+p)*16
                cnt[b,pl.ds(at,16),p*SPAN:(p+1)*SPAN]=made[r:r+16,:]
    def body(g,_):
        for u in range(step): group(g*step+u)
        return 0
    lax.fori_loop(start//step,stop//step,body,0)

def add_self(cnt, block, rows):
    eye=(lax.broadcasted_iota(jnp.int32,(SPAN,SPAN),0)==lax.broadcasted_iota(jnp.int32,(SPAN,SPAN),1))
    one=jnp.where(eye,1.0,0.0).astype(bf16)
    for p in range(rows//SPAN):
        s=slice(p*SPAN,(p+1)*SPAN)
        cnt[block,s,s]=cnt[block,s,s]+one

def attend_rows(b, first, at, size, q, table, e, m, l, acc, fac, scale):
    lane=lax.broadcasted_iota(jnp.int32,(size,128),1)
    s=lax.dot_general(q[at,:],table[b,:,0:128],NT,preferred_element_type=f32)*scale
    c=e[b,at,:].astype(f32)
    s=jnp.where(c>0,s,-1e30)
    top=jnp.max(s,axis=1,keepdims=True)
    if not first:
        old=m[at,0:1]
        top=jnp.maximum(top,old)
    w=(jnp.exp2(s-top)*c).astype(bf16)
    e[b,at,:]=w
    out=jnp.dot(w,table[b,:,128:384],preferred_element_type=f32)
    if first:
        acc[at,:]=out[:,:128]; l[at,:]=out[:,128:]
        fac[at,:]=jnp.where(lane==b,top,0.0)
    else:
        shrink=jnp.exp2(old-top)
        acc[at,:]=acc[at,:]*shrink+out[:,:128]
        l[at,:]=l[at,:]*shrink+out[:,128:]
        fac[at,:]=jnp.where(lane==b,top,fac[at,:])
    m[at,:]=jnp.broadcast_to(top,(size,128))

def back_block(b, q_t, dof, fac, delta, table, e, dq, write, first, chunk, keyscale):
    rows=dof.shape[0]
    f=fac[:,b:b+1]
    dobh=(dof*f).astype(bf16)
    d=-(delta*f)
    h=d.astype(bf16); r=d-h.astype(f32); h2=r.astype(bf16); h3=(r-h2.astype(f32)).astype(bf16)
    lane=lax.broadcasted_iota(jnp.int32,(rows,128),1)
    dcol=jnp.where(lane==0,h.astype(f32),jnp.where(lane==1,h2.astype(f32),jnp.where(lane==2,h3.astype(f32),0.0))).astype(bf16)
    left=jnp.concatenate([dobh,dcol],axis=1)
    dob_t=dobh.T
    for i in range(rows//chunk):
        s=slice(i*chunk,(i+1)*chunk)
        dp=lax.dot_general(left,table[b,s,128:384],NT,preferred_element_type=f32)
        w=e[b,:,s]
        ds=(dp*w.astype(f32)).astype(bf16)
        write(slice(0,128),s,jnp.dot(q_t,ds,preferred_element_type=f32)*keyscale)
        write(slice(128,256),s,jnp.dot(dob_t,w,preferred_element_type=f32))
        out=jnp.dot(ds,table[b,s,0:128],preferred_element_type=f32)
        if first and i==0: dq[...]=out
        else: dq[...]+=out


def by_batch(pos, limits, table, row, lanes):
    pick=[table[row+b:row+b+1,lanes] for b in range(4)]
    out=jnp.where(pos>=limits[0],pick[1],pick[0])
    out=jnp.where(pos>=limits[1],pick[2],out)
    return jnp.where(pos>=limits[2],pick[3],out)


def batch_sums(pos, limits, values):
    lane=lax.broadcasted_iota(jnp.int32,(pos.shape[0],8),1)
    member=(pos>=limits[0]).astype(jnp.int32)+(pos>=limits[1]).astype(jnp.int32)+(pos>=limits[2]).astype(jnp.int32)
    onehot=jnp.where(lane==member,1.0,0.0).astype(f32)
    return lax.dot_general(onehot,values,(((0,),(0,)),((),())),precision=highest,preferred_element_type=f32)[0:4,:]


class Links:
    def __init__(self, send, recv):
        self.send, self.recv, self.used = send, recv, 0

    def copy(self, src, dst, head, node):
        made=pltpu.make_async_remote_copy(src_ref=src,dst_ref=dst,send_sem=self.send.at[self.used],recv_sem=self.recv.at[self.used],
            device_id=(head,node),device_id_type=pl.DeviceIdType.MESH)
        self.used+=1
        return made

    def go(self, src, dst, head, node):
        made=self.copy(src,dst,head,node)
        made.start()
        return made


def meet(peers):
    barrier=pltpu.get_barrier_semaphore()
    for head,node in peers:
        pl.semaphore_signal(barrier,inc=1,device_id=(head,node),device_id_type=pl.DeviceIdType.MESH)
    pl.semaphore_wait(barrier,len(peers))


class Shown:
    def __init__(self, links, head, node, place):
        self.end=(head==0)|(head==3)
        own=place(head)
        self.two=links.go(own,own,head^2,node)
        self.one=links.go(own,own,head^1,node)
        self.three=links.copy(own,own,head^3,node)
        pl.when(~self.end)(self.three.start)
        far=place(jnp.where(self.end,head^3,head^2))
        self.pass_copy=links.copy(far,far,head^1,node)

    def onward(self):
        @pl.when(~self.end)
        def _():
            self.two.wait_recv()
            self.pass_copy.start()

    def wait(self):
        self.one.wait()
        self.two.wait_send()
        @pl.when(self.end)
        def _():
            self.two.wait_recv()
            self.pass_copy.wait_recv()
        @pl.when(~self.end)
        def _():
            self.three.wait()
            self.pass_copy.wait_send()


class Added:
    def __init__(self, links, head, node, part, got, relay):
        self.end=(head==0)|(head==3)
        self.relay=relay
        self.far=part(head^2)
        self.zero=links.copy(part(head^3),relay,head^1,node)
        self.two=links.copy(self.far,got(1),head^2,node)
        self.one=links.copy(part(head^1),got(0),head^1,node)
        self.three=links.copy(part(head^3),got(2),head^3,node)
        @pl.when(self.end)
        def _():
            self.zero.start()
            self.two.start()
            self.one.start()
            got(2)[...]=jnp.zeros(relay.shape,bf16)
        @pl.when(~self.end)
        def _():
            self.three.start()
            self.one.start()

    def onward(self):
        @pl.when(~self.end)
        def _():
            self.zero.wait_recv()
            self.far[...]=summed(self.far,self.relay).astype(bf16)
            self.two.start()

    def wait(self):
        pl.when(self.end)(self.zero.wait_send)
        pl.when(~self.end)(self.three.wait)
        self.one.wait()
        self.two.wait()


def wait_all(copies):
    for c in copies: c.wait()


def block_of(index, size):
    return pl.ds(pl.multiple_of(index*size,size),size)


def summed(*refs):
    total=refs[0][...].astype(f32)
    for r in refs[1:]: total=total+r[...].astype(f32)
    return total


NAMES=("ada","qkv","out","up","down")


def scratch(rows):
    part=rows//4
    return dict(
        e=((5,rows,rows),bf16),m=((rows,128),f32),l=((rows,128),f32),att=((rows,128),f32),fac=((rows,128),f32),
        queries=((rows,128),bf16),table=((5,rows,384),bf16),xn_one=((rows,512),bf16),
        qkv_full=((512,384),bf16),out_full=((4,128,512),bf16),up_full=((512,2048),bf16),down_full=((4,512,512),bf16),
        modp=((8,1024),f32),modbuf=((8,8,1024),f32),modulation=((8,1024),f32),
        mixed=((rows,128),bf16),heads=((part,512),bf16),do=((rows,128),bf16),do_rows=((part,512),bf16),
        act=((part,2048),bf16),pre=((part,2048),bf16),dy=((part,512),f32),
        up_grad=((4,2,64,2048),bf16),down_grad=((4,4,2,64,512),bf16),out_grad=((4,4,2,16,512),bf16),
        dq=((rows,128),f32),dkv=((256,rows),f32),near=((5,256,rows),bf16),
        got_pair=((256,rows),bf16),got_y=((256,rows),bf16),got_x=((256,rows),bf16),got_one=((256,rows),bf16),
        proj_grad=((rows,384),bf16),partial=((4,part,512),bf16),got_partial=((3,part,512),bf16),normed=((rows,512),f32),
        up1=((4,64,2048),bf16),down1=((4,4,64,512),bf16),out1=((4,4,16,512),bf16),
        up2=((2,64,2048),bf16),down2=((4,2,64,512),bf16),out2=((4,2,16,512),bf16),
        up3=((64,2048),bf16),down3=((4,64,512),bf16),out3=((4,16,512),bf16),
        up_z=((3,64,512),bf16),down_z=((3,64,512),bf16),out_z=((3,16,512),bf16),
        up_relay=((64,512),bf16),down_relay=((64,512),bf16),out_relay=((16,512),bf16),relay=((part,512),bf16),
        qkv_grad=((8,64,384),bf16),qkv_got=((7,64,384),bf16),dm_own=((8,1024),f32),dm_z=((4,8,1024),f32),dm_n=((8,8,1024),f32),
    )


class Bag:
    pass


COPIES=150


def layer_kernel(scale, names, *refs):
    refs=list(refs)
    take=lambda n: [refs.pop(0) for _ in range(n)]
    node_input,cotangent,sigma,code,counts=take(5)
    w={n:refs.pop(0) for n in NAMES}
    node_output,row_all,qkv_sum,out_sum,up_sum,down_sum,mod_sum=take(7)
    k=Bag()
    for n in names: setattr(k,n,refs.pop(0))
    send,recv=take(2)
    head=lax.axis_index("head"); node=lax.axis_index("node")
    y_at=node//4; x_at=(node//2)%2; core=node%2
    rows=node_input.shape[0]
    part=rows//4
    links=Links(send,recv)
    go=links.go
    normed=k.normed
    quarter=[slice(i*part,(i+1)*part) for i in range(4)]
    limits=(counts[0],counts[0]+counts[1],counts[0]+counts[1]+counts[2])
    mine=block_of(head,part)
    head_cols=block_of(head,512)
    own_pos=node*rows+head*part+lax.broadcasted_iota(jnp.int32,(part,1),0)

    own=block_of(node,64); own_out=block_of(node,16)
    k.qkv_full[own,:]=w["qkv"][...].astype(bf16)
    sig=sigma[:,0:64]
    for i in range(1,8): sig=jnp.where(node==i,sigma[:,i*64:(i+1)*64],sig)
    made=jnp.dot(sig,w["ada"][...].astype(bf16),preferred_element_type=f32)
    k.modp[0:4,:]=made[:,:1024]
    k.modp[4:8,:]=made[:,1024:]
    k.up_full[own,head_cols]=w["up"][...].astype(bf16)
    k.down_full[head,own,:]=w["down"][...].astype(bf16)
    k.out_full[head,own_out,:]=w["out"][...].astype(bf16)
    meet([(head,node^i) for i in range(1,8)]+[(head^i,node) for i in range(1,4)])
    first=[]
    for i in range(1,8):
        first.append(go(k.modp,k.modbuf.at[node],head,node^i))
        first.append(go(k.qkv_full.at[own],k.qkv_full.at[own],head,node^i))
    along=[]
    for place in (lambda h: k.up_full.at[own,block_of(h,512)],lambda h: k.down_full.at[h,own],lambda h: k.out_full.at[h,own_out]):
        along.append(Shown(links,head,node,place))
    k.modbuf[node,:,:]=k.modp[...]
    for b in range(5): k.table[b,:,256:384]=jnp.ones((rows,128),bf16)
    def norm(i,_):
        at=block_of(i,256)
        v=node_input[at,:].astype(f32)
        centred=v-jnp.mean(v,axis=1,keepdims=True)
        normed[at,:]=centred*lax.rsqrt(jnp.mean(centred*centred,axis=1,keepdims=True)+norm_eps)
        return 0
    lax.fori_loop(0,rows//256,norm,0)
    groups=code.shape[0]
    half=groups//2
    count_groups(k.e,code,rows,0,half,4)
    for a in along: a.onward()
    def column(which):
        at=block_of(node^which,64)
        return [k.up_full.at[at],k.down_full.at[:,at],k.out_full.at[:,block_of(node^which,16)]]
    own_column=column(0); from_x=column(2); from_y=column(4)
    along[0].wait()
    up_x=go(own_column[0],own_column[0],head,node^2)
    wait_all(first)
    mod=k.modbuf[0]
    for i in range(1,8): mod=mod+k.modbuf[i]
    k.modulation[...]=mod

    kv=slice(0,256)
    across=[]; paired=[]
    for at in quarter:
        pos=node*rows+at.start+lax.broadcasted_iota(jnp.int32,(part,1),0)
        xn=(normed[at,:]*(1.0+by_batch(pos,limits,k.modulation,0,slice(0,512)))+by_batch(pos,limits,k.modulation,0,slice(512,1024))).astype(bf16)
        k.xn_one[at,:]=xn
        proj=jnp.dot(xn,k.qkv_full[...],preferred_element_type=f32).astype(bf16)
        k.queries[at,:]=proj[:,:128]
        k.table[0,at,kv]=proj[:,128:]
        across.append(go(k.table.at[0,at,kv],k.table.at[2,at,kv],head,node^2))
        paired.append(go(k.table.at[0,at,kv],k.table.at[1,at,kv],head,node^1))
    wait_all(along[1:])
    rest_y=[go(r,r,head,node^4) for r in own_column[1:]]
    count_groups(k.e,code,rows,half,groups,4)
    add_self(k.e,0,rows)

    onward=[]
    def pass_keys(i):
        at=quarter[i]
        across[i].wait_recv()
        onward.append(go(k.table.at[2,at,kv],k.table.at[3,at,kv],head,node^4))
    def attend(b,at):
        attend_rows(b,b==0,at,part,k.queries,k.table,k.e,k.m,k.l,k.att,k.fac,scale*math.log2(math.e))
    def attend_all(b):
        def two(i,_):
            for u in range(2): attend(b,block_of(2*i+u,part))
            return 0
        lax.fori_loop(0,2,two,0)
    pass_keys(0)
    attend_all(0)
    pass_keys(1)
    wait_all(paired)
    attend_all(1)
    pass_keys(2)
    pass_keys(3)
    up_y=go(own_column[0],own_column[0],head,node^4)
    rest_x=[go(r,r,head,node^2) for r in own_column[1:]]
    to_pair=[go(r,r,head,node^1) for r in own_column]
    up_x.wait()
    wait_all(rest_y)
    cross=[go(from_x[0],from_x[0],head,node^4)]+[go(r,r,head,node^2) for r in from_y[1:]]
    hand=[go(r,r,head,node^1) for r in from_x[:1]+from_y[1:]]
    attend_all(2)
    wait_all(onward)
    fifth=go(k.table.at[jnp.where(x_at==core,2,3),:,kv],k.table.at[4,:,kv],head,node^1)
    for at in quarter: attend(3,at)
    fifth.wait()
    lanes=block_of(head,128)
    moved=[]
    for i in range(4):
        at=quarter[i]
        attend(4,at)
        inv=1.0/k.l[at,:]
        o=k.att[at,:]*inv
        k.att[at,:]=o
        k.fac[at,:]=jnp.exp2(k.fac[at,:]-k.m[at,:])*inv
        k.mixed[at,:]=o.astype(bf16)
    for i in range(1,4):
        moved.append(go(k.mixed.at[block_of(head^i,part)],k.heads.at[:,lanes],head^i,node))
    k.heads[:,lanes]=k.mixed[mine,:]
    for c in across: c.wait_send()
    up_y.wait()
    wait_all(rest_x)
    hand+=[go(r,r,head,node^1) for r in from_y[:1]+from_x[1:]]
    wait_all(cross)
    last=[go(r,r,head,node^1) for r in column(6)]
    scale_two=1.0+by_batch(own_pos,limits,k.modulation,4,slice(0,512))
    shift_two=by_batch(own_pos,limits,k.modulation,4,slice(512,1024))
    g=cotangent[mine,:]
    wait_all(moved)
    wait_all(to_pair+hand+last)

    out_all=k.out_full[...].reshape(512,512)
    y=node_input[mine,:].astype(f32)+jnp.dot(k.heads[...],out_all,preferred_element_type=f32)
    n_two,inv_two=norm_parts(y)
    xn=(n_two*scale_two+shift_two).astype(bf16)
    mlp=jnp.zeros((part,512),f32); dxn=jnp.zeros((part,512),f32)
    for j in range(4):
        s=slice(j*512,(j+1)*512)
        h=jnp.dot(xn,k.up_full[:,s],preferred_element_type=f32)
        gate=1.0/(1.0+jnp.exp(-h))
        u=(h*gate).astype(bf16)
        k.act[:,s]=u
        mlp+=jnp.dot(u,k.down_full[j],preferred_element_type=f32)
        du=lax.dot_general(g,k.down_full[j],NT,preferred_element_type=f32)
        d=(du*gate*(1.0+h*(1.0-gate))).astype(bf16)
        k.pre[:,s]=d
        dxn+=lax.dot_general(d,k.up_full[:,s],NT,preferred_element_type=f32)
    dyv=g.astype(f32)+norm_back(dxn*scale_two,n_two,inv_two)
    k.dy[...]=dyv
    da=dyv.astype(bf16)
    k.do_rows[...]=lax.dot_general(da,out_all,NT,preferred_element_type=f32).astype(bf16)
    returned=[]
    for i in range(1,4):
        returned.append(go(k.do_rows.at[:,block_of(head^i,128)],k.do.at[mine],head^i,node))
    k.do[mine,:]=k.do_rows[:,lanes]
    node_output[mine,:]=(y+mlp).astype(bf16)
    xn_t=xn.T
    heads_t=k.heads[...].T
    k.out_grad[...]=jnp.dot(heads_t,da,preferred_element_type=f32).astype(bf16).reshape(4,4,2,16,512)
    for j in range(4):
        s=slice(j*512,(j+1)*512)
        k.up_grad[:,:,:,s]=jnp.dot(xn_t,k.pre[:,s],preferred_element_type=f32).astype(bf16).reshape(4,2,64,512)
        k.down_grad[j]=jnp.dot(k.act[:,s].T,g,preferred_element_type=f32).astype(bf16).reshape(4,2,64,512)
    stage1=[go(k.up_grad.at[:,1-core],k.up1,head,node^1),go(k.down_grad.at[:,:,1-core],k.down1,head,node^1),go(k.out_grad.at[:,:,1-core],k.out1,head,node^1)]
    k.dm_own[4:8,0:512]=batch_sums(own_pos,limits,dxn*n_two)
    k.dm_own[4:8,512:1024]=batch_sums(own_pos,limits,dxn)
    wait_all(returned)
    shown=Shown(links,head,node,lambda h: node_output.at[block_of(h,part)])

    q_t=k.queries[...].T
    dof=k.do[...].astype(f32)
    delta=jnp.sum(dof*k.att[...],axis=1,keepdims=True)
    def block(b):
        def write(r,s,v):
            if b==0: k.dkv[r,s]=v
            else: k.near[b,r,s]=v.astype(bf16)
        back_block(b,q_t,dof,k.fac,delta,k.table,k.e,k.dq,write,b==4,512,scale)
    near=k.near
    block(4)
    give=go(near.at[4],k.got_pair,head,node^1)
    block(3)
    give.wait()
    @pl.when(x_at!=core)
    def _(): near[3]=summed(near[3],k.got_pair[...]).astype(bf16)
    via_y=[go(near.at[3,:,s],k.got_y.at[:,s],head,node^4) for s in quarter]
    block(2)
    @pl.when(x_at==core)
    def _(): near[2]=summed(near[2],k.got_pair[...]).astype(bf16)
    via_x=[]
    def pass_on(i):
        s=quarter[i]
        via_y[i].wait()
        near[2,:,s]=summed(near[2,:,s],k.got_y[:,s]).astype(bf16)
        via_x.append(go(near.at[2,:,s],k.got_x.at[:,s],head,node^2))
    pass_on(0)
    shown.onward()
    block(1)
    one=go(near.at[1],k.got_one,head,node^1)
    pass_on(1)
    pass_on(2)
    block(0)
    pass_on(3)
    wait_all(stage1)
    for i in range(4):
        k.up1[i]=summed(k.up1[i],k.up_grad[i,core]).astype(bf16)
        k.down1[i]=summed(k.down1[i],k.down_grad[i,:,core]).astype(bf16)
        k.out1[i]=summed(k.out1[i],k.out_grad[i,:,core]).astype(bf16)
    stage2=[go(k.up1.at[i*2+1-x_at],k.up2.at[i],head,node^2) for i in range(2)]
    there=pl.ds((1-y_at)*2,2)
    stage2+=[go(k.down1.at[:,there],k.down2,head,node^4),go(k.out1.at[:,there],k.out2,head,node^4)]
    xn_t=k.xn_one[...].T
    one.wait()
    for i in range(4):
        s=quarter[i]
        via_x[i].wait()
        total=k.dkv[:,s]+k.got_one[:,s].astype(f32)+k.got_x[:,s].astype(f32)
        k.proj_grad[s,128:]=total.T.astype(bf16)
        k.proj_grad[s,:128]=(k.dq[s,:]*scale).astype(bf16)
        k.partial[i]=lax.dot_general(k.proj_grad[s,:],k.qkv_full[...],NT,preferred_element_type=f32).astype(bf16)
    reduce=Added(links,head,node,lambda h: k.partial.at[h],lambda i: k.got_partial.at[i],k.relay)
    k.qkv_grad[...]=jnp.dot(xn_t,k.proj_grad[...],preferred_element_type=f32).astype(bf16).reshape(8,64,384)
    qkv_moves=[go(k.qkv_grad.at[node^i],k.qkv_got.at[i-1],head,node^i) for i in range(1,8)]
    reduce.onward()
    wait_all(stage2)
    for i in range(2):
        k.up2[i]=summed(k.up2[i],k.up1[i*2+x_at]).astype(bf16)
    here=pl.ds(y_at*2,2)
    k.down2[...]=summed(k.down2[...],k.down1[:,here]).astype(bf16)
    k.out2[...]=summed(k.out2[...],k.out1[:,here]).astype(bf16)
    stage3=[go(k.up2.at[1-y_at],k.up3,head,node^4),go(k.down2.at[:,1-x_at],k.down3,head,node^2),go(k.out2.at[:,1-x_at],k.out3,head,node^2)]
    scale_one=1.0+by_batch(own_pos,limits,k.modulation,0,slice(0,512))
    n_one,inv_one=norm_parts(node_input[mine,:].astype(f32))
    wait_all(qkv_moves)
    qkv_sum[...]=summed(k.qkv_grad[node],*[k.qkv_got[i] for i in range(7)])
    wait_all(stage3)
    k.up3[...]=summed(k.up3[...],k.up2[y_at]).astype(bf16)
    k.down3[...]=summed(k.down3[...],k.down2[:,x_at]).astype(bf16)
    k.out3[...]=summed(k.out3[...],k.out2[:,x_at]).astype(bf16)
    stage4=[Added(links,head,node,lambda h: k.up3.at[:,block_of(h,512)],lambda i: k.up_z.at[i],k.up_relay),
        Added(links,head,node,lambda h: k.down3.at[h],lambda i: k.down_z.at[i],k.down_relay),
        Added(links,head,node,lambda h: k.out3.at[h],lambda i: k.out_z.at[i],k.out_relay)]
    reduce.wait()
    dxn=summed(k.partial.at[head],*[k.got_partial.at[i] for i in range(3)])
    k.dm_own[0:4,0:512]=batch_sums(own_pos,limits,dxn*n_one)
    k.dm_own[0:4,512:1024]=batch_sums(own_pos,limits,dxn)
    dm_moves=[go(k.dm_own,k.dm_z.at[head],head^i,node) for i in range(1,4)]
    row_all[head,:,:]=(k.dy[...]+norm_back(dxn*scale_one,n_one,inv_one)).astype(bf16)
    spread=Shown(links,head,node,lambda h: row_all.at[h])
    for s in stage4: s.onward()
    k.dm_z[head,:,:]=k.dm_own[...]
    wait_all(dm_moves)
    k.modp[...]=k.dm_z[0]+k.dm_z[1]+k.dm_z[2]+k.dm_z[3]
    dm_last=[go(k.modp,k.dm_n.at[node],head,node^i) for i in range(1,8)]
    k.dm_n[node,:,:]=k.modp[...]
    spread.onward()
    wait_all(dm_last)
    total=k.dm_n[0]
    for i in range(1,8): total=total+k.dm_n[i]
    mod_sum[...]=total
    wait_all(stage4)
    up_sum[...]=summed(k.up3[:,head_cols],*[k.up_z[i] for i in range(3)])
    down_sum[...]=summed(k.down3[head],*[k.down_z[i] for i in range(3)])
    out_sum[...]=summed(k.out3[head],*[k.out_z[i] for i in range(3)])
    spread.wait()
    shown.wait()


def finish_kernel(sigma, step_count, *refs):
    sources=refs[:22]; results=refs[22:39]; held=refs[39:62]; load,store=refs[62:]
    loads=[pltpu.make_async_copy(sources[i],held[i],load.at[i]) for i in range(22)]
    for i in (0,1)+tuple(range(7,22))+tuple(range(2,7)): loads[i].start()
    node=lax.axis_index("node")
    stores=[]
    def keep(ref, result):
        stores.append(pltpu.make_async_copy(ref,results[result],store.at[result])); stores[-1].start()
    loads[0].wait()
    keep(held[0],0)
    loads[1].wait()
    wide=held[22]
    rows=wide.shape[0]
    for i in range(4): wide[i*rows//4:(i+1)*rows//4,:]=held[1][i].astype(f32)
    keep(wide,1)
    count=jnp.full((8,128),step_count[0],jnp.int32).astype(f32)
    correct=(1.0-jnp.exp2(-count))[0:1,0:1]
    sig=sigma[:,0:64]
    for i in range(1,8): sig=jnp.where(node==i,sigma[:,i*64:(i+1)*64],sig)
    rates=((4*COND)**-0.5,(WIDTH//2)**-0.5,(WIDTH//4)**-0.5,WIDTH**-0.5,HIDDEN_SIZE**-0.5)
    for w in (0,3,4,1,2):
        at=7+3*w
        for i in range(3): loads[at+i].wait()
        if w==0:
            loads[6].wait()
            total=held[6]
            batch_grad=jnp.concatenate([total[0:4,:],total[4:8,:]],axis=1)
            grad=lax.dot_general(sig.astype(f32),batch_grad,(((0,),(0,)),((),())),precision=highest,preferred_element_type=f32)
        else:
            loads[1+w].wait()
            grad=held[1+w][...]
        master,first,second=held[at:at+3]
        first_new=beta_rate*first[...]+(1.0-beta_rate)*grad
        second_new=beta_rate*second[...]+(1.0-beta_rate)*grad*grad
        step=first_new/correct/(jnp.sqrt(second_new/correct)+adam_eps)
        old=master[...]
        master[...]=old-rates[w]*(step+weight_decay*old)
        first[...]=first_new
        second[...]=second_new
        for i in range(3): keep(held[at+i],2+3*w+i)
    for c in stores: c.wait()


def slots(neighbours, valid, node, rows):
    which=(neighbours//rows)^node
    slot=jnp.where(which==6,3,jnp.where((which==3)|(which==7),4,which))
    local=neighbours%rows
    spot=lax.broadcasted_iota(jnp.int32,neighbours.shape,0)%16
    hi=(slot*(rows//SPAN)+local//SPAN)*16+spot
    return jnp.where(valid>0,hi*256+local%SPAN,-1).reshape(-1,256)


def per_device_near(
    node_input, cotangent, sigma_embed, neighbours, neighbour_valid, batch_counts, step_count,
    ada_master, ada_first, ada_second, qkv_master, qkv_first, qkv_second, out_master, out_first, out_second,
    up_master, up_first, up_second, down_master, down_first, down_second,
):
    rows=node_input.shape[0]
    code=slots(neighbours,neighbour_valid,lax.axis_index("node"),rows)
    masters=(ada_master,qkv_master,out_master,up_master,down_master)
    firsts=(ada_first,qkv_first,out_first,up_first,down_first)
    seconds=(ada_second,qkv_second,out_second,up_second,down_second)
    V=pltpu.VMEM
    full=pl.BlockSpec(memory_space=V); few=pl.BlockSpec(memory_space=pltpu.SMEM); hbm=pl.BlockSpec(memory_space=pltpu.HBM)
    S=jax.ShapeDtypeStruct
    held=scratch(rows)
    sums=pl.pallas_call(functools.partial(layer_kernel,128**-0.5,tuple(held)),
        out_shape=(S((rows,512),bf16),S((4,rows//4,512),bf16))+tuple(S(a.shape,f32) for a in masters[1:])+(S((8,1024),f32),),
        in_specs=[full]*4+[few]+[full]*5,
        out_specs=(full,)*7,
        scratch_shapes=[V(*v) for v in held.values()]+[pltpu.SemaphoreType.DMA((COPIES,))]*2,
        compiler_params=pltpu.CompilerParams(vmem_limit_bytes=67043328,collective_id=1,has_side_effects=True),
        name="layer")(node_input,cotangent,sigma_embed,code,batch_counts,*masters)
    news=tuple(S(a.shape,f32) for a in masters for _ in range(3))
    inner=[V(a.shape,a.dtype) for a in sums]+[V(a.shape,f32) for a in masters for _ in range(3)]+[V((rows,512),f32)]
    return pl.pallas_call(finish_kernel,
        out_shape=(S((rows,512),bf16),S((rows,512),f32))+news,
        in_specs=[full,few]+[hbm]*(7+15),
        out_specs=(hbm,)*17,
        scratch_shapes=inner+[pltpu.SemaphoreType.DMA((22,)),pltpu.SemaphoreType.DMA((17,))],
        compiler_params=pltpu.CompilerParams(vmem_limit_bytes=67043328),
        name="finish")(sigma_embed,step_count,*sums,*[a for three in zip(masters,firsts,seconds) for a in three])


def wide_count_groups(cnt, hik, lok, rows):
    steps=hik.shape[0]
    parts=rows//SPAN
    total=5*parts*16
    rowid=lax.broadcasted_iota(jnp.int32,(total,1),0)
    rowkey=lax.div(rowid,16)*16+lax.rem(rowid,16)
    spot=lax.broadcasted_iota(jnp.int32,(SPAN,1),0)
    def body(g,_):
        keys=hik[pl.ds(g,1),:]
        low=lok[pl.ds(g,1),:]
        left=jnp.where(rowkey==keys,1.0,0.0).astype(bf16)
        right=jnp.where(spot==low,1.0,0.0).astype(bf16)
        made=lax.dot_general(left,right,NT,preferred_element_type=f32).astype(bf16)
        at=pl.multiple_of(g*16,16)
        for b in range(5):
            for p in range(parts):
                r=(b*parts+p)*16
                cnt[b,pl.ds(at,16),p*SPAN:(p+1)*SPAN]=made[r:r+16,:]
        return 0
    lax.fori_loop(0,steps,body,0)

def wide_add_self(cnt, block, rows):
    eye=(lax.broadcasted_iota(jnp.int32,(SPAN,SPAN),0)==lax.broadcasted_iota(jnp.int32,(SPAN,SPAN),1))
    one=jnp.where(eye,1.0,0.0).astype(bf16)
    for p in range(rows//SPAN):
        s=slice(p*SPAN,(p+1)*SPAN)
        cnt[block,s,s]=cnt[block,s,s]+one

def wide_attend_block(b, first, q, keys, vals, cnt, e, m, l, acc, fac, chunk, scale):
    rows=q.shape[0]
    lane=lax.broadcasted_iota(jnp.int32,(chunk,128),1)
    def body(i,_):
        at=pl.ds(pl.multiple_of(i*chunk,chunk),chunk)
        s=lax.dot_general(q[at,:],keys,NT,preferred_element_type=f32)*scale
        c=cnt[b,at,:].astype(f32)
        s=jnp.where(c>0,s,-1e30)
        top=jnp.max(s,axis=1,keepdims=True)
        if not first:
            old=m[at,0:1]
            top=jnp.maximum(top,old)
        w=(jnp.exp2(s-top)*c)
        total=jnp.sum(w,axis=1,keepdims=True)
        w=w.astype(bf16)
        e[b,at,:]=w
        out=jnp.dot(w,vals,preferred_element_type=f32)
        if first:
            acc[at,:]=out; l[at,:]=jnp.broadcast_to(total,(chunk,128))
            fac[at,:]=jnp.where(lane==b,top,0.0)
        else:
            shrink=jnp.exp2(old-top)
            acc[at,:]=acc[at,:]*shrink+out
            l[at,:]=l[at,:]*shrink+total
            fac[at,:]=jnp.where(lane==b,top,fac[at,:])
        m[at,:]=jnp.broadcast_to(top,(chunk,128))
        return 0
    lax.fori_loop(0,rows//chunk,body,0)

def wide_fwd_kernel(order, self_block, scale, q, kv, hik, lok, att, e, fac, cnt, m, l):
    rows=q.shape[0]
    wide_count_groups(cnt,hik,lok,rows)
    wide_add_self(cnt,self_block,rows)
    for t,b in enumerate(order):
        wide_attend_block(b,t==0,q,kv[b,:,:128],kv[b,:,128:],cnt,e,m,l,att,fac,256,scale)
    inv=1.0/l[...]
    att[...]=att[...]*inv
    fac[...]=jnp.exp2(fac[...]-m[...])*inv

def wide_attention_fwd(q,kv,hik,lok,scale):
    rows=q.shape[0]
    V=pltpu.VMEM
    full=pl.BlockSpec(memory_space=V)
    return pl.pallas_call(functools.partial(wide_fwd_kernel,(2,1,3,0,4),2,scale*math.log2(math.e)),
        out_shape=(jax.ShapeDtypeStruct((rows,128),f32),jax.ShapeDtypeStruct((5,rows,rows),bf16),jax.ShapeDtypeStruct((rows,128),f32)),
        in_specs=[full]*4,out_specs=(full,)*3,
        scratch_shapes=[V((5,rows,rows),bf16),V((rows,128),f32),V((rows,128),f32)],
        compiler_params=pltpu.CompilerParams(vmem_limit_bytes=60<<20),name="attend_fwd")(q,kv,hik,lok)

def wide_back_block(b, q_t, do, fac, delta, kv, e, dq, dkv, first, chunk, keyscale):
    rows=do.shape[0]
    f=fac[:,b:b+1]
    dob=(do*f)
    dobh=dob.astype(bf16)
    d=-(delta*f)
    h=d.astype(bf16); r=d-h.astype(f32); h2=r.astype(bf16); h3=(r-h2.astype(f32)).astype(bf16)
    lane=lax.broadcasted_iota(jnp.int32,(rows,128),1)
    zero=jnp.zeros((rows,128),bf16)
    dcol=jnp.where(lane==0,h.astype(f32),jnp.where(lane==1,h2.astype(f32),jnp.where(lane==2,h3.astype(f32),0.0))).astype(bf16)
    left=jnp.concatenate([dobh,dcol],axis=1)
    dob_t=dobh.T
    ones=jnp.ones((chunk,128),bf16)
    for i in range(kv.shape[1]//chunk):
        s=slice(i*chunk,(i+1)*chunk)
        right=jnp.concatenate([kv[b,s,128:],ones],axis=1)
        dp=lax.dot_general(left,right,NT,preferred_element_type=f32)
        w=e[b,:,s]
        ds=(dp*w.astype(f32)).astype(bf16)
        dkv[b,:128,s]=jnp.dot(q_t,ds,preferred_element_type=f32)*keyscale
        dkv[b,128:,s]=jnp.dot(dob_t,w,preferred_element_type=f32)
        out=jnp.dot(ds,kv[b,s,:128],preferred_element_type=f32)
        if first and i==0: dq[...]=out
        else: dq[...]+=out

def wide_bwd_kernel(scale, q, do, att, fac, kv, e, dq, dkv, ):
    q_t=q[...].T
    dof=do[...].astype(f32)
    delta=jnp.sum(dof*att[...],axis=1,keepdims=True)
    for t,b in enumerate((0,4,1,3,2)):
        wide_back_block(b,q_t,dof,fac,delta,kv,e,dq,dkv,t==0,512,scale)
    dq[...]=dq[...]*scale

def wide_attention_bwd(q,do,att,fac,kv,e,scale):
    rows=q.shape[0]
    V=pltpu.VMEM
    full=pl.BlockSpec(memory_space=V)
    return pl.pallas_call(functools.partial(wide_bwd_kernel,scale),
        out_shape=(jax.ShapeDtypeStruct((rows,128),f32),jax.ShapeDtypeStruct((5,256,rows),f32)),
        in_specs=[full]*6,out_specs=(full,)*2,
        compiler_params=pltpu.CompilerParams(vmem_limit_bytes=60<<20),name="attend_bwd")(q,do,att,fac,kv,e)

def wide_tables(slot_index, valid, rows):
    parts=rows//SPAN
    flat=slot_index.reshape(-1,256)
    ok=(valid>0).reshape(-1,256)
    node=lax.broadcasted_iota(jnp.int32,flat.shape,1)//16
    hi=jnp.where(ok,(flat//SPAN)*16+node,-1)
    lo=flat%SPAN
    return hi,lo


def per_device(
    node_input,
    cotangent,
    sigma_embed,
    neighbours,
    neighbour_valid,
    batch_counts,
    step_count,
    ada_master,
    ada_first,
    ada_second,
    qkv_master,
    qkv_first,
    qkv_second,
    out_master,
    out_first,
    out_second,
    up_master,
    up_first,
    up_second,
    down_master,
    down_first,
    down_second,
):
    f32 = jnp.float32
    bf16 = jnp.bfloat16
    node_rows = node_input.shape[0]
    model_width = node_input.shape[1]
    head_dim = qkv_master.shape[1] // 3
    score_scale = head_dim ** (-0.5)
    node_index = lax.axis_index("node")
    total_nodes = node_rows * lax.axis_size("node")
    qkv_full, out_full, up_full, down_full = (
        lax.all_gather(qkv_master.astype(bf16), "node", axis=0, tiled=True),
        lax.all_gather(out_master.astype(bf16), "node", axis=0, tiled=True),
        lax.all_gather(up_master.astype(bf16), "node", axis=0, tiled=True),
        lax.all_gather(down_master.astype(bf16), "node", axis=0, tiled=True),
    )
    cond_rows = ada_master.shape[0]
    sigma_part = lax.dynamic_slice_in_dim(sigma_embed, node_index * cond_rows, cond_rows, 1)
    limits = jnp.cumsum(batch_counts)[:-1]
    positions = node_index * node_rows + jnp.arange(node_rows, dtype=jnp.int32)
    member = jnp.sum((positions[:, None] >= limits[None, :]).astype(jnp.int32), axis=1)
    onehot = (
        member[:, None] == jnp.arange(batch_counts.shape[0], dtype=jnp.int32)[None, :]
    ).astype(f32)
    modulation = lax.psum(
        jnp.dot(sigma_part, ada_master.astype(bf16), preferred_element_type=f32), "node"
    )
    per_node = jnp.dot(onehot, modulation, precision=highest)
    scale_one = per_node[:, :model_width]
    shift_one = per_node[:, model_width : 2 * model_width]
    scale_two = per_node[:, 2 * model_width : 3 * model_width]
    shift_two = per_node[:, 3 * model_width :]
    normed_one, inverse_one = norm_parts(node_input.astype(f32))
    xn_one = (normed_one * (1.0 + scale_one) + shift_one).astype(bf16)
    projected = jnp.dot(xn_one, qkv_full, preferred_element_type=f32).astype(bf16)
    queries = projected[:, :head_dim]
    keys_values = projected[:, head_dim:]
    offsets = (-2, -1, 1, 2)
    fetched = {0: keys_values}
    for offset in offsets:
        fetched[offset] = passed_along(keys_values, "node", -offset)
    table = jnp.stack([fetched[offset] for offset in (-2, -1, 0, 1, 2)], axis=0)
    slot_index = jnp.mod(neighbours - (node_index - 2) * node_rows, total_nodes)
    high_keys, low_keys = wide_tables(slot_index, neighbour_valid, node_rows)
    mixed, weights, factors = wide_attention_fwd(queries, table, high_keys, low_keys, score_scale)
    heads_out = mixed.astype(bf16)
    branch = lax.psum(
        jnp.dot(heads_out, out_full, preferred_element_type=f32).astype(jnp.bfloat16), "head"
    ).astype(jnp.float32)
    middle = node_input.astype(f32) + branch
    normed_two, inverse_two = norm_parts(middle)
    xn_two = (normed_two * (1.0 + scale_two) + shift_two).astype(bf16)
    hidden_pre = jnp.dot(xn_two, up_full, preferred_element_type=f32)
    gate_sig = jax.nn.sigmoid(hidden_pre)
    activated = (hidden_pre * gate_sig).astype(bf16)
    mlp_sum = lax.psum(
        jnp.dot(activated, down_full, preferred_element_type=f32).astype(jnp.bfloat16), "head"
    ).astype(jnp.float32)
    node_output = (middle + mlp_sum).astype(bf16)
    down_grad = jnp.einsum("nf,nd->fd", activated, cotangent, preferred_element_type=f32)
    act_grad = jnp.einsum("nd,fd->nf", cotangent, down_full, preferred_element_type=f32)
    pre_grad = (act_grad * gate_sig * (1.0 + hidden_pre * (1.0 - gate_sig))).astype(bf16)
    up_grad = jnp.einsum("nw,nf->wf", xn_two, pre_grad, preferred_element_type=f32)
    normed_two_grad = lax.psum(
        jnp.einsum("nf,wf->nw", pre_grad, up_full, preferred_element_type=f32).astype(jnp.bfloat16),
        "head",
    ).astype(jnp.float32)
    middle_grad = cotangent.astype(f32) + norm_back(
        normed_two_grad * (1.0 + scale_two), normed_two, inverse_two
    )
    branch_grad = middle_grad.astype(bf16)
    out_grad = jnp.einsum("nh,nd->hd", heads_out, branch_grad, preferred_element_type=f32)
    mixed_grad = jnp.einsum("nd,hd->nh", branch_grad, out_full, preferred_element_type=f32).astype(
        bf16
    )
    query_grad, pair_sums = wide_attention_bwd(
        queries, mixed_grad, mixed, factors, table, weights, score_scale
    )
    remote_terms = pair_sums[2]
    for offset in offsets:
        remote_terms = remote_terms + passed_along(
            pair_sums[offset + 2].astype(bf16), "node", offset
        ).astype(f32)
    key_value_grad = remote_terms.T
    projected_grad = jnp.concatenate([query_grad, key_value_grad], axis=1).astype(bf16)
    qkv_grad = jnp.einsum("nw,nc->wc", xn_one, projected_grad, preferred_element_type=f32)
    normed_one_grad = lax.psum(
        jnp.einsum("nc,wc->nw", projected_grad, qkv_full, preferred_element_type=f32).astype(
            jnp.bfloat16
        ),
        "head",
    ).astype(jnp.float32)
    input_grad = middle_grad + norm_back(
        normed_one_grad * (1.0 + scale_one), normed_one, inverse_one
    )
    rows_grad = jnp.concatenate(
        [
            normed_one_grad * normed_one,
            normed_one_grad,
            normed_two_grad * normed_two,
            normed_two_grad,
        ],
        axis=1,
    )
    batch_grad = jnp.dot(onehot.T, rows_grad, precision=highest)
    batch_grad = lax.psum(batch_grad, "node")
    ada_sum = jnp.dot(sigma_part.astype(f32).T, batch_grad, precision=highest)
    qkv_sum, out_sum, up_sum, down_sum = (
        lax.psum_scatter(qkv_grad, "node", scatter_dimension=0, tiled=True),
        lax.psum_scatter(out_grad, "node", scatter_dimension=0, tiled=True),
        lax.psum_scatter(up_grad, "node", scatter_dimension=0, tiled=True),
        lax.psum_scatter(down_grad, "node", scatter_dimension=0, tiled=True),
    )
    count_value = step_count[0].astype(f32)
    ada_res = adamw_update(
        ada_master, ada_first, ada_second, ada_sum, (4 * COND) ** (-0.5), count_value
    )
    qkv_res = adamw_update(
        qkv_master, qkv_first, qkv_second, qkv_sum, (WIDTH // 2) ** (-0.5), count_value
    )
    out_res = adamw_update(
        out_master, out_first, out_second, out_sum, (WIDTH // 4) ** (-0.5), count_value
    )
    up_res = adamw_update(up_master, up_first, up_second, up_sum, WIDTH ** (-0.5), count_value)
    down_res = adamw_update(
        down_master, down_first, down_second, down_sum, HIDDEN_SIZE ** (-0.5), count_value
    )
    return (
        node_output,
        input_grad,
        ada_res[0],
        ada_res[1],
        ada_res[2],
        qkv_res[0],
        qkv_res[1],
        qkv_res[2],
        out_res[0],
        out_res[1],
        out_res[2],
        up_res[0],
        up_res[1],
        up_res[2],
        down_res[0],
        down_res[1],
        down_res[2],
    )


def solution(mesh):
    chosen = per_device_near if mesh.shape["node"] == 8 and mesh.shape["head"] == 4 else per_device
    placed = (
        P("node", None),
        P("node", None),
        P(),
        P("node", None),
        P("node", None),
        P(),
        P(),
        P("node", None),
        P("node", None),
        P("node", None),
        P("node", "head"),
        P("node", "head"),
        P("node", "head"),
        P(("head", "node"), None),
        P(("head", "node"), None),
        P(("head", "node"), None),
        P("node", "head"),
        P("node", "head"),
        P("node", "head"),
        P(("head", "node"), None),
        P(("head", "node"), None),
        P(("head", "node"), None),
    )
    return jax.shard_map(
        chosen,
        mesh=mesh,
        in_specs=placed,
        out_specs=(
            P("node", None),
            P("node", None),
            P("node", None),
            P("node", None),
            P("node", None),
            P("node", "head"),
            P("node", "head"),
            P("node", "head"),
            P(("head", "node"), None),
            P(("head", "node"), None),
            P(("head", "node"), None),
            P("node", "head"),
            P("node", "head"),
            P("node", "head"),
            P(("head", "node"), None),
            P(("head", "node"), None),
            P(("head", "node"), None),
        ),
        check_vma=False,
    )
```

```python
import functools
import math

import jax
import jax.numpy as jnp
from jax import lax
from jax.experimental import pallas as pl
from jax.experimental.pallas import tpu as pltpu
from jax.sharding import PartitionSpec as P


WIDTH = 512
HIDDEN_SIZE = 2048
COND = 512


norm_eps = 1e-06
beta_rate = 0.5
adam_eps = 1e-08
weight_decay = 0.1
highest = lax.Precision.HIGHEST


def passed_along(block, axis, distance):
    devices = range(lax.axis_size(axis))
    route = [((i - distance) % len(devices), i) for i in devices]
    return lax.ppermute(block, axis, route)


def norm_parts(values):
    centred = values - jnp.mean(values, axis=1, keepdims=True)
    inverse = lax.rsqrt(jnp.mean(centred * centred, axis=1, keepdims=True) + norm_eps)
    return (centred * inverse, inverse)


def norm_back(grad_normed, normed, inverse):
    first_mean = jnp.mean(grad_normed, axis=1, keepdims=True)
    second_mean = jnp.mean(grad_normed * normed, axis=1, keepdims=True)
    return inverse * (grad_normed - first_mean - normed * second_mean)


def adamw_update(master, first, second, grad, rate, count_value):
    first_new = beta_rate * first + (1.0 - beta_rate) * grad
    second_new = beta_rate * second + (1.0 - beta_rate) * grad * grad
    correct = 1.0 - jnp.power(jnp.float32(beta_rate), count_value)
    normed_step = first_new / correct / (jnp.sqrt(second_new / correct) + adam_eps)
    master_new = master - rate * (normed_step + weight_decay * master)
    return (master_new, first_new, second_new)


f32=jnp.float32; bf16=jnp.bfloat16
NT=(((1,),(1,)),((),()))
SPAN=256

def count_groups(cnt, code, rows, start, stop, step):
    parts=rows//SPAN
    total=5*parts*16
    short=jnp.int16
    rowid=lax.broadcasted_iota(jnp.int32,(total,SPAN),0).astype(short)
    spot=lax.broadcasted_iota(jnp.int32,(SPAN,SPAN),0).astype(short)
    one=bf16(1); zero=bf16(0)
    def group(g):
        both=code[pl.ds(g,1),:]
        keys=lax.shift_right_arithmetic(both,8).astype(short)
        low=lax.bitwise_and(both,255).astype(short)
        left=jnp.where(rowid==jnp.broadcast_to(keys,(total,SPAN)),one,zero)
        right=jnp.where(spot==jnp.broadcast_to(low,(SPAN,SPAN)),one,zero)
        made=lax.dot_general(left,right,NT,preferred_element_type=f32).astype(bf16)
        at=pl.multiple_of(g*16,16)
        for b in range(5):
            for p in range(parts):
                r=(b*parts+p)*16
                cnt[b,pl.ds(at,16),p*SPAN:(p+1)*SPAN]=made[r:r+16,:]
    def body(g,_):
        for u in range(step): group(g*step+u)
        return 0
    lax.fori_loop(start//step,stop//step,body,0)

def add_self(cnt, block, rows):
    eye=(lax.broadcasted_iota(jnp.int32,(SPAN,SPAN),0)==lax.broadcasted_iota(jnp.int32,(SPAN,SPAN),1))
    one=jnp.where(eye,1.0,0.0).astype(bf16)
    for p in range(rows//SPAN):
        s=slice(p*SPAN,(p+1)*SPAN)
        cnt[block,s,s]=cnt[block,s,s]+one

def attend_rows(b, first, at, size, q, table, e, m, l, acc, fac, scale):
    lane=lax.broadcasted_iota(jnp.int32,(size,128),1)
    s=lax.dot_general(q[at,:],table[b,:,0:128],NT,preferred_element_type=f32)*scale
    c=e[b,at,:].astype(f32)
    s=jnp.where(c>0,s,-1e30)
    top=jnp.max(s,axis=1,keepdims=True)
    if not first:
        old=m[at,0:1]
        top=jnp.maximum(top,old)
    w=(jnp.exp2(s-top)*c).astype(bf16)
    e[b,at,:]=w
    out=jnp.dot(w,table[b,:,128:384],preferred_element_type=f32)
    if first:
        acc[at,:]=out[:,:128]; l[at,:]=out[:,128:]
        fac[at,:]=jnp.where(lane==b,top,0.0)
    else:
        shrink=jnp.exp2(old-top)
        acc[at,:]=acc[at,:]*shrink+out[:,:128]
        l[at,:]=l[at,:]*shrink+out[:,128:]
        fac[at,:]=jnp.where(lane==b,top,fac[at,:])
    m[at,:]=jnp.broadcast_to(top,(size,128))

def back_block(b, q_t, dof, fac, delta, table, e, dq, write, first, chunk, keyscale):
    rows=dof.shape[0]
    f=fac[:,b:b+1]
    dobh=(dof*f).astype(bf16)
    d=-(delta*f)
    h=d.astype(bf16); r=d-h.astype(f32); h2=r.astype(bf16); h3=(r-h2.astype(f32)).astype(bf16)
    lane=lax.broadcasted_iota(jnp.int32,(rows,128),1)
    dcol=jnp.where(lane==0,h.astype(f32),jnp.where(lane==1,h2.astype(f32),jnp.where(lane==2,h3.astype(f32),0.0))).astype(bf16)
    left=jnp.concatenate([dobh,dcol],axis=1)
    dob_t=dobh.T
    for i in range(rows//chunk):
        s=slice(i*chunk,(i+1)*chunk)
        dp=lax.dot_general(left,table[b,s,128:384],NT,preferred_element_type=f32)
        w=e[b,:,s]
        ds=(dp*w.astype(f32)).astype(bf16)
        write(slice(0,128),s,jnp.dot(q_t,ds,preferred_element_type=f32)*keyscale)
        write(slice(128,256),s,jnp.dot(dob_t,w,preferred_element_type=f32))
        out=jnp.dot(ds,table[b,s,0:128],preferred_element_type=f32)
        if first and i==0: dq[...]=out
        else: dq[...]+=out


def by_batch(pos, limits, table, row, lanes):
    pick=[table[row+b:row+b+1,lanes] for b in range(4)]
    out=jnp.where(pos>=limits[0],pick[1],pick[0])
    out=jnp.where(pos>=limits[1],pick[2],out)
    return jnp.where(pos>=limits[2],pick[3],out)


def batch_sums(pos, limits, values):
    lane=lax.broadcasted_iota(jnp.int32,(pos.shape[0],8),1)
    member=(pos>=limits[0]).astype(jnp.int32)+(pos>=limits[1]).astype(jnp.int32)+(pos>=limits[2]).astype(jnp.int32)
    onehot=jnp.where(lane==member,1.0,0.0).astype(f32)
    return lax.dot_general(onehot,values,(((0,),(0,)),((),())),precision=highest,preferred_element_type=f32)[0:4,:]


class Links:
    def __init__(self, send, recv):
        self.send, self.recv, self.used = send, recv, 0

    def copy(self, src, dst, head, node):
        made=pltpu.make_async_remote_copy(src_ref=src,dst_ref=dst,send_sem=self.send.at[self.used],recv_sem=self.recv.at[self.used],
            device_id=(head,node),device_id_type=pl.DeviceIdType.MESH)
        self.used+=1
        return made

    def go(self, src, dst, head, node):
        made=self.copy(src,dst,head,node)
        made.start()
        return made


def meet(peers):
    barrier=pltpu.get_barrier_semaphore()
    for head,node in peers:
        pl.semaphore_signal(barrier,inc=1,device_id=(head,node),device_id_type=pl.DeviceIdType.MESH)
    pl.semaphore_wait(barrier,len(peers))


class Shown:
    def __init__(self, links, head, node, place):
        self.end=(head==0)|(head==3)
        own=place(head)
        self.two=links.go(own,own,head^2,node)
        self.one=links.go(own,own,head^1,node)
        self.three=links.copy(own,own,head^3,node)
        pl.when(~self.end)(self.three.start)
        far=place(jnp.where(self.end,head^3,head^2))
        self.pass_copy=links.copy(far,far,head^1,node)

    def onward(self):
        @pl.when(~self.end)
        def _():
            self.two.wait_recv()
            self.pass_copy.start()

    def wait(self):
        self.one.wait()
        self.two.wait_send()
        @pl.when(self.end)
        def _():
            self.two.wait_recv()
            self.pass_copy.wait_recv()
        @pl.when(~self.end)
        def _():
            self.three.wait()
            self.pass_copy.wait_send()


class Added:
    def __init__(self, links, head, node, part, got, relay):
        self.end=(head==0)|(head==3)
        self.relay=relay
        self.far=part(head^2)
        self.zero=links.copy(part(head^3),relay,head^1,node)
        self.two=links.copy(self.far,got(1),head^2,node)
        self.one=links.copy(part(head^1),got(0),head^1,node)
        self.three=links.copy(part(head^3),got(2),head^3,node)
        self.head=head
        @pl.when(self.end)
        def _(): got(2)[...]=jnp.zeros(relay.shape,bf16)

    def begin(self, to):
        pl.when(self.end&(self.head==to^3))(self.zero.start)
        pl.when((~self.end)&(self.head==to^3))(self.three.start)
        pl.when(self.end&(self.head==to^2))(self.two.start)
        pl.when(self.head==to^1)(self.one.start)

    def begin_all(self):
        @pl.when(self.end)
        def _():
            self.zero.start()
            self.two.start()
            self.one.start()
        @pl.when(~self.end)
        def _():
            self.three.start()
            self.one.start()
        return self

    def onward(self):
        @pl.when(~self.end)
        def _():
            self.zero.wait_recv()
            self.far[...]=summed(self.far,self.relay).astype(bf16)
            self.two.start()

    def wait(self):
        pl.when(self.end)(self.zero.wait_send)
        pl.when(~self.end)(self.three.wait)
        self.one.wait()
        self.two.wait()


def wait_all(copies):
    for c in copies: c.wait()


def block_of(index, size):
    return pl.ds(pl.multiple_of(index*size,size),size)


def summed(*refs):
    total=refs[0][...].astype(f32)
    for r in refs[1:]: total=total+r[...].astype(f32)
    return total


NAMES=("ada","qkv","out","up","down")


def scratch(rows):
    part=rows//4
    return dict(
        e=((5,rows,rows),bf16),m=((rows,128),f32),l=((rows,128),f32),att=((rows,128),f32),fac=((rows,128),f32),
        queries=((rows,128),bf16),table=((5,rows,384),bf16),xn_one=((rows,512),bf16),
        qkv_full=((512,384),bf16),out_full=((4,128,512),bf16),up_full=((512,2048),bf16),down_full=((4,512,512),bf16),
        modp=((8,1024),f32),modbuf=((8,8,1024),f32),modulation=((8,1024),f32),
        mixed=((rows,128),bf16),heads=((part,512),bf16),do=((rows,128),bf16),do_rows=((part,512),bf16),
        act=((part,2048),bf16),pre=((part,2048),bf16),dy=((part,512),f32),
        up_grad=((4,2,64,2048),bf16),down_grad=((4,4,2,64,512),bf16),out_grad=((4,4,2,16,512),bf16),
        dq=((rows,128),f32),dkv=((256,rows),f32),near=((5,256,rows),bf16),
        got_pair=((256,rows),bf16),got_y=((256,rows),bf16),got_x=((256,rows),bf16),got_one=((256,rows),bf16),
        proj_grad=((rows,384),bf16),partial=((4,part,512),bf16),got_partial=((3,part,512),bf16),normed=((rows,512),f32),
        up1=((4,64,2048),bf16),down1=((4,4,64,512),bf16),out1=((4,4,16,512),bf16),
        up2=((2,64,2048),bf16),down2=((4,2,64,512),bf16),out2=((4,2,16,512),bf16),
        up3=((64,2048),bf16),down3=((4,64,512),bf16),out3=((4,16,512),bf16),
        up_z=((3,64,512),bf16),down_z=((3,64,512),bf16),out_z=((3,16,512),bf16),
        up_relay=((64,512),bf16),down_relay=((64,512),bf16),out_relay=((16,512),bf16),relay=((part,512),bf16),
        qkv_grad=((8,64,384),bf16),qkv_got=((7,64,384),bf16),dm_own=((8,1024),f32),dm_z=((4,8,1024),f32),dm_n=((8,8,1024),f32),
    )


class Bag:
    pass


COPIES=150


def layer_kernel(scale, names, *refs):
    refs=list(refs)
    take=lambda n: [refs.pop(0) for _ in range(n)]
    node_input,cotangent,sigma,code,counts=take(5)
    w={n:refs.pop(0) for n in NAMES}
    node_output,row_all,qkv_sum,out_sum,up_sum,down_sum,mod_sum=take(7)
    k=Bag()
    for n in names: setattr(k,n,refs.pop(0))
    send,recv=take(2)
    head=lax.axis_index("head"); node=lax.axis_index("node")
    y_at=node//4; x_at=(node//2)%2; core=node%2
    rows=node_input.shape[0]
    part=rows//4
    links=Links(send,recv)
    go=links.go
    normed=k.normed
    quarter=[slice(i*part,(i+1)*part) for i in range(4)]
    limits=(counts[0],counts[0]+counts[1],counts[0]+counts[1]+counts[2])
    mine=block_of(head,part)
    head_cols=block_of(head,512)
    own_pos=node*rows+head*part+lax.broadcasted_iota(jnp.int32,(part,1),0)

    own=block_of(node,64); own_out=block_of(node,16)
    k.qkv_full[own,:]=w["qkv"][...].astype(bf16)
    sig=sigma[:,0:64]
    for i in range(1,8): sig=jnp.where(node==i,sigma[:,i*64:(i+1)*64],sig)
    made=jnp.dot(sig,w["ada"][...].astype(bf16),preferred_element_type=f32)
    k.modp[0:4,:]=made[:,:1024]
    k.modp[4:8,:]=made[:,1024:]
    k.up_full[own,head_cols]=w["up"][...].astype(bf16)
    k.down_full[head,own,:]=w["down"][...].astype(bf16)
    k.out_full[head,own_out,:]=w["out"][...].astype(bf16)
    meet([(head,node^i) for i in range(1,8)]+[(head^i,node) for i in range(1,4)])
    first=[]
    for i in range(1,8):
        first.append(go(k.modp,k.modbuf.at[node],head,node^i))
        first.append(go(k.qkv_full.at[own],k.qkv_full.at[own],head,node^i))
    along=[]
    for place in (lambda h: k.up_full.at[own,block_of(h,512)],lambda h: k.down_full.at[h,own],lambda h: k.out_full.at[h,own_out]):
        along.append(Shown(links,head,node,place))
    k.modbuf[node,:,:]=k.modp[...]
    for b in range(5): k.table[b,:,256:384]=jnp.ones((rows,128),bf16)
    def norm(i,_):
        at=block_of(i,256)
        v=node_input[at,:].astype(f32)
        centred=v-jnp.mean(v,axis=1,keepdims=True)
        normed[at,:]=centred*lax.rsqrt(jnp.mean(centred*centred,axis=1,keepdims=True)+norm_eps)
        return 0
    lax.fori_loop(0,rows//256,norm,0)
    groups=code.shape[0]
    half=groups//2
    count_groups(k.e,code,rows,0,half,4)
    for a in along: a.onward()
    def column(which):
        at=block_of(node^which,64)
        return [k.up_full.at[at],k.down_full.at[:,at],k.out_full.at[:,block_of(node^which,16)]]
    own_column=column(0); from_x=column(2); from_y=column(4)
    along[0].wait()
    up_x=go(own_column[0],own_column[0],head,node^2)
    wait_all(first)
    mod=k.modbuf[0]
    for i in range(1,8): mod=mod+k.modbuf[i]
    k.modulation[...]=mod

    kv=slice(0,256)
    across=[]; paired=[]
    for at in quarter:
        pos=node*rows+at.start+lax.broadcasted_iota(jnp.int32,(part,1),0)
        xn=(normed[at,:]*(1.0+by_batch(pos,limits,k.modulation,0,slice(0,512)))+by_batch(pos,limits,k.modulation,0,slice(512,1024))).astype(bf16)
        k.xn_one[at,:]=xn
        proj=jnp.dot(xn,k.qkv_full[...],preferred_element_type=f32).astype(bf16)
        k.queries[at,:]=proj[:,:128]
        k.table[0,at,kv]=proj[:,128:]
        across.append(go(k.table.at[0,at,kv],k.table.at[2,at,kv],head,node^2))
        paired.append(go(k.table.at[0,at,kv],k.table.at[1,at,kv],head,node^1))
    wait_all(along[1:])
    rest_y=[go(r,r,head,node^4) for r in own_column[1:]]
    count_groups(k.e,code,rows,half,groups,4)
    add_self(k.e,0,rows)

    onward=[]
    def pass_keys(i):
        at=quarter[i]
        across[i].wait_recv()
        onward.append(go(k.table.at[2,at,kv],k.table.at[3,at,kv],head,node^4))
    def attend(b,at):
        attend_rows(b,b==0,at,part,k.queries,k.table,k.e,k.m,k.l,k.att,k.fac,scale*math.log2(math.e))
    def attend_all(b):
        def two(i,_):
            for u in range(2): attend(b,block_of(2*i+u,part))
            return 0
        lax.fori_loop(0,2,two,0)
    pass_keys(0)
    attend_all(0)
    pass_keys(1)
    wait_all(paired)
    attend_all(1)
    pass_keys(2)
    pass_keys(3)
    up_y=go(own_column[0],own_column[0],head,node^4)
    rest_x=[go(r,r,head,node^2) for r in own_column[1:]]
    to_pair=[go(r,r,head,node^1) for r in own_column]
    up_x.wait()
    wait_all(rest_y)
    cross=[go(from_x[0],from_x[0],head,node^4)]+[go(r,r,head,node^2) for r in from_y[1:]]
    hand=[go(r,r,head,node^1) for r in from_x[:1]+from_y[1:]]
    attend_all(2)
    wait_all(onward)
    fifth=go(k.table.at[jnp.where(x_at==core,2,3),:,kv],k.table.at[4,:,kv],head,node^1)
    for at in quarter: attend(3,at)
    fifth.wait()
    lanes=block_of(head,128)
    moved=[]
    for i in range(4):
        at=quarter[i]
        attend(4,at)
        inv=1.0/k.l[at,:]
        o=k.att[at,:]*inv
        k.att[at,:]=o
        k.fac[at,:]=jnp.exp2(k.fac[at,:]-k.m[at,:])*inv
        k.mixed[at,:]=o.astype(bf16)
    for i in range(1,4):
        moved.append(go(k.mixed.at[block_of(head^i,part)],k.heads.at[:,lanes],head^i,node))
    k.heads[:,lanes]=k.mixed[mine,:]
    for c in across: c.wait_send()
    up_y.wait()
    wait_all(rest_x)
    hand+=[go(r,r,head,node^1) for r in from_y[:1]+from_x[1:]]
    wait_all(cross)
    last=[go(r,r,head,node^1) for r in column(6)]
    scale_two=1.0+by_batch(own_pos,limits,k.modulation,4,slice(0,512))
    shift_two=by_batch(own_pos,limits,k.modulation,4,slice(512,1024))
    g=cotangent[mine,:]
    wait_all(moved)
    wait_all(to_pair+hand+last)

    out_all=k.out_full[...].reshape(512,512)
    y=node_input[mine,:].astype(f32)+jnp.dot(k.heads[...],out_all,preferred_element_type=f32)
    n_two,inv_two=norm_parts(y)
    xn=(n_two*scale_two+shift_two).astype(bf16)
    mlp=jnp.zeros((part,512),f32); dxn=jnp.zeros((part,512),f32)
    for j in range(4):
        s=slice(j*512,(j+1)*512)
        h=jnp.dot(xn,k.up_full[:,s],preferred_element_type=f32)
        gate=1.0/(1.0+jnp.exp(-h))
        u=(h*gate).astype(bf16)
        k.act[:,s]=u
        mlp+=jnp.dot(u,k.down_full[j],preferred_element_type=f32)
        du=lax.dot_general(g,k.down_full[j],NT,preferred_element_type=f32)
        d=(du*gate*(1.0+h*(1.0-gate))).astype(bf16)
        k.pre[:,s]=d
        dxn+=lax.dot_general(d,k.up_full[:,s],NT,preferred_element_type=f32)
    dyv=g.astype(f32)+norm_back(dxn*scale_two,n_two,inv_two)
    k.dy[...]=dyv
    da=dyv.astype(bf16)
    k.do_rows[...]=lax.dot_general(da,out_all,NT,preferred_element_type=f32).astype(bf16)
    returned=[]
    for i in range(1,4):
        returned.append(go(k.do_rows.at[:,block_of(head^i,128)],k.do.at[mine],head^i,node))
    k.do[mine,:]=k.do_rows[:,lanes]
    node_output[mine,:]=(y+mlp).astype(bf16)
    xn_t=xn.T
    heads_t=k.heads[...].T
    k.out_grad[...]=jnp.dot(heads_t,da,preferred_element_type=f32).astype(bf16).reshape(4,4,2,16,512)
    for j in range(4):
        s=slice(j*512,(j+1)*512)
        k.up_grad[:,:,:,s]=jnp.dot(xn_t,k.pre[:,s],preferred_element_type=f32).astype(bf16).reshape(4,2,64,512)
        k.down_grad[j]=jnp.dot(k.act[:,s].T,g,preferred_element_type=f32).astype(bf16).reshape(4,2,64,512)
    stage1=[go(k.up_grad.at[:,1-core],k.up1,head,node^1),go(k.down_grad.at[:,:,1-core],k.down1,head,node^1),go(k.out_grad.at[:,:,1-core],k.out1,head,node^1)]
    k.dm_own[4:8,0:512]=batch_sums(own_pos,limits,dxn*n_two)
    k.dm_own[4:8,512:1024]=batch_sums(own_pos,limits,dxn)
    wait_all(returned)
    shown=Shown(links,head,node,lambda h: node_output.at[block_of(h,part)])

    q_t=k.queries[...].T
    dof=k.do[...].astype(f32)
    delta=jnp.sum(dof*k.att[...],axis=1,keepdims=True)
    def block(b):
        def write(r,s,v):
            if b==0: k.dkv[r,s]=v
            else: k.near[b,r,s]=v.astype(bf16)
        back_block(b,q_t,dof,k.fac,delta,k.table,k.e,k.dq,write,b==4,512,scale)
    near=k.near
    block(4)
    give=go(near.at[4],k.got_pair,head,node^1)
    block(3)
    give.wait()
    @pl.when(x_at!=core)
    def _(): near[3]=summed(near[3],k.got_pair[...]).astype(bf16)
    order=(0,3,1,2)
    via_y={i:go(near.at[3,:,quarter[i]],k.got_y.at[:,quarter[i]],head,node^4) for i in order}
    block(2)
    @pl.when(x_at==core)
    def _(): near[2]=summed(near[2],k.got_pair[...]).astype(bf16)
    via_x={}
    def pass_on(i):
        i=order[i]
        s=quarter[i]
        via_y[i].wait()
        near[2,:,s]=summed(near[2,:,s],k.got_y[:,s]).astype(bf16)
        via_x[i]=go(near.at[2,:,s],k.got_x.at[:,s],head,node^2)
    pass_on(0)
    shown.onward()
    block(1)
    one=go(near.at[1],k.got_one,head,node^1)
    pass_on(1)
    block(0)
    wait_all(stage1)
    for i in range(4):
        k.down1[i]=summed(k.down1[i],k.down_grad[i,:,core]).astype(bf16)
        k.out1[i]=summed(k.out1[i],k.out_grad[i,:,core]).astype(bf16)
    there=pl.ds((1-y_at)*2,2)
    stage2=[go(k.down1.at[:,there],k.down2,head,node^4),go(k.out1.at[:,there],k.out2,head,node^4)]
    pass_on(2)
    one.wait()
    reduce=Added(links,head,node,lambda h: k.partial.at[h],lambda i: k.got_partial.at[i],k.relay)
    def finish_rows(i):
        i=order[i]
        s=quarter[i]
        via_x[i].wait()
        total=k.dkv[:,s]+k.got_one[:,s].astype(f32)+k.got_x[:,s].astype(f32)
        k.proj_grad[s,128:]=total.T.astype(bf16)
        k.proj_grad[s,:128]=(k.dq[s,:]*scale).astype(bf16)
        k.partial[i]=lax.dot_general(k.proj_grad[s,:],k.qkv_full[...],NT,preferred_element_type=f32).astype(bf16)
        reduce.begin(i)
    finish_rows(0)
    pass_on(3)
    for i in range(4):
        k.up1[i]=summed(k.up1[i],k.up_grad[i,core]).astype(bf16)
    stage2+=[go(k.up1.at[i*2+1-x_at],k.up2.at[i],head,node^2) for i in range(2)]
    for i in range(1,4): finish_rows(i)
    xn_t=k.xn_one[...].T
    k.qkv_grad[...]=jnp.dot(xn_t,k.proj_grad[...],preferred_element_type=f32).astype(bf16).reshape(8,64,384)
    qkv_moves=[go(k.qkv_grad.at[node^i],k.qkv_got.at[i-1],head,node^i) for i in range(1,8)]
    reduce.onward()
    wait_all(stage2)
    for i in range(2):
        k.up2[i]=summed(k.up2[i],k.up1[i*2+x_at]).astype(bf16)
    here=pl.ds(y_at*2,2)
    k.down2[...]=summed(k.down2[...],k.down1[:,here]).astype(bf16)
    k.out2[...]=summed(k.out2[...],k.out1[:,here]).astype(bf16)
    stage3=[go(k.up2.at[1-y_at],k.up3,head,node^4),go(k.down2.at[:,1-x_at],k.down3,head,node^2),go(k.out2.at[:,1-x_at],k.out3,head,node^2)]
    scale_one=1.0+by_batch(own_pos,limits,k.modulation,0,slice(0,512))
    n_one,inv_one=norm_parts(node_input[mine,:].astype(f32))
    reduce.wait()
    dxn=summed(k.partial.at[head],*[k.got_partial.at[i] for i in range(3)])
    k.dm_own[0:4,0:512]=batch_sums(own_pos,limits,dxn*n_one)
    k.dm_own[0:4,512:1024]=batch_sums(own_pos,limits,dxn)
    dm_moves=[go(k.dm_own,k.dm_z.at[head],head^i,node) for i in range(1,4)]
    row_all[head,:,:]=(k.dy[...]+norm_back(dxn*scale_one,n_one,inv_one)).astype(bf16)
    spread=Shown(links,head,node,lambda h: row_all.at[h])
    wait_all(qkv_moves)
    qkv_sum[...]=summed(k.qkv_grad[node],*[k.qkv_got[i] for i in range(7)])
    wait_all(stage3)
    k.up3[...]=summed(k.up3[...],k.up2[y_at]).astype(bf16)
    k.down3[...]=summed(k.down3[...],k.down2[:,x_at]).astype(bf16)
    k.out3[...]=summed(k.out3[...],k.out2[:,x_at]).astype(bf16)
    stage4=[Added(links,head,node,lambda h: k.up3.at[:,block_of(h,512)],lambda i: k.up_z.at[i],k.up_relay).begin_all(),
        Added(links,head,node,lambda h: k.down3.at[h],lambda i: k.down_z.at[i],k.down_relay).begin_all(),
        Added(links,head,node,lambda h: k.out3.at[h],lambda i: k.out_z.at[i],k.out_relay).begin_all()]
    spread.onward()
    for s in stage4: s.onward()
    k.dm_z[head,:,:]=k.dm_own[...]
    wait_all(dm_moves)
    k.modp[...]=k.dm_z[0]+k.dm_z[1]+k.dm_z[2]+k.dm_z[3]
    dm_last=[go(k.modp,k.dm_n.at[node],head,node^i) for i in range(1,8)]
    k.dm_n[node,:,:]=k.modp[...]
    wait_all(dm_last)
    total=k.dm_n[0]
    for i in range(1,8): total=total+k.dm_n[i]
    mod_sum[...]=total
    wait_all(stage4)
    up_sum[...]=summed(k.up3[:,head_cols],*[k.up_z[i] for i in range(3)])
    down_sum[...]=summed(k.down3[head],*[k.down_z[i] for i in range(3)])
    out_sum[...]=summed(k.out3[head],*[k.out_z[i] for i in range(3)])
    spread.wait()
    shown.wait()


def finish_kernel(sigma, step_count, *refs):
    sources=refs[:22]; results=refs[22:39]; held=refs[39:62]; load,store=refs[62:]
    loads=[pltpu.make_async_copy(sources[i],held[i],load.at[i]) for i in range(22)]
    for i in (0,1)+tuple(range(7,22))+tuple(range(2,7)): loads[i].start()
    node=lax.axis_index("node")
    stores=[]
    def keep(ref, result):
        stores.append(pltpu.make_async_copy(ref,results[result],store.at[result])); stores[-1].start()
    loads[0].wait()
    keep(held[0],0)
    loads[1].wait()
    wide=held[22]
    rows=wide.shape[0]
    for i in range(4): wide[i*rows//4:(i+1)*rows//4,:]=held[1][i].astype(f32)
    keep(wide,1)
    count=jnp.full((8,128),step_count[0],jnp.int32).astype(f32)
    correct=(1.0-jnp.exp2(-count))[0:1,0:1]
    sig=sigma[:,0:64]
    for i in range(1,8): sig=jnp.where(node==i,sigma[:,i*64:(i+1)*64],sig)
    rates=((4*COND)**-0.5,(WIDTH//2)**-0.5,(WIDTH//4)**-0.5,WIDTH**-0.5,HIDDEN_SIZE**-0.5)
    for w in (0,3,4,1,2):
        at=7+3*w
        for i in range(3): loads[at+i].wait()
        if w==0:
            loads[6].wait()
            total=held[6]
            batch_grad=jnp.concatenate([total[0:4,:],total[4:8,:]],axis=1)
            grad=lax.dot_general(sig.astype(f32),batch_grad,(((0,),(0,)),((),())),precision=highest,preferred_element_type=f32)
        else:
            loads[1+w].wait()
            grad=held[1+w][...]
        master,first,second=held[at:at+3]
        first_new=beta_rate*first[...]+(1.0-beta_rate)*grad
        second_new=beta_rate*second[...]+(1.0-beta_rate)*grad*grad
        step=first_new/correct/(jnp.sqrt(second_new/correct)+adam_eps)
        old=master[...]
        master[...]=old-rates[w]*(step+weight_decay*old)
        first[...]=first_new
        second[...]=second_new
        for i in range(3): keep(held[at+i],2+3*w+i)
    for c in stores: c.wait()


def slots(neighbours, valid, node, rows):
    which=(neighbours//rows)^node
    slot=jnp.where(which==6,3,jnp.where((which==3)|(which==7),4,which))
    local=neighbours%rows
    spot=lax.broadcasted_iota(jnp.int32,neighbours.shape,0)%16
    hi=(slot*(rows//SPAN)+local//SPAN)*16+spot
    return jnp.where(valid>0,hi*256+local%SPAN,-1).reshape(-1,256)


def per_device_near(
    node_input, cotangent, sigma_embed, neighbours, neighbour_valid, batch_counts, step_count,
    ada_master, ada_first, ada_second, qkv_master, qkv_first, qkv_second, out_master, out_first, out_second,
    up_master, up_first, up_second, down_master, down_first, down_second,
):
    rows=node_input.shape[0]
    code=slots(neighbours,neighbour_valid,lax.axis_index("node"),rows)
    masters=(ada_master,qkv_master,out_master,up_master,down_master)
    firsts=(ada_first,qkv_first,out_first,up_first,down_first)
    seconds=(ada_second,qkv_second,out_second,up_second,down_second)
    V=pltpu.VMEM
    full=pl.BlockSpec(memory_space=V); few=pl.BlockSpec(memory_space=pltpu.SMEM); hbm=pl.BlockSpec(memory_space=pltpu.HBM)
    S=jax.ShapeDtypeStruct
    held=scratch(rows)
    sums=pl.pallas_call(functools.partial(layer_kernel,128**-0.5,tuple(held)),
        out_shape=(S((rows,512),bf16),S((4,rows//4,512),bf16))+tuple(S(a.shape,f32) for a in masters[1:])+(S((8,1024),f32),),
        in_specs=[full]*4+[few]+[full]*5,
        out_specs=(full,)*7,
        scratch_shapes=[V(*v) for v in held.values()]+[pltpu.SemaphoreType.DMA((COPIES,))]*2,
        compiler_params=pltpu.CompilerParams(vmem_limit_bytes=67043328,collective_id=1,has_side_effects=True),
        name="layer")(node_input,cotangent,sigma_embed,code,batch_counts,*masters)
    news=tuple(S(a.shape,f32) for a in masters for _ in range(3))
    inner=[V(a.shape,a.dtype) for a in sums]+[V(a.shape,f32) for a in masters for _ in range(3)]+[V((rows,512),f32)]
    return pl.pallas_call(finish_kernel,
        out_shape=(S((rows,512),bf16),S((rows,512),f32))+news,
        in_specs=[full,few]+[hbm]*(7+15),
        out_specs=(hbm,)*17,
        scratch_shapes=inner+[pltpu.SemaphoreType.DMA((22,)),pltpu.SemaphoreType.DMA((17,))],
        compiler_params=pltpu.CompilerParams(vmem_limit_bytes=67043328),
        name="finish")(sigma_embed,step_count,*sums,*[a for three in zip(masters,firsts,seconds) for a in three])


def wide_count_groups(cnt, hik, lok, rows):
    steps=hik.shape[0]
    parts=rows//SPAN
    total=5*parts*16
    rowid=lax.broadcasted_iota(jnp.int32,(total,1),0)
    rowkey=lax.div(rowid,16)*16+lax.rem(rowid,16)
    spot=lax.broadcasted_iota(jnp.int32,(SPAN,1),0)
    def body(g,_):
        keys=hik[pl.ds(g,1),:]
        low=lok[pl.ds(g,1),:]
        left=jnp.where(rowkey==keys,1.0,0.0).astype(bf16)
        right=jnp.where(spot==low,1.0,0.0).astype(bf16)
        made=lax.dot_general(left,right,NT,preferred_element_type=f32).astype(bf16)
        at=pl.multiple_of(g*16,16)
        for b in range(5):
            for p in range(parts):
                r=(b*parts+p)*16
                cnt[b,pl.ds(at,16),p*SPAN:(p+1)*SPAN]=made[r:r+16,:]
        return 0
    lax.fori_loop(0,steps,body,0)

def wide_add_self(cnt, block, rows):
    eye=(lax.broadcasted_iota(jnp.int32,(SPAN,SPAN),0)==lax.broadcasted_iota(jnp.int32,(SPAN,SPAN),1))
    one=jnp.where(eye,1.0,0.0).astype(bf16)
    for p in range(rows//SPAN):
        s=slice(p*SPAN,(p+1)*SPAN)
        cnt[block,s,s]=cnt[block,s,s]+one

def wide_attend_block(b, first, q, keys, vals, cnt, e, m, l, acc, fac, chunk, scale):
    rows=q.shape[0]
    lane=lax.broadcasted_iota(jnp.int32,(chunk,128),1)
    def body(i,_):
        at=pl.ds(pl.multiple_of(i*chunk,chunk),chunk)
        s=lax.dot_general(q[at,:],keys,NT,preferred_element_type=f32)*scale
        c=cnt[b,at,:].astype(f32)
        s=jnp.where(c>0,s,-1e30)
        top=jnp.max(s,axis=1,keepdims=True)
        if not first:
            old=m[at,0:1]
            top=jnp.maximum(top,old)
        w=(jnp.exp2(s-top)*c)
        total=jnp.sum(w,axis=1,keepdims=True)
        w=w.astype(bf16)
        e[b,at,:]=w
        out=jnp.dot(w,vals,preferred_element_type=f32)
        if first:
            acc[at,:]=out; l[at,:]=jnp.broadcast_to(total,(chunk,128))
            fac[at,:]=jnp.where(lane==b,top,0.0)
        else:
            shrink=jnp.exp2(old-top)
            acc[at,:]=acc[at,:]*shrink+out
            l[at,:]=l[at,:]*shrink+total
            fac[at,:]=jnp.where(lane==b,top,fac[at,:])
        m[at,:]=jnp.broadcast_to(top,(chunk,128))
        return 0
    lax.fori_loop(0,rows//chunk,body,0)

def wide_fwd_kernel(order, self_block, scale, q, kv, hik, lok, att, e, fac, cnt, m, l):
    rows=q.shape[0]
    wide_count_groups(cnt,hik,lok,rows)
    wide_add_self(cnt,self_block,rows)
    for t,b in enumerate(order):
        wide_attend_block(b,t==0,q,kv[b,:,:128],kv[b,:,128:],cnt,e,m,l,att,fac,256,scale)
    inv=1.0/l[...]
    att[...]=att[...]*inv
    fac[...]=jnp.exp2(fac[...]-m[...])*inv

def wide_attention_fwd(q,kv,hik,lok,scale):
    rows=q.shape[0]
    V=pltpu.VMEM
    full=pl.BlockSpec(memory_space=V)
    return pl.pallas_call(functools.partial(wide_fwd_kernel,(2,1,3,0,4),2,scale*math.log2(math.e)),
        out_shape=(jax.ShapeDtypeStruct((rows,128),f32),jax.ShapeDtypeStruct((5,rows,rows),bf16),jax.ShapeDtypeStruct((rows,128),f32)),
        in_specs=[full]*4,out_specs=(full,)*3,
        scratch_shapes=[V((5,rows,rows),bf16),V((rows,128),f32),V((rows,128),f32)],
        compiler_params=pltpu.CompilerParams(vmem_limit_bytes=60<<20),name="attend_fwd")(q,kv,hik,lok)

def wide_back_block(b, q_t, do, fac, delta, kv, e, dq, dkv, first, chunk, keyscale):
    rows=do.shape[0]
    f=fac[:,b:b+1]
    dob=(do*f)
    dobh=dob.astype(bf16)
    d=-(delta*f)
    h=d.astype(bf16); r=d-h.astype(f32); h2=r.astype(bf16); h3=(r-h2.astype(f32)).astype(bf16)
    lane=lax.broadcasted_iota(jnp.int32,(rows,128),1)
    zero=jnp.zeros((rows,128),bf16)
    dcol=jnp.where(lane==0,h.astype(f32),jnp.where(lane==1,h2.astype(f32),jnp.where(lane==2,h3.astype(f32),0.0))).astype(bf16)
    left=jnp.concatenate([dobh,dcol],axis=1)
    dob_t=dobh.T
    ones=jnp.ones((chunk,128),bf16)
    for i in range(kv.shape[1]//chunk):
        s=slice(i*chunk,(i+1)*chunk)
        right=jnp.concatenate([kv[b,s,128:],ones],axis=1)
        dp=lax.dot_general(left,right,NT,preferred_element_type=f32)
        w=e[b,:,s]
        ds=(dp*w.astype(f32)).astype(bf16)
        dkv[b,:128,s]=jnp.dot(q_t,ds,preferred_element_type=f32)*keyscale
        dkv[b,128:,s]=jnp.dot(dob_t,w,preferred_element_type=f32)
        out=jnp.dot(ds,kv[b,s,:128],preferred_element_type=f32)
        if first and i==0: dq[...]=out
        else: dq[...]+=out

def wide_bwd_kernel(scale, q, do, att, fac, kv, e, dq, dkv, ):
    q_t=q[...].T
    dof=do[...].astype(f32)
    delta=jnp.sum(dof*att[...],axis=1,keepdims=True)
    for t,b in enumerate((0,4,1,3,2)):
        wide_back_block(b,q_t,dof,fac,delta,kv,e,dq,dkv,t==0,512,scale)
    dq[...]=dq[...]*scale

def wide_attention_bwd(q,do,att,fac,kv,e,scale):
    rows=q.shape[0]
    V=pltpu.VMEM
    full=pl.BlockSpec(memory_space=V)
    return pl.pallas_call(functools.partial(wide_bwd_kernel,scale),
        out_shape=(jax.ShapeDtypeStruct((rows,128),f32),jax.ShapeDtypeStruct((5,256,rows),f32)),
        in_specs=[full]*6,out_specs=(full,)*2,
        compiler_params=pltpu.CompilerParams(vmem_limit_bytes=60<<20),name="attend_bwd")(q,do,att,fac,kv,e)

def wide_tables(slot_index, valid, rows):
    parts=rows//SPAN
    flat=slot_index.reshape(-1,256)
    ok=(valid>0).reshape(-1,256)
    node=lax.broadcasted_iota(jnp.int32,flat.shape,1)//16
    hi=jnp.where(ok,(flat//SPAN)*16+node,-1)
    lo=flat%SPAN
    return hi,lo


def per_device(
    node_input,
    cotangent,
    sigma_embed,
    neighbours,
    neighbour_valid,
    batch_counts,
    step_count,
    ada_master,
    ada_first,
    ada_second,
    qkv_master,
    qkv_first,
    qkv_second,
    out_master,
    out_first,
    out_second,
    up_master,
    up_first,
    up_second,
    down_master,
    down_first,
    down_second,
):
    f32 = jnp.float32
    bf16 = jnp.bfloat16
    node_rows = node_input.shape[0]
    model_width = node_input.shape[1]
    head_dim = qkv_master.shape[1] // 3
    score_scale = head_dim ** (-0.5)
    node_index = lax.axis_index("node")
    total_nodes = node_rows * lax.axis_size("node")
    qkv_full, out_full, up_full, down_full = (
        lax.all_gather(qkv_master.astype(bf16), "node", axis=0, tiled=True),
        lax.all_gather(out_master.astype(bf16), "node", axis=0, tiled=True),
        lax.all_gather(up_master.astype(bf16), "node", axis=0, tiled=True),
        lax.all_gather(down_master.astype(bf16), "node", axis=0, tiled=True),
    )
    cond_rows = ada_master.shape[0]
    sigma_part = lax.dynamic_slice_in_dim(sigma_embed, node_index * cond_rows, cond_rows, 1)
    limits = jnp.cumsum(batch_counts)[:-1]
    positions = node_index * node_rows + jnp.arange(node_rows, dtype=jnp.int32)
    member = jnp.sum((positions[:, None] >= limits[None, :]).astype(jnp.int32), axis=1)
    onehot = (
        member[:, None] == jnp.arange(batch_counts.shape[0], dtype=jnp.int32)[None, :]
    ).astype(f32)
    modulation = lax.psum(
        jnp.dot(sigma_part, ada_master.astype(bf16), preferred_element_type=f32), "node"
    )
    per_node = jnp.dot(onehot, modulation, precision=highest)
    scale_one = per_node[:, :model_width]
    shift_one = per_node[:, model_width : 2 * model_width]
    scale_two = per_node[:, 2 * model_width : 3 * model_width]
    shift_two = per_node[:, 3 * model_width :]
    normed_one, inverse_one = norm_parts(node_input.astype(f32))
    xn_one = (normed_one * (1.0 + scale_one) + shift_one).astype(bf16)
    projected = jnp.dot(xn_one, qkv_full, preferred_element_type=f32).astype(bf16)
    queries = projected[:, :head_dim]
    keys_values = projected[:, head_dim:]
    offsets = (-2, -1, 1, 2)
    fetched = {0: keys_values}
    for offset in offsets:
        fetched[offset] = passed_along(keys_values, "node", -offset)
    table = jnp.stack([fetched[offset] for offset in (-2, -1, 0, 1, 2)], axis=0)
    slot_index = jnp.mod(neighbours - (node_index - 2) * node_rows, total_nodes)
    high_keys, low_keys = wide_tables(slot_index, neighbour_valid, node_rows)
    mixed, weights, factors = wide_attention_fwd(queries, table, high_keys, low_keys, score_scale)
    heads_out = mixed.astype(bf16)
    branch = lax.psum(
        jnp.dot(heads_out, out_full, preferred_element_type=f32).astype(jnp.bfloat16), "head"
    ).astype(jnp.float32)
    middle = node_input.astype(f32) + branch
    normed_two, inverse_two = norm_parts(middle)
    xn_two = (normed_two * (1.0 + scale_two) + shift_two).astype(bf16)
    hidden_pre = jnp.dot(xn_two, up_full, preferred_element_type=f32)
    gate_sig = jax.nn.sigmoid(hidden_pre)
    activated = (hidden_pre * gate_sig).astype(bf16)
    mlp_sum = lax.psum(
        jnp.dot(activated, down_full, preferred_element_type=f32).astype(jnp.bfloat16), "head"
    ).astype(jnp.float32)
    node_output = (middle + mlp_sum).astype(bf16)
    down_grad = jnp.einsum("nf,nd->fd", activated, cotangent, preferred_element_type=f32)
    act_grad = jnp.einsum("nd,fd->nf", cotangent, down_full, preferred_element_type=f32)
    pre_grad = (act_grad * gate_sig * (1.0 + hidden_pre * (1.0 - gate_sig))).astype(bf16)
    up_grad = jnp.einsum("nw,nf->wf", xn_two, pre_grad, preferred_element_type=f32)
    normed_two_grad = lax.psum(
        jnp.einsum("nf,wf->nw", pre_grad, up_full, preferred_element_type=f32).astype(jnp.bfloat16),
        "head",
    ).astype(jnp.float32)
    middle_grad = cotangent.astype(f32) + norm_back(
        normed_two_grad * (1.0 + scale_two), normed_two, inverse_two
    )
    branch_grad = middle_grad.astype(bf16)
    out_grad = jnp.einsum("nh,nd->hd", heads_out, branch_grad, preferred_element_type=f32)
    mixed_grad = jnp.einsum("nd,hd->nh", branch_grad, out_full, preferred_element_type=f32).astype(
        bf16
    )
    query_grad, pair_sums = wide_attention_bwd(
        queries, mixed_grad, mixed, factors, table, weights, score_scale
    )
    remote_terms = pair_sums[2]
    for offset in offsets:
        remote_terms = remote_terms + passed_along(
            pair_sums[offset + 2].astype(bf16), "node", offset
        ).astype(f32)
    key_value_grad = remote_terms.T
    projected_grad = jnp.concatenate([query_grad, key_value_grad], axis=1).astype(bf16)
    qkv_grad = jnp.einsum("nw,nc->wc", xn_one, projected_grad, preferred_element_type=f32)
    normed_one_grad = lax.psum(
        jnp.einsum("nc,wc->nw", projected_grad, qkv_full, preferred_element_type=f32).astype(
            jnp.bfloat16
        ),
        "head",
    ).astype(jnp.float32)
    input_grad = middle_grad + norm_back(
        normed_one_grad * (1.0 + scale_one), normed_one, inverse_one
    )
    rows_grad = jnp.concatenate(
        [
            normed_one_grad * normed_one,
            normed_one_grad,
            normed_two_grad * normed_two,
            normed_two_grad,
        ],
        axis=1,
    )
    batch_grad = jnp.dot(onehot.T, rows_grad, precision=highest)
    batch_grad = lax.psum(batch_grad, "node")
    ada_sum = jnp.dot(sigma_part.astype(f32).T, batch_grad, precision=highest)
    qkv_sum, out_sum, up_sum, down_sum = (
        lax.psum_scatter(qkv_grad, "node", scatter_dimension=0, tiled=True),
        lax.psum_scatter(out_grad, "node", scatter_dimension=0, tiled=True),
        lax.psum_scatter(up_grad, "node", scatter_dimension=0, tiled=True),
        lax.psum_scatter(down_grad, "node", scatter_dimension=0, tiled=True),
    )
    count_value = step_count[0].astype(f32)
    ada_res = adamw_update(
        ada_master, ada_first, ada_second, ada_sum, (4 * COND) ** (-0.5), count_value
    )
    qkv_res = adamw_update(
        qkv_master, qkv_first, qkv_second, qkv_sum, (WIDTH // 2) ** (-0.5), count_value
    )
    out_res = adamw_update(
        out_master, out_first, out_second, out_sum, (WIDTH // 4) ** (-0.5), count_value
    )
    up_res = adamw_update(up_master, up_first, up_second, up_sum, WIDTH ** (-0.5), count_value)
    down_res = adamw_update(
        down_master, down_first, down_second, down_sum, HIDDEN_SIZE ** (-0.5), count_value
    )
    return (
        node_output,
        input_grad,
        ada_res[0],
        ada_res[1],
        ada_res[2],
        qkv_res[0],
        qkv_res[1],
        qkv_res[2],
        out_res[0],
        out_res[1],
        out_res[2],
        up_res[0],
        up_res[1],
        up_res[2],
        down_res[0],
        down_res[1],
        down_res[2],
    )


def solution(mesh):
    chosen = per_device_near if mesh.shape["node"] == 8 and mesh.shape["head"] == 4 else per_device
    placed = (
        P("node", None),
        P("node", None),
        P(),
        P("node", None),
        P("node", None),
        P(),
        P(),
        P("node", None),
        P("node", None),
        P("node", None),
        P("node", "head"),
        P("node", "head"),
        P("node", "head"),
        P(("head", "node"), None),
        P(("head", "node"), None),
        P(("head", "node"), None),
        P("node", "head"),
        P("node", "head"),
        P("node", "head"),
        P(("head", "node"), None),
        P(("head", "node"), None),
        P(("head", "node"), None),
    )
    return jax.shard_map(
        chosen,
        mesh=mesh,
        in_specs=placed,
        out_specs=(
            P("node", None),
            P("node", None),
            P("node", None),
            P("node", None),
            P("node", None),
            P("node", "head"),
            P("node", "head"),
            P("node", "head"),
            P(("head", "node"), None),
            P(("head", "node"), None),
            P(("head", "node"), None),
            P("node", "head"),
            P("node", "head"),
            P("node", "head"),
            P(("head", "node"), None),
            P(("head", "node"), None),
            P(("head", "node"), None),
        ),
        check_vma=False,
    )
```

```python
import functools
import math

import jax
import jax.numpy as jnp
from jax import lax
from jax.experimental import pallas as pl
from jax.experimental.pallas import tpu as pltpu
from jax.sharding import PartitionSpec as P


WIDTH = 512
HIDDEN_SIZE = 2048
COND = 512


norm_eps = 1e-06
beta_rate = 0.5
adam_eps = 1e-08
weight_decay = 0.1
highest = lax.Precision.HIGHEST


def passed_along(block, axis, distance):
    devices = range(lax.axis_size(axis))
    route = [((i - distance) % len(devices), i) for i in devices]
    return lax.ppermute(block, axis, route)


def norm_parts(values):
    centred = values - jnp.mean(values, axis=1, keepdims=True)
    inverse = lax.rsqrt(jnp.mean(centred * centred, axis=1, keepdims=True) + norm_eps)
    return (centred * inverse, inverse)


def norm_back(grad_normed, normed, inverse):
    first_mean = jnp.mean(grad_normed, axis=1, keepdims=True)
    second_mean = jnp.mean(grad_normed * normed, axis=1, keepdims=True)
    return inverse * (grad_normed - first_mean - normed * second_mean)


def adamw_update(master, first, second, grad, rate, count_value):
    first_new = beta_rate * first + (1.0 - beta_rate) * grad
    second_new = beta_rate * second + (1.0 - beta_rate) * grad * grad
    correct = 1.0 - jnp.power(jnp.float32(beta_rate), count_value)
    normed_step = first_new / correct / (jnp.sqrt(second_new / correct) + adam_eps)
    master_new = master - rate * (normed_step + weight_decay * master)
    return (master_new, first_new, second_new)


f32=jnp.float32; bf16=jnp.bfloat16
NT=(((1,),(1,)),((),()))
SPAN=256

def count_groups(cnt, code, rows, start, stop, step):
    parts=rows//SPAN
    total=5*parts*16
    short=jnp.int16
    rowid=lax.broadcasted_iota(jnp.int32,(total,SPAN),0).astype(short)
    spot=lax.broadcasted_iota(jnp.int32,(SPAN,SPAN),0).astype(short)
    one=bf16(1); zero=bf16(0)
    def group(g):
        both=code[pl.ds(g,1),:]
        keys=lax.shift_right_arithmetic(both,8).astype(short)
        low=lax.bitwise_and(both,255).astype(short)
        left=jnp.where(rowid==jnp.broadcast_to(keys,(total,SPAN)),one,zero)
        right=jnp.where(spot==jnp.broadcast_to(low,(SPAN,SPAN)),one,zero)
        made=lax.dot_general(left,right,NT,preferred_element_type=f32).astype(bf16)
        at=pl.multiple_of(g*16,16)
        for b in range(5):
            for p in range(parts):
                r=(b*parts+p)*16
                cnt[b,pl.ds(at,16),p*SPAN:(p+1)*SPAN]=made[r:r+16,:]
    def body(g,_):
        for u in range(step): group(g*step+u)
        return 0
    lax.fori_loop(start//step,stop//step,body,0)

def add_self(cnt, block, rows):
    eye=(lax.broadcasted_iota(jnp.int32,(SPAN,SPAN),0)==lax.broadcasted_iota(jnp.int32,(SPAN,SPAN),1))
    one=jnp.where(eye,1.0,0.0).astype(bf16)
    for p in range(rows//SPAN):
        s=slice(p*SPAN,(p+1)*SPAN)
        cnt[block,s,s]=cnt[block,s,s]+one

def attend_rows(b, first, at, size, q, table, e, m, l, acc, fac, scale):
    lane=lax.broadcasted_iota(jnp.int32,(size,128),1)
    s=lax.dot_general(q[at,:],table[b,:,0:128],NT,preferred_element_type=f32)*scale
    c=e[b,at,:].astype(f32)
    s=jnp.where(c>0,s,-1e30)
    top=jnp.max(s,axis=1,keepdims=True)
    if not first:
        old=m[at,0:1]
        top=jnp.maximum(top,old)
    w=(jnp.exp2(s-top)*c).astype(bf16)
    e[b,at,:]=w
    out=jnp.dot(w,table[b,:,128:384],preferred_element_type=f32)
    if first:
        acc[at,:]=out[:,:128]; l[at,:]=out[:,128:]
        fac[at,:]=jnp.where(lane==b,top,0.0)
    else:
        shrink=jnp.exp2(old-top)
        acc[at,:]=acc[at,:]*shrink+out[:,:128]
        l[at,:]=l[at,:]*shrink+out[:,128:]
        fac[at,:]=jnp.where(lane==b,top,fac[at,:])
    m[at,:]=jnp.broadcast_to(top,(size,128))

def back_block(b, q_t, dof, fac, delta, table, e, dq, write, first, chunk, keyscale):
    rows=dof.shape[0]
    f=fac[:,b:b+1]
    dobh=(dof*f).astype(bf16)
    d=-(delta*f)
    h=d.astype(bf16); r=d-h.astype(f32); h2=r.astype(bf16); h3=(r-h2.astype(f32)).astype(bf16)
    lane=lax.broadcasted_iota(jnp.int32,(rows,128),1)
    dcol=jnp.where(lane==0,h.astype(f32),jnp.where(lane==1,h2.astype(f32),jnp.where(lane==2,h3.astype(f32),0.0))).astype(bf16)
    left=jnp.concatenate([dobh,dcol],axis=1)
    dob_t=dobh.T
    for i in range(rows//chunk):
        s=slice(i*chunk,(i+1)*chunk)
        dp=lax.dot_general(left,table[b,s,128:384],NT,preferred_element_type=f32)
        w=e[b,:,s]
        ds=(dp*w.astype(f32)).astype(bf16)
        write(slice(0,128),s,jnp.dot(q_t,ds,preferred_element_type=f32)*keyscale)
        write(slice(128,256),s,jnp.dot(dob_t,w,preferred_element_type=f32))
        out=jnp.dot(ds,table[b,s,0:128],preferred_element_type=f32)
        if first and i==0: dq[...]=out
        else: dq[...]+=out


def by_batch(pos, limits, table, row, lanes):
    pick=[table[row+b:row+b+1,lanes] for b in range(4)]
    out=jnp.where(pos>=limits[0],pick[1],pick[0])
    out=jnp.where(pos>=limits[1],pick[2],out)
    return jnp.where(pos>=limits[2],pick[3],out)


def batch_sums(pos, limits, values):
    lane=lax.broadcasted_iota(jnp.int32,(pos.shape[0],8),1)
    member=(pos>=limits[0]).astype(jnp.int32)+(pos>=limits[1]).astype(jnp.int32)+(pos>=limits[2]).astype(jnp.int32)
    onehot=jnp.where(lane==member,1.0,0.0).astype(f32)
    return lax.dot_general(onehot,values,(((0,),(0,)),((),())),precision=highest,preferred_element_type=f32)[0:4,:]


class Links:
    def __init__(self, send, recv):
        self.send, self.recv, self.used = send, recv, 0

    def copy(self, src, dst, head, node):
        made=pltpu.make_async_remote_copy(src_ref=src,dst_ref=dst,send_sem=self.send.at[self.used],recv_sem=self.recv.at[self.used],
            device_id=(head,node),device_id_type=pl.DeviceIdType.MESH)
        self.used+=1
        return made

    def go(self, src, dst, head, node):
        made=self.copy(src,dst,head,node)
        made.start()
        return made


def meet(peers):
    barrier=pltpu.get_barrier_semaphore()
    for head,node in peers:
        pl.semaphore_signal(barrier,inc=1,device_id=(head,node),device_id_type=pl.DeviceIdType.MESH)
    pl.semaphore_wait(barrier,len(peers))


class Shown:
    def __init__(self, links, head, node, place):
        self.end=(head==0)|(head==3)
        own=place(head)
        self.two=links.go(own,own,head^2,node)
        self.one=links.go(own,own,head^1,node)
        self.three=links.copy(own,own,head^3,node)
        pl.when(~self.end)(self.three.start)
        far=place(jnp.where(self.end,head^3,head^2))
        self.pass_copy=links.copy(far,far,head^1,node)

    def onward(self):
        @pl.when(~self.end)
        def _():
            self.two.wait_recv()
            self.pass_copy.start()

    def wait(self):
        self.one.wait()
        self.two.wait_send()
        @pl.when(self.end)
        def _():
            self.two.wait_recv()
            self.pass_copy.wait_recv()
        @pl.when(~self.end)
        def _():
            self.three.wait()
            self.pass_copy.wait_send()


class Added:
    def __init__(self, links, head, node, part, got, relay):
        self.end=(head==0)|(head==3)
        self.relay=relay
        self.far=part(head^2)
        self.zero=links.copy(part(head^3),relay,head^1,node)
        self.two=links.copy(self.far,got(1),head^2,node)
        self.one=links.copy(part(head^1),got(0),head^1,node)
        self.three=links.copy(part(head^3),got(2),head^3,node)
        self.head=head
        @pl.when(self.end)
        def _(): got(2)[...]=jnp.zeros(relay.shape,bf16)

    def begin(self, to):
        pl.when(self.end&(self.head==to^3))(self.zero.start)
        pl.when((~self.end)&(self.head==to^3))(self.three.start)
        pl.when(self.end&(self.head==to^2))(self.two.start)
        pl.when(self.head==to^1)(self.one.start)

    def begin_all(self):
        @pl.when(self.end)
        def _():
            self.zero.start()
            self.two.start()
            self.one.start()
        @pl.when(~self.end)
        def _():
            self.three.start()
            self.one.start()
        return self

    def onward(self):
        @pl.when(~self.end)
        def _():
            self.zero.wait_recv()
            self.far[...]=summed(self.far,self.relay).astype(bf16)
            self.two.start()

    def wait(self):
        pl.when(self.end)(self.zero.wait_send)
        pl.when(~self.end)(self.three.wait)
        self.one.wait()
        self.two.wait()


def wait_all(copies):
    for c in copies: c.wait()


def block_of(index, size):
    return pl.ds(pl.multiple_of(index*size,size),size)


def summed(*refs):
    total=refs[0][...].astype(f32)
    for r in refs[1:]: total=total+r[...].astype(f32)
    return total


NAMES=("ada","qkv","out","up","down")


def scratch(rows):
    part=rows//4
    return dict(
        e=((5,rows,rows),bf16),m=((rows,128),f32),l=((rows,128),f32),att=((rows,128),f32),fac=((rows,128),f32),
        queries=((rows,128),bf16),table=((5,rows,384),bf16),xn_one=((rows,512),bf16),
        qkv_full=((512,384),bf16),out_full=((4,128,512),bf16),up_full=((512,2048),bf16),down_full=((4,512,512),bf16),
        modp=((8,1024),f32),modbuf=((8,8,1024),f32),modulation=((8,1024),f32),
        mixed=((rows,128),bf16),heads=((part,512),bf16),do=((rows,128),bf16),do_rows=((part,512),bf16),
        act=((part,2048),bf16),pre=((part,2048),bf16),dy=((part,512),f32),
        up_grad=((4,2,64,2048),bf16),down_grad=((4,4,2,64,512),bf16),out_grad=((4,4,2,16,512),bf16),
        dq=((rows,128),f32),dkv=((256,rows),f32),near=((5,256,rows),bf16),
        got_pair=((256,rows),bf16),got_y=((256,rows),bf16),got_x=((256,rows),bf16),got_one=((256,rows),bf16),
        proj_grad=((rows,384),bf16),partial=((4,part,512),bf16),got_partial=((3,part,512),bf16),normed=((rows,512),f32),
        up1=((4,64,2048),bf16),down1=((4,4,64,512),bf16),out1=((4,4,16,512),bf16),
        up2=((2,64,2048),bf16),down2=((4,2,64,512),bf16),out2=((4,2,16,512),bf16),
        up3=((64,2048),bf16),down3=((4,64,512),bf16),out3=((4,16,512),bf16),
        up_z=((3,64,512),bf16),down_z=((3,64,512),bf16),out_z=((3,16,512),bf16),
        up_relay=((64,512),bf16),down_relay=((64,512),bf16),out_relay=((16,512),bf16),relay=((part,512),bf16),
        qkv_grad=((8,64,384),bf16),qkv_got=((7,64,384),bf16),dm_own=((8,1024),f32),dm_z=((4,8,1024),f32),dm_n=((8,8,1024),f32),
    )


class Bag:
    pass


COPIES=150


def layer_kernel(scale, names, *refs):
    refs=list(refs)
    take=lambda n: [refs.pop(0) for _ in range(n)]
    node_input,cotangent,sigma,code,counts=take(5)
    w={n:refs.pop(0) for n in NAMES}
    node_output,row_all,qkv_sum,out_sum,up_sum,down_sum,mod_sum=take(7)
    k=Bag()
    for n in names: setattr(k,n,refs.pop(0))
    send,recv=take(2)
    head=lax.axis_index("head"); node=lax.axis_index("node")
    y_at=node//4; x_at=(node//2)%2; core=node%2
    rows=node_input.shape[0]
    part=rows//4
    links=Links(send,recv)
    go=links.go
    normed=k.normed
    quarter=[slice(i*part,(i+1)*part) for i in range(4)]
    limits=(counts[0],counts[0]+counts[1],counts[0]+counts[1]+counts[2])
    mine=block_of(head,part)
    head_cols=block_of(head,512)
    own_pos=node*rows+head*part+lax.broadcasted_iota(jnp.int32,(part,1),0)

    own=block_of(node,64); own_out=block_of(node,16)
    k.qkv_full[own,:]=w["qkv"][...].astype(bf16)
    sig=sigma[:,0:64]
    for i in range(1,8): sig=jnp.where(node==i,sigma[:,i*64:(i+1)*64],sig)
    made=jnp.dot(sig,w["ada"][...].astype(bf16),preferred_element_type=f32)
    k.modp[0:4,:]=made[:,:1024]
    k.modp[4:8,:]=made[:,1024:]
    k.up_full[own,head_cols]=w["up"][...].astype(bf16)
    k.down_full[head,own,:]=w["down"][...].astype(bf16)
    k.out_full[head,own_out,:]=w["out"][...].astype(bf16)
    meet([(head,node^i) for i in range(1,8)]+[(head^i,node) for i in range(1,4)])
    first=[]
    for i in range(1,8):
        first.append(go(k.modp,k.modbuf.at[node],head,node^i))
        first.append(go(k.qkv_full.at[own],k.qkv_full.at[own],head,node^i))
    along=[]
    for place in (lambda h: k.up_full.at[own,block_of(h,512)],lambda h: k.down_full.at[h,own],lambda h: k.out_full.at[h,own_out]):
        along.append(Shown(links,head,node,place))
    k.modbuf[node,:,:]=k.modp[...]
    for b in range(5): k.table[b,:,256:384]=jnp.ones((rows,128),bf16)
    def norm(i,_):
        at=block_of(i,256)
        v=node_input[at,:].astype(f32)
        centred=v-jnp.mean(v,axis=1,keepdims=True)
        normed[at,:]=centred*lax.rsqrt(jnp.mean(centred*centred,axis=1,keepdims=True)+norm_eps)
        return 0
    lax.fori_loop(0,rows//256,norm,0)
    groups=code.shape[0]
    half=groups//2
    count_groups(k.e,code,rows,0,half,4)
    for a in along: a.onward()
    def column(which):
        at=block_of(node^which,64)
        return [k.up_full.at[at],k.down_full.at[:,at],k.out_full.at[:,block_of(node^which,16)]]
    own_column=column(0); from_x=column(2); from_y=column(4)
    along[0].wait()
    up_x=go(own_column[0],own_column[0],head,node^2)
    wait_all(first)
    mod=k.modbuf[0]
    for i in range(1,8): mod=mod+k.modbuf[i]
    k.modulation[...]=mod

    kv=slice(0,256)
    across=[]; paired=[]
    for at in quarter:
        pos=node*rows+at.start+lax.broadcasted_iota(jnp.int32,(part,1),0)
        xn=(normed[at,:]*(1.0+by_batch(pos,limits,k.modulation,0,slice(0,512)))+by_batch(pos,limits,k.modulation,0,slice(512,1024))).astype(bf16)
        k.xn_one[at,:]=xn
        proj=jnp.dot(xn,k.qkv_full[...],preferred_element_type=f32).astype(bf16)
        k.queries[at,:]=proj[:,:128]
        k.table[0,at,kv]=proj[:,128:]
        across.append(go(k.table.at[0,at,kv],k.table.at[2,at,kv],head,node^2))
        paired.append(go(k.table.at[0,at,kv],k.table.at[1,at,kv],head,node^1))
    wait_all(along[1:])
    rest_y=[go(r,r,head,node^4) for r in own_column[1:]]
    count_groups(k.e,code,rows,half,groups,4)
    add_self(k.e,0,rows)

    onward=[]
    def pass_keys(i):
        at=quarter[i]
        across[i].wait_recv()
        onward.append(go(k.table.at[2,at,kv],k.table.at[3,at,kv],head,node^4))
    def attend(b,at):
        attend_rows(b,b==0,at,part,k.queries,k.table,k.e,k.m,k.l,k.att,k.fac,scale*math.log2(math.e))
    def attend_all(b):
        def two(i,_):
            for u in range(2): attend(b,block_of(2*i+u,part))
            return 0
        lax.fori_loop(0,2,two,0)
    pass_keys(0)
    attend_all(0)
    pass_keys(1)
    wait_all(paired)
    attend_all(1)
    pass_keys(2)
    pass_keys(3)
    up_y=go(own_column[0],own_column[0],head,node^4)
    rest_x=[go(r,r,head,node^2) for r in own_column[1:]]
    to_pair=[go(r,r,head,node^1) for r in own_column]
    up_x.wait()
    wait_all(rest_y)
    cross=[go(from_x[0],from_x[0],head,node^4)]+[go(r,r,head,node^2) for r in from_y[1:]]
    hand=[go(r,r,head,node^1) for r in from_x[:1]+from_y[1:]]
    attend_all(2)
    wait_all(onward)
    fifth=go(k.table.at[jnp.where(x_at==core,2,3),:,kv],k.table.at[4,:,kv],head,node^1)
    for at in quarter: attend(3,at)
    fifth.wait()
    lanes=block_of(head,128)
    moved=[]
    for i in range(4):
        at=quarter[i]
        attend(4,at)
        inv=1.0/k.l[at,:]
        o=k.att[at,:]*inv
        k.att[at,:]=o
        k.fac[at,:]=jnp.exp2(k.fac[at,:]-k.m[at,:])*inv
        k.mixed[at,:]=o.astype(bf16)
    for i in range(1,4):
        moved.append(go(k.mixed.at[block_of(head^i,part)],k.heads.at[:,lanes],head^i,node))
    k.heads[:,lanes]=k.mixed[mine,:]
    for c in across: c.wait_send()
    up_y.wait()
    wait_all(rest_x)
    hand+=[go(r,r,head,node^1) for r in from_y[:1]+from_x[1:]]
    wait_all(cross)
    last=[go(r,r,head,node^1) for r in column(6)]
    scale_two=1.0+by_batch(own_pos,limits,k.modulation,4,slice(0,512))
    shift_two=by_batch(own_pos,limits,k.modulation,4,slice(512,1024))
    g=cotangent[mine,:]
    wait_all(moved)
    wait_all(to_pair+hand+last)

    out_all=k.out_full[...].reshape(512,512)
    y=node_input[mine,:].astype(f32)+jnp.dot(k.heads[...],out_all,preferred_element_type=f32)
    n_two,inv_two=norm_parts(y)
    xn=(n_two*scale_two+shift_two).astype(bf16)
    mlp=jnp.zeros((part,512),f32); dxn=jnp.zeros((part,512),f32)
    for j in range(4):
        s=slice(j*512,(j+1)*512)
        h=jnp.dot(xn,k.up_full[:,s],preferred_element_type=f32)
        gate=1.0/(1.0+jnp.exp(-h))
        u=(h*gate).astype(bf16)
        k.act[:,s]=u
        mlp+=jnp.dot(u,k.down_full[j],preferred_element_type=f32)
        du=lax.dot_general(g,k.down_full[j],NT,preferred_element_type=f32)
        d=(du*gate*(1.0+h*(1.0-gate))).astype(bf16)
        k.pre[:,s]=d
        dxn+=lax.dot_general(d,k.up_full[:,s],NT,preferred_element_type=f32)
    dyv=g.astype(f32)+norm_back(dxn*scale_two,n_two,inv_two)
    k.dy[...]=dyv
    da=dyv.astype(bf16)
    k.do_rows[...]=lax.dot_general(da,out_all,NT,preferred_element_type=f32).astype(bf16)
    returned=[]
    for i in range(1,4):
        returned.append(go(k.do_rows.at[:,block_of(head^i,128)],k.do.at[mine],head^i,node))
    k.do[mine,:]=k.do_rows[:,lanes]
    node_output[mine,:]=(y+mlp).astype(bf16)
    xn_t=xn.T
    heads_t=k.heads[...].T
    k.out_grad[...]=jnp.dot(heads_t,da,preferred_element_type=f32).astype(bf16).reshape(4,4,2,16,512)
    for j in range(4):
        s=slice(j*512,(j+1)*512)
        k.up_grad[:,:,:,s]=jnp.dot(xn_t,k.pre[:,s],preferred_element_type=f32).astype(bf16).reshape(4,2,64,512)
        k.down_grad[j]=jnp.dot(k.act[:,s].T,g,preferred_element_type=f32).astype(bf16).reshape(4,2,64,512)
    stage1=[go(k.up_grad.at[:,1-core],k.up1,head,node^1),go(k.down_grad.at[:,:,1-core],k.down1,head,node^1),go(k.out_grad.at[:,:,1-core],k.out1,head,node^1)]
    k.dm_own[4:8,0:512]=batch_sums(own_pos,limits,dxn*n_two)
    k.dm_own[4:8,512:1024]=batch_sums(own_pos,limits,dxn)
    wait_all(returned)
    shown=Shown(links,head,node,lambda h: node_output.at[block_of(h,part)])

    q_t=k.queries[...].T
    dof=k.do[...].astype(f32)
    delta=jnp.sum(dof*k.att[...],axis=1,keepdims=True)
    def block(b):
        def write(r,s,v):
            if b==0: k.dkv[r,s]=v
            else: k.near[b,r,s]=v.astype(bf16)
        back_block(b,q_t,dof,k.fac,delta,k.table,k.e,k.dq,write,b==4,512,scale)
    near=k.near
    block(4)
    give=go(near.at[4],k.got_pair,head,node^1)
    block(3)
    give.wait()
    @pl.when(x_at!=core)
    def _(): near[3]=summed(near[3],k.got_pair[...]).astype(bf16)
    order=(0,3,1,2)
    via_y={i:go(near.at[3,:,quarter[i]],k.got_y.at[:,quarter[i]],head,node^4) for i in order}
    block(2)
    @pl.when(x_at==core)
    def _(): near[2]=summed(near[2],k.got_pair[...]).astype(bf16)
    via_x={}
    def pass_on(i):
        i=order[i]
        s=quarter[i]
        via_y[i].wait()
        near[2,:,s]=summed(near[2,:,s],k.got_y[:,s]).astype(bf16)
        via_x[i]=go(near.at[2,:,s],k.got_x.at[:,s],head,node^2)
    pass_on(0)
    shown.onward()
    block(1)
    one=go(near.at[1],k.got_one,head,node^1)
    pass_on(1)
    block(0)
    wait_all(stage1)
    for i in range(4):
        k.down1[i]=summed(k.down1[i],k.down_grad[i,:,core]).astype(bf16)
        k.out1[i]=summed(k.out1[i],k.out_grad[i,:,core]).astype(bf16)
    there=pl.ds((1-y_at)*2,2)
    stage2=[go(k.down1.at[:,there],k.down2,head,node^4),go(k.out1.at[:,there],k.out2,head,node^4)]
    pass_on(2)
    one.wait()
    reduce=Added(links,head,node,lambda h: k.partial.at[h],lambda i: k.got_partial.at[i],k.relay)
    def finish_rows(i):
        i=order[i]
        s=quarter[i]
        via_x[i].wait()
        total=k.dkv[:,s]+k.got_one[:,s].astype(f32)+k.got_x[:,s].astype(f32)
        k.proj_grad[s,128:]=total.T.astype(bf16)
        k.proj_grad[s,:128]=(k.dq[s,:]*scale).astype(bf16)
        k.partial[i]=lax.dot_general(k.proj_grad[s,:],k.qkv_full[...],NT,preferred_element_type=f32).astype(bf16)
        reduce.begin(i)
    finish_rows(0)
    pass_on(3)
    for i in range(4):
        k.up1[i]=summed(k.up1[i],k.up_grad[i,core]).astype(bf16)
    stage2+=[go(k.up1.at[i*2+1-x_at],k.up2.at[i],head,node^2) for i in range(2)]
    for i in range(1,4): finish_rows(i)
    xn_t=k.xn_one[...].T
    k.qkv_grad[...]=jnp.dot(xn_t,k.proj_grad[...],preferred_element_type=f32).astype(bf16).reshape(8,64,384)
    qkv_moves=[go(k.qkv_grad.at[node^i],k.qkv_got.at[i-1],head,node^i) for i in range(1,8)]
    reduce.onward()
    wait_all(stage2)
    for i in range(2):
        k.up2[i]=summed(k.up2[i],k.up1[i*2+x_at]).astype(bf16)
    here=pl.ds(y_at*2,2)
    k.down2[...]=summed(k.down2[...],k.down1[:,here]).astype(bf16)
    k.out2[...]=summed(k.out2[...],k.out1[:,here]).astype(bf16)
    stage3=[go(k.up2.at[1-y_at],k.up3,head,node^4),go(k.down2.at[:,1-x_at],k.down3,head,node^2),go(k.out2.at[:,1-x_at],k.out3,head,node^2)]
    scale_one=1.0+by_batch(own_pos,limits,k.modulation,0,slice(0,512))
    n_one,inv_one=norm_parts(node_input[mine,:].astype(f32))
    reduce.wait()
    dxn=summed(k.partial.at[head],*[k.got_partial.at[i] for i in range(3)])
    row_all[head,:,:]=(k.dy[...]+norm_back(dxn*scale_one,n_one,inv_one)).astype(bf16)
    spread=Shown(links,head,node,lambda h: row_all.at[h])
    k.dm_own[0:4,0:512]=batch_sums(own_pos,limits,dxn*n_one)
    k.dm_own[0:4,512:1024]=batch_sums(own_pos,limits,dxn)
    dm_moves=[go(k.dm_own,k.dm_z.at[head],head^i,node) for i in range(1,4)]
    wait_all(qkv_moves)
    qkv_sum[...]=summed(k.qkv_grad[node],*[k.qkv_got[i] for i in range(7)])
    wait_all(stage3)
    k.up3[...]=summed(k.up3[...],k.up2[y_at]).astype(bf16)
    k.down3[...]=summed(k.down3[...],k.down2[:,x_at]).astype(bf16)
    k.out3[...]=summed(k.out3[...],k.out2[:,x_at]).astype(bf16)
    stage4=[Added(links,head,node,lambda h: k.up3.at[:,block_of(h,512)],lambda i: k.up_z.at[i],k.up_relay).begin_all(),
        Added(links,head,node,lambda h: k.down3.at[h],lambda i: k.down_z.at[i],k.down_relay).begin_all(),
        Added(links,head,node,lambda h: k.out3.at[h],lambda i: k.out_z.at[i],k.out_relay).begin_all()]
    spread.onward()
    for s in stage4: s.onward()
    k.dm_z[head,:,:]=k.dm_own[...]
    wait_all(dm_moves)
    k.modp[...]=k.dm_z[0]+k.dm_z[1]+k.dm_z[2]+k.dm_z[3]
    dm_last=[go(k.modp,k.dm_n.at[node],head,node^i) for i in range(1,8)]
    k.dm_n[node,:,:]=k.modp[...]
    wait_all(dm_last)
    total=k.dm_n[0]
    for i in range(1,8): total=total+k.dm_n[i]
    mod_sum[...]=total
    wait_all(stage4)
    up_sum[...]=summed(k.up3[:,head_cols],*[k.up_z[i] for i in range(3)])
    down_sum[...]=summed(k.down3[head],*[k.down_z[i] for i in range(3)])
    out_sum[...]=summed(k.out3[head],*[k.out_z[i] for i in range(3)])
    spread.wait()
    shown.wait()


def finish_kernel(sigma, step_count, *refs):
    sources=refs[:22]; results=refs[22:39]; held=refs[39:62]; load,store=refs[62:]
    loads=[pltpu.make_async_copy(sources[i],held[i],load.at[i]) for i in range(22)]
    for i in (0,1)+tuple(range(7,22))+tuple(range(2,7)): loads[i].start()
    node=lax.axis_index("node")
    stores=[]
    def keep(ref, result):
        stores.append(pltpu.make_async_copy(ref,results[result],store.at[result])); stores[-1].start()
    loads[0].wait()
    keep(held[0],0)
    loads[1].wait()
    wide=held[22]
    rows=wide.shape[0]
    for i in range(4): wide[i*rows//4:(i+1)*rows//4,:]=held[1][i].astype(f32)
    keep(wide,1)
    count=jnp.full((8,128),step_count[0],jnp.int32).astype(f32)
    correct=(1.0-jnp.exp2(-count))[0:1,0:1]
    sig=sigma[:,0:64]
    for i in range(1,8): sig=jnp.where(node==i,sigma[:,i*64:(i+1)*64],sig)
    rates=((4*COND)**-0.5,(WIDTH//2)**-0.5,(WIDTH//4)**-0.5,WIDTH**-0.5,HIDDEN_SIZE**-0.5)
    for w in (0,3,4,1,2):
        at=7+3*w
        for i in range(3): loads[at+i].wait()
        if w==0:
            loads[6].wait()
            total=held[6]
            batch_grad=jnp.concatenate([total[0:4,:],total[4:8,:]],axis=1)
            grad=lax.dot_general(sig.astype(f32),batch_grad,(((0,),(0,)),((),())),precision=highest,preferred_element_type=f32)
        else:
            loads[1+w].wait()
            grad=held[1+w][...]
        master,first,second=held[at:at+3]
        first_new=beta_rate*first[...]+(1.0-beta_rate)*grad
        second_new=beta_rate*second[...]+(1.0-beta_rate)*grad*grad
        step=first_new/correct/(jnp.sqrt(second_new/correct)+adam_eps)
        old=master[...]
        master[...]=old-rates[w]*(step+weight_decay*old)
        first[...]=first_new
        second[...]=second_new
        for i in range(3): keep(held[at+i],2+3*w+i)
    for c in stores: c.wait()


def slots(neighbours, valid, node, rows):
    which=(neighbours//rows)^node
    slot=jnp.where(which==6,3,jnp.where((which==3)|(which==7),4,which))
    local=neighbours%rows
    spot=lax.broadcasted_iota(jnp.int32,neighbours.shape,0)%16
    hi=(slot*(rows//SPAN)+local//SPAN)*16+spot
    return jnp.where(valid>0,hi*256+local%SPAN,-1).reshape(-1,256)


def per_device_near(
    node_input, cotangent, sigma_embed, neighbours, neighbour_valid, batch_counts, step_count,
    ada_master, ada_first, ada_second, qkv_master, qkv_first, qkv_second, out_master, out_first, out_second,
    up_master, up_first, up_second, down_master, down_first, down_second,
):
    rows=node_input.shape[0]
    code=slots(neighbours,neighbour_valid,lax.axis_index("node"),rows)
    masters=(ada_master,qkv_master,out_master,up_master,down_master)
    firsts=(ada_first,qkv_first,out_first,up_first,down_first)
    seconds=(ada_second,qkv_second,out_second,up_second,down_second)
    V=pltpu.VMEM
    full=pl.BlockSpec(memory_space=V); few=pl.BlockSpec(memory_space=pltpu.SMEM); hbm=pl.BlockSpec(memory_space=pltpu.HBM)
    S=jax.ShapeDtypeStruct
    held=scratch(rows)
    sums=pl.pallas_call(functools.partial(layer_kernel,128**-0.5,tuple(held)),
        out_shape=(S((rows,512),bf16),S((4,rows//4,512),bf16))+tuple(S(a.shape,f32) for a in masters[1:])+(S((8,1024),f32),),
        in_specs=[full]*4+[few]+[full]*5,
        out_specs=(full,)*7,
        scratch_shapes=[V(*v) for v in held.values()]+[pltpu.SemaphoreType.DMA((COPIES,))]*2,
        compiler_params=pltpu.CompilerParams(vmem_limit_bytes=67043328,collective_id=1,has_side_effects=True),
        name="layer")(node_input,cotangent,sigma_embed,code,batch_counts,*masters)
    news=tuple(S(a.shape,f32) for a in masters for _ in range(3))
    inner=[V(a.shape,a.dtype) for a in sums]+[V(a.shape,f32) for a in masters for _ in range(3)]+[V((rows,512),f32)]
    return pl.pallas_call(finish_kernel,
        out_shape=(S((rows,512),bf16),S((rows,512),f32))+news,
        in_specs=[full,few]+[hbm]*(7+15),
        out_specs=(hbm,)*17,
        scratch_shapes=inner+[pltpu.SemaphoreType.DMA((22,)),pltpu.SemaphoreType.DMA((17,))],
        compiler_params=pltpu.CompilerParams(vmem_limit_bytes=67043328),
        name="finish")(sigma_embed,step_count,*sums,*[a for three in zip(masters,firsts,seconds) for a in three])


def wide_count_groups(cnt, hik, lok, rows):
    steps=hik.shape[0]
    parts=rows//SPAN
    total=5*parts*16
    rowid=lax.broadcasted_iota(jnp.int32,(total,1),0)
    rowkey=lax.div(rowid,16)*16+lax.rem(rowid,16)
    spot=lax.broadcasted_iota(jnp.int32,(SPAN,1),0)
    def body(g,_):
        keys=hik[pl.ds(g,1),:]
        low=lok[pl.ds(g,1),:]
        left=jnp.where(rowkey==keys,1.0,0.0).astype(bf16)
        right=jnp.where(spot==low,1.0,0.0).astype(bf16)
        made=lax.dot_general(left,right,NT,preferred_element_type=f32).astype(bf16)
        at=pl.multiple_of(g*16,16)
        for b in range(5):
            for p in range(parts):
                r=(b*parts+p)*16
                cnt[b,pl.ds(at,16),p*SPAN:(p+1)*SPAN]=made[r:r+16,:]
        return 0
    lax.fori_loop(0,steps,body,0)

def wide_add_self(cnt, block, rows):
    eye=(lax.broadcasted_iota(jnp.int32,(SPAN,SPAN),0)==lax.broadcasted_iota(jnp.int32,(SPAN,SPAN),1))
    one=jnp.where(eye,1.0,0.0).astype(bf16)
    for p in range(rows//SPAN):
        s=slice(p*SPAN,(p+1)*SPAN)
        cnt[block,s,s]=cnt[block,s,s]+one

def wide_attend_block(b, first, q, keys, vals, cnt, e, m, l, acc, fac, chunk, scale):
    rows=q.shape[0]
    lane=lax.broadcasted_iota(jnp.int32,(chunk,128),1)
    def body(i,_):
        at=pl.ds(pl.multiple_of(i*chunk,chunk),chunk)
        s=lax.dot_general(q[at,:],keys,NT,preferred_element_type=f32)*scale
        c=cnt[b,at,:].astype(f32)
        s=jnp.where(c>0,s,-1e30)
        top=jnp.max(s,axis=1,keepdims=True)
        if not first:
            old=m[at,0:1]
            top=jnp.maximum(top,old)
        w=(jnp.exp2(s-top)*c)
        total=jnp.sum(w,axis=1,keepdims=True)
        w=w.astype(bf16)
        e[b,at,:]=w
        out=jnp.dot(w,vals,preferred_element_type=f32)
        if first:
            acc[at,:]=out; l[at,:]=jnp.broadcast_to(total,(chunk,128))
            fac[at,:]=jnp.where(lane==b,top,0.0)
        else:
            shrink=jnp.exp2(old-top)
            acc[at,:]=acc[at,:]*shrink+out
            l[at,:]=l[at,:]*shrink+total
            fac[at,:]=jnp.where(lane==b,top,fac[at,:])
        m[at,:]=jnp.broadcast_to(top,(chunk,128))
        return 0
    lax.fori_loop(0,rows//chunk,body,0)

def wide_fwd_kernel(order, self_block, scale, q, kv, hik, lok, att, e, fac, cnt, m, l):
    rows=q.shape[0]
    wide_count_groups(cnt,hik,lok,rows)
    wide_add_self(cnt,self_block,rows)
    for t,b in enumerate(order):
        wide_attend_block(b,t==0,q,kv[b,:,:128],kv[b,:,128:],cnt,e,m,l,att,fac,256,scale)
    inv=1.0/l[...]
    att[...]=att[...]*inv
    fac[...]=jnp.exp2(fac[...]-m[...])*inv

def wide_attention_fwd(q,kv,hik,lok,scale):
    rows=q.shape[0]
    V=pltpu.VMEM
    full=pl.BlockSpec(memory_space=V)
    return pl.pallas_call(functools.partial(wide_fwd_kernel,(2,1,3,0,4),2,scale*math.log2(math.e)),
        out_shape=(jax.ShapeDtypeStruct((rows,128),f32),jax.ShapeDtypeStruct((5,rows,rows),bf16),jax.ShapeDtypeStruct((rows,128),f32)),
        in_specs=[full]*4,out_specs=(full,)*3,
        scratch_shapes=[V((5,rows,rows),bf16),V((rows,128),f32),V((rows,128),f32)],
        compiler_params=pltpu.CompilerParams(vmem_limit_bytes=60<<20),name="attend_fwd")(q,kv,hik,lok)

def wide_back_block(b, q_t, do, fac, delta, kv, e, dq, dkv, first, chunk, keyscale):
    rows=do.shape[0]
    f=fac[:,b:b+1]
    dob=(do*f)
    dobh=dob.astype(bf16)
    d=-(delta*f)
    h=d.astype(bf16); r=d-h.astype(f32); h2=r.astype(bf16); h3=(r-h2.astype(f32)).astype(bf16)
    lane=lax.broadcasted_iota(jnp.int32,(rows,128),1)
    zero=jnp.zeros((rows,128),bf16)
    dcol=jnp.where(lane==0,h.astype(f32),jnp.where(lane==1,h2.astype(f32),jnp.where(lane==2,h3.astype(f32),0.0))).astype(bf16)
    left=jnp.concatenate([dobh,dcol],axis=1)
    dob_t=dobh.T
    ones=jnp.ones((chunk,128),bf16)
    for i in range(kv.shape[1]//chunk):
        s=slice(i*chunk,(i+1)*chunk)
        right=jnp.concatenate([kv[b,s,128:],ones],axis=1)
        dp=lax.dot_general(left,right,NT,preferred_element_type=f32)
        w=e[b,:,s]
        ds=(dp*w.astype(f32)).astype(bf16)
        dkv[b,:128,s]=jnp.dot(q_t,ds,preferred_element_type=f32)*keyscale
        dkv[b,128:,s]=jnp.dot(dob_t,w,preferred_element_type=f32)
        out=jnp.dot(ds,kv[b,s,:128],preferred_element_type=f32)
        if first and i==0: dq[...]=out
        else: dq[...]+=out

def wide_bwd_kernel(scale, q, do, att, fac, kv, e, dq, dkv, ):
    q_t=q[...].T
    dof=do[...].astype(f32)
    delta=jnp.sum(dof*att[...],axis=1,keepdims=True)
    for t,b in enumerate((0,4,1,3,2)):
        wide_back_block(b,q_t,dof,fac,delta,kv,e,dq,dkv,t==0,512,scale)
    dq[...]=dq[...]*scale

def wide_attention_bwd(q,do,att,fac,kv,e,scale):
    rows=q.shape[0]
    V=pltpu.VMEM
    full=pl.BlockSpec(memory_space=V)
    return pl.pallas_call(functools.partial(wide_bwd_kernel,scale),
        out_shape=(jax.ShapeDtypeStruct((rows,128),f32),jax.ShapeDtypeStruct((5,256,rows),f32)),
        in_specs=[full]*6,out_specs=(full,)*2,
        compiler_params=pltpu.CompilerParams(vmem_limit_bytes=60<<20),name="attend_bwd")(q,do,att,fac,kv,e)

def wide_tables(slot_index, valid, rows):
    parts=rows//SPAN
    flat=slot_index.reshape(-1,256)
    ok=(valid>0).reshape(-1,256)
    node=lax.broadcasted_iota(jnp.int32,flat.shape,1)//16
    hi=jnp.where(ok,(flat//SPAN)*16+node,-1)
    lo=flat%SPAN
    return hi,lo


def per_device(
    node_input,
    cotangent,
    sigma_embed,
    neighbours,
    neighbour_valid,
    batch_counts,
    step_count,
    ada_master,
    ada_first,
    ada_second,
    qkv_master,
    qkv_first,
    qkv_second,
    out_master,
    out_first,
    out_second,
    up_master,
    up_first,
    up_second,
    down_master,
    down_first,
    down_second,
):
    f32 = jnp.float32
    bf16 = jnp.bfloat16
    node_rows = node_input.shape[0]
    model_width = node_input.shape[1]
    head_dim = qkv_master.shape[1] // 3
    score_scale = head_dim ** (-0.5)
    node_index = lax.axis_index("node")
    total_nodes = node_rows * lax.axis_size("node")
    qkv_full, out_full, up_full, down_full = (
        lax.all_gather(qkv_master.astype(bf16), "node", axis=0, tiled=True),
        lax.all_gather(out_master.astype(bf16), "node", axis=0, tiled=True),
        lax.all_gather(up_master.astype(bf16), "node", axis=0, tiled=True),
        lax.all_gather(down_master.astype(bf16), "node", axis=0, tiled=True),
    )
    cond_rows = ada_master.shape[0]
    sigma_part = lax.dynamic_slice_in_dim(sigma_embed, node_index * cond_rows, cond_rows, 1)
    limits = jnp.cumsum(batch_counts)[:-1]
    positions = node_index * node_rows + jnp.arange(node_rows, dtype=jnp.int32)
    member = jnp.sum((positions[:, None] >= limits[None, :]).astype(jnp.int32), axis=1)
    onehot = (
        member[:, None] == jnp.arange(batch_counts.shape[0], dtype=jnp.int32)[None, :]
    ).astype(f32)
    modulation = lax.psum(
        jnp.dot(sigma_part, ada_master.astype(bf16), preferred_element_type=f32), "node"
    )
    per_node = jnp.dot(onehot, modulation, precision=highest)
    scale_one = per_node[:, :model_width]
    shift_one = per_node[:, model_width : 2 * model_width]
    scale_two = per_node[:, 2 * model_width : 3 * model_width]
    shift_two = per_node[:, 3 * model_width :]
    normed_one, inverse_one = norm_parts(node_input.astype(f32))
    xn_one = (normed_one * (1.0 + scale_one) + shift_one).astype(bf16)
    projected = jnp.dot(xn_one, qkv_full, preferred_element_type=f32).astype(bf16)
    queries = projected[:, :head_dim]
    keys_values = projected[:, head_dim:]
    offsets = (-2, -1, 1, 2)
    fetched = {0: keys_values}
    for offset in offsets:
        fetched[offset] = passed_along(keys_values, "node", -offset)
    table = jnp.stack([fetched[offset] for offset in (-2, -1, 0, 1, 2)], axis=0)
    slot_index = jnp.mod(neighbours - (node_index - 2) * node_rows, total_nodes)
    high_keys, low_keys = wide_tables(slot_index, neighbour_valid, node_rows)
    mixed, weights, factors = wide_attention_fwd(queries, table, high_keys, low_keys, score_scale)
    heads_out = mixed.astype(bf16)
    branch = lax.psum(
        jnp.dot(heads_out, out_full, preferred_element_type=f32).astype(jnp.bfloat16), "head"
    ).astype(jnp.float32)
    middle = node_input.astype(f32) + branch
    normed_two, inverse_two = norm_parts(middle)
    xn_two = (normed_two * (1.0 + scale_two) + shift_two).astype(bf16)
    hidden_pre = jnp.dot(xn_two, up_full, preferred_element_type=f32)
    gate_sig = jax.nn.sigmoid(hidden_pre)
    activated = (hidden_pre * gate_sig).astype(bf16)
    mlp_sum = lax.psum(
        jnp.dot(activated, down_full, preferred_element_type=f32).astype(jnp.bfloat16), "head"
    ).astype(jnp.float32)
    node_output = (middle + mlp_sum).astype(bf16)
    down_grad = jnp.einsum("nf,nd->fd", activated, cotangent, preferred_element_type=f32)
    act_grad = jnp.einsum("nd,fd->nf", cotangent, down_full, preferred_element_type=f32)
    pre_grad = (act_grad * gate_sig * (1.0 + hidden_pre * (1.0 - gate_sig))).astype(bf16)
    up_grad = jnp.einsum("nw,nf->wf", xn_two, pre_grad, preferred_element_type=f32)
    normed_two_grad = lax.psum(
        jnp.einsum("nf,wf->nw", pre_grad, up_full, preferred_element_type=f32).astype(jnp.bfloat16),
        "head",
    ).astype(jnp.float32)
    middle_grad = cotangent.astype(f32) + norm_back(
        normed_two_grad * (1.0 + scale_two), normed_two, inverse_two
    )
    branch_grad = middle_grad.astype(bf16)
    out_grad = jnp.einsum("nh,nd->hd", heads_out, branch_grad, preferred_element_type=f32)
    mixed_grad = jnp.einsum("nd,hd->nh", branch_grad, out_full, preferred_element_type=f32).astype(
        bf16
    )
    query_grad, pair_sums = wide_attention_bwd(
        queries, mixed_grad, mixed, factors, table, weights, score_scale
    )
    remote_terms = pair_sums[2]
    for offset in offsets:
        remote_terms = remote_terms + passed_along(
            pair_sums[offset + 2].astype(bf16), "node", offset
        ).astype(f32)
    key_value_grad = remote_terms.T
    projected_grad = jnp.concatenate([query_grad, key_value_grad], axis=1).astype(bf16)
    qkv_grad = jnp.einsum("nw,nc->wc", xn_one, projected_grad, preferred_element_type=f32)
    normed_one_grad = lax.psum(
        jnp.einsum("nc,wc->nw", projected_grad, qkv_full, preferred_element_type=f32).astype(
            jnp.bfloat16
        ),
        "head",
    ).astype(jnp.float32)
    input_grad = middle_grad + norm_back(
        normed_one_grad * (1.0 + scale_one), normed_one, inverse_one
    )
    rows_grad = jnp.concatenate(
        [
            normed_one_grad * normed_one,
            normed_one_grad,
            normed_two_grad * normed_two,
            normed_two_grad,
        ],
        axis=1,
    )
    batch_grad = jnp.dot(onehot.T, rows_grad, precision=highest)
    batch_grad = lax.psum(batch_grad, "node")
    ada_sum = jnp.dot(sigma_part.astype(f32).T, batch_grad, precision=highest)
    qkv_sum, out_sum, up_sum, down_sum = (
        lax.psum_scatter(qkv_grad, "node", scatter_dimension=0, tiled=True),
        lax.psum_scatter(out_grad, "node", scatter_dimension=0, tiled=True),
        lax.psum_scatter(up_grad, "node", scatter_dimension=0, tiled=True),
        lax.psum_scatter(down_grad, "node", scatter_dimension=0, tiled=True),
    )
    count_value = step_count[0].astype(f32)
    ada_res = adamw_update(
        ada_master, ada_first, ada_second, ada_sum, (4 * COND) ** (-0.5), count_value
    )
    qkv_res = adamw_update(
        qkv_master, qkv_first, qkv_second, qkv_sum, (WIDTH // 2) ** (-0.5), count_value
    )
    out_res = adamw_update(
        out_master, out_first, out_second, out_sum, (WIDTH // 4) ** (-0.5), count_value
    )
    up_res = adamw_update(up_master, up_first, up_second, up_sum, WIDTH ** (-0.5), count_value)
    down_res = adamw_update(
        down_master, down_first, down_second, down_sum, HIDDEN_SIZE ** (-0.5), count_value
    )
    return (
        node_output,
        input_grad,
        ada_res[0],
        ada_res[1],
        ada_res[2],
        qkv_res[0],
        qkv_res[1],
        qkv_res[2],
        out_res[0],
        out_res[1],
        out_res[2],
        up_res[0],
        up_res[1],
        up_res[2],
        down_res[0],
        down_res[1],
        down_res[2],
    )


def solution(mesh):
    chosen = per_device_near if mesh.shape["node"] == 8 and mesh.shape["head"] == 4 else per_device
    placed = (
        P("node", None),
        P("node", None),
        P(),
        P("node", None),
        P("node", None),
        P(),
        P(),
        P("node", None),
        P("node", None),
        P("node", None),
        P("node", "head"),
        P("node", "head"),
        P("node", "head"),
        P(("head", "node"), None),
        P(("head", "node"), None),
        P(("head", "node"), None),
        P("node", "head"),
        P("node", "head"),
        P("node", "head"),
        P(("head", "node"), None),
        P(("head", "node"), None),
        P(("head", "node"), None),
    )
    return jax.shard_map(
        chosen,
        mesh=mesh,
        in_specs=placed,
        out_specs=(
            P("node", None),
            P("node", None),
            P("node", None),
            P("node", None),
            P("node", None),
            P("node", "head"),
            P("node", "head"),
            P("node", "head"),
            P(("head", "node"), None),
            P(("head", "node"), None),
            P(("head", "node"), None),
            P("node", "head"),
            P("node", "head"),
            P("node", "head"),
            P(("head", "node"), None),
            P(("head", "node"), None),
            P(("head", "node"), None),
        ),
        check_vma=False,
    )
```
